32 devices in a mesh: row: 8 (over z, y), col: 4 (over x, core).
Axes of the slice: x: 2, y: 2, z: 4, core: 2. Of those that a mesh axis runs over, the one named last changes fastest.
Arguments:
- image_states: bfloat16 [64, 3072], P(('row', 'col')), may hold values from -6 to 6
- latent: float32 [64, 64], P(('row', 'col')), may hold values from -6 to 6
- text_keys: bfloat16 [1024, 3072], P('row', 'col')
- text_values: bfloat16 [1024, 3072], P('row', 'col'), may hold values from -6 to 6
- mod_table: float32 [4, 8, 3072], replicated, may hold values from -3 to 3
- timestep: int32 [4], replicated, may hold values from 0 to 3
- grid_size: int32 [4, 2], replicated, may hold values from 1 to 8, as said below
- rope_offset: int32 [4, 2], replicated, may hold values from 0 to 63
- w_qkv: bfloat16 [3072, 9216], P(None, 'row'), may hold values from -0.109375 to 0.109375
- q_gain: float32 [128], replicated, may hold values from 0.1 to 1.9
- k_gain: float32 [128], replicated, may hold values from 0.5 to 4
- w_out: bfloat16 [3072, 3072], P('col', 'row'), may hold values from -0.109375 to 0.109375
- w_fc1: bfloat16 [3072, 12288], P(None, 'row'), may hold values from -0.109375 to 0.109375
- w_fc2: bfloat16 [12288, 3072], P('row'), may hold values from -0.0546875 to 0.0546875
- w_final: bfloat16 [3072, 64], replicated, may hold values from -0.109375 to 0.109375
Outputs:
- velocity: float32 [64, 64], P(('row', 'col'))
- next_latent: float32 [64, 64], P(('row', 'col'))
The draws below stay inside these ranges and needn't reach their ends.
Inputs may be any that keep to these rules, and one draw needn't show every extreme that they name: `grid_size`: column 0 is a request's grid height, at most 2; column 1 its grid width, at most 8; in every draw some request has height 2 and some request width 8.
All inputs are finite; a program needn't handle non-finite values.
Results may differ from the reference program's by a relative error of at most 0.008.
Values may be sent and summed in bfloat16 or wider, within the bound.
No kernel may reach another device: no remote copies, remote signals or barrier semaphores. Data moves between devices by JAX's collectives and lax.ppermute only.
A program may use at most 128 MiB of HBM per device.

```python
import math
import jax
import jax.numpy as jnp
from jax import lax

D = 3072
HEADS = 24
HEAD = 128
FF = 12288
LAT = 64
REQ = 4
TXT = 256
STEPS = 4
RROWS = 2
GRID_W = 8
TOKENS = 64


def draw_grid_size(key, part):
    height_key = jax.random.fold_in(key, 11)
    width_key = jax.random.fold_in(key, 12)
    full_height_key = jax.random.fold_in(key, 13)
    full_width_key = jax.random.fold_in(key, 14)
    heights = jax.random.randint(height_key, (REQ,), 1, RROWS + 1)
    widths = jax.random.randint(width_key, (REQ,), 1, GRID_W + 1)
    full_height = jax.random.randint(full_height_key, (), 0, REQ)
    full_width = jax.random.randint(full_width_key, (), 0, REQ)
    slots = jnp.arange(REQ)
    heights = jnp.where(slots == full_height, RROWS, heights)
    widths = jnp.where(slots == full_width, GRID_W, widths)
    return jnp.stack([heights, widths], 1).astype(jnp.int32)


def draw_text_keys(key, part):
    values = jax.random.normal(jax.random.fold_in(key, 21), (REQ * TXT, D), jnp.float32)
    return values.astype(jnp.bfloat16)


def with_ends(entries, rng, low, largest):
    longest = entries.shape.index(max(entries.shape))
    spots = []
    for shift in (0, 1):
        where = [jax.random.randint(jax.random.fold_in(rng, axis), (), 0, length) for axis, length in enumerate(entries.shape)]
        where[longest] = (where[longest] + shift) % entries.shape[longest]
        spots.append(tuple(where))
    return entries.at[spots[0]].set(low).at[spots[1]].set(largest)


def level_of(stream_key, dims, shards, low, top_value):
    def one(dim, blocks):
        steps = jax.random.uniform(jax.random.fold_in(jax.random.fold_in(stream_key, 6), dim), (blocks,), jnp.float32, low / len(shards), top_value / len(shards))
        return jnp.repeat(jnp.exp(steps), dims[dim] // blocks).reshape((-1,) + (1,) * (len(dims) - dim - 1))

    loudness = one(*shards[0])
    for cut in shards[1:]:
        loudness = loudness * one(*cut)
    return loudness


def scatter_about(key, dims, spread, bound, shards=(), kind=jnp.bfloat16):
    factor_of = level_of(key, dims, shards, -0.22, 0.18) if shards else 1.0
    entries = jax.random.normal(key, dims, jnp.float32) * spread * factor_of
    return jnp.minimum(jnp.maximum(entries, -bound), bound).astype(kind)


def setup_inputs(seed: int = 0) -> dict:
    splits = jax.random.split(jax.random.key(seed), 16)
    image_states = scatter_about(splits[0], (TOKENS, D), 1.0, 6.0, ((0, 32),))
    latent = scatter_about(splits[1], (TOKENS, LAT), 1.0, 6.0, ((0, 32),), jnp.float32)
    text_keys = draw_text_keys(jax.random.fold_in(splits[15], 71), 0)
    text_values = scatter_about(splits[3], (REQ * TXT, D), 1.0, 6.0, ((0, 8), (1, 4)))
    mod_table = scatter_about(splits[4], (STEPS, 8, D), 0.5, 3.0, (), jnp.float32)
    timestep = with_ends(jax.random.randint(splits[5], (REQ,), 0, STEPS), jax.random.fold_in(splits[5], 1), 0, STEPS - 1).astype(jnp.int32)
    grid_size = draw_grid_size(jax.random.fold_in(splits[15], 71), 0)
    rope_offset = with_ends(jax.random.randint(splits[7], (REQ, 2), 0, 64), jax.random.fold_in(splits[7], 1), 0, 63).astype(jnp.int32)
    w_qkv = scatter_about(splits[8], (D, 3 * D), D ** -0.5, 0.109375, ((1, 8),))
    q_gain = jnp.clip(1.0 + 0.18 * jax.random.normal(splits[9], (HEAD,), jnp.float32), 0.1, 1.9)
    k_gain = jnp.clip(jnp.exp(jax.random.uniform(splits[10], (HEAD,), jnp.float32, math.log(0.5), math.log(4.0))), 0.5, 4.0)
    w_out = scatter_about(splits[11], (D, D), D ** -0.5, 0.109375, ((0, 4), (1, 8)))
    w_fc1 = scatter_about(splits[12], (D, FF), D ** -0.5, 0.109375, ((1, 8),))
    w_fc2 = scatter_about(splits[13], (FF, D), FF ** -0.5, 0.0546875, ((0, 8),))
    w_final = scatter_about(splits[14], (D, LAT), D ** -0.5, 0.109375)
    return dict(image_states=image_states, latent=latent, text_keys=text_keys, text_values=text_values, mod_table=mod_table, timestep=timestep, grid_size=grid_size, rope_offset=rope_offset, w_qkv=w_qkv, q_gain=q_gain, k_gain=k_gain, w_out=w_out, w_fc1=w_fc1, w_fc2=w_fc2, w_final=w_final)


eps_norm = 1e-06
blend = 0.25
mask_floor = -1e+30

def layer_norm(values):
    mean_value = lax.optimization_barrier(jnp.mean(values, -1, keepdims=True))
    centred = values - mean_value
    return centred * lax.rsqrt(lax.optimization_barrier(jnp.mean(centred * centred, -1, keepdims=True)) + eps_norm)

def modulate(values, shift_vec, scale_vec):
    return (layer_norm(values) * (1.0 + scale_vec) + shift_vec).astype(jnp.bfloat16)

def rope_tables(pos_h, pos_w, head_size):
    time_half = head_size // 16
    axis_dim = (head_size - head_size // 8) // 2
    freq_index = jnp.arange(axis_dim // 2, dtype=jnp.float32)
    frequency = 10000.0 ** (-2.0 * freq_index / axis_dim)
    angles = jnp.concatenate([jnp.zeros((pos_h.shape[0], time_half), jnp.float32), pos_h[:, None] * frequency[None, :], pos_w[:, None] * frequency[None, :]], 1)
    return (jnp.cos(angles), jnp.sin(angles))

def norm_rope(values, gain_vec, cosine_table, sine_table, head_count, head_size):
    row_total = values.shape[0]
    per_head = values.astype(jnp.float32).reshape(row_total, head_count, head_size)
    per_head = per_head * lax.rsqrt(lax.optimization_barrier(jnp.mean(per_head * per_head, -1, keepdims=True)) + eps_norm) * gain_vec.astype(jnp.float32)
    paired = per_head.reshape(row_total, head_count, head_size // 2, 2)
    even_part = paired[..., 0]
    odd_part = paired[..., 1]
    cos_wide = cosine_table[:, None, :]
    sin_wide = sine_table[:, None, :]
    turned = jnp.stack([even_part * cos_wide - odd_part * sin_wide, even_part * sin_wide + odd_part * cos_wide], -1)
    return turned.reshape(row_total, head_count * head_size).astype(jnp.bfloat16)

def reference(image_states, latent, text_keys, text_values, mod_table, timestep, grid_size, rope_offset, w_qkv, q_gain, k_gain, w_out, w_fc1, w_fc2, w_final):
    token_total = image_states.shape[0]
    token_id = jnp.arange(token_total, dtype=jnp.int32)
    request = (token_id // GRID_W % REQ).astype(jnp.int32)
    grid_row = (token_id // (GRID_W * REQ)).astype(jnp.int32)
    grid_col = (token_id % GRID_W).astype(jnp.int32)
    token_ok = (grid_row < grid_size[request, 0]) & (grid_col < grid_size[request, 1])
    modulation = mod_table[timestep][request].astype(jnp.float32)
    states = image_states.astype(jnp.float32)
    normed = modulate(states, modulation[:, 0], modulation[:, 1])
    joined = jnp.dot(normed, w_qkv, preferred_element_type=jnp.float32).astype(jnp.bfloat16)
    pos_h = (grid_row + rope_offset[request, 0]).astype(jnp.float32)
    pos_w = (grid_col + rope_offset[request, 1]).astype(jnp.float32)
    cosine_table, sine_table = rope_tables(pos_h, pos_w, HEAD)
    queries = norm_rope(joined[:, :D], q_gain, cosine_table, sine_table, HEADS, HEAD)
    image_keys = norm_rope(joined[:, D:2 * D], k_gain, cosine_table, sine_table, HEADS, HEAD)
    image_values = joined[:, 2 * D:]
    per_req = token_total // REQ
    order = jnp.arange(token_total, dtype=jnp.int32).reshape(RROWS, REQ, GRID_W).transpose(1, 0, 2).reshape(REQ, per_req)
    mixed_parts = []
    for req_id in range(REQ):
        picked = order[req_id]
        q_block = queries[picked].reshape(per_req, HEADS, HEAD).astype(jnp.float32)
        k_block = jnp.concatenate([image_keys[picked], text_keys[req_id * TXT:(req_id + 1) * TXT]], 0).reshape(per_req + TXT, HEADS, HEAD).astype(jnp.float32)
        v_block = jnp.concatenate([image_values[picked], text_values[req_id * TXT:(req_id + 1) * TXT]], 0).reshape(per_req + TXT, HEADS, HEAD).astype(jnp.float32)
        key_ok = jnp.concatenate([token_ok[picked], jnp.ones((TXT,), dtype=bool)])
        scores = jnp.einsum('qhd,khd->qhk', q_block, k_block) * HEAD ** (-0.5)
        top_score = lax.optimization_barrier(jnp.max(jnp.where(key_ok, scores, mask_floor), -1, keepdims=True))
        weights = jnp.where(key_ok, jnp.exp(scores - top_score), 0.0)
        weight_sum = lax.optimization_barrier(jnp.sum(weights, -1))
        summed = jnp.einsum('qhk,khd->qhd', weights.astype(jnp.bfloat16).astype(jnp.float32), v_block)
        mixed_parts.append((summed / weight_sum[..., None]).astype(jnp.bfloat16).reshape(per_req, D))
    mixed = jnp.stack(mixed_parts, 0).reshape(REQ, RROWS, GRID_W, D).transpose(1, 0, 2, 3).reshape(token_total, D)
    attended = jnp.dot(mixed, w_out, preferred_element_type=jnp.float32)
    first_res = (states + modulation[:, 2] * attended).astype(jnp.bfloat16)
    normed_two = modulate(first_res.astype(jnp.float32), modulation[:, 3], modulation[:, 4])
    hidden = jax.nn.gelu(jnp.dot(normed_two, w_fc1, preferred_element_type=jnp.float32), approximate=True).astype(jnp.bfloat16)
    second_res = first_res.astype(jnp.float32) + modulation[:, 5] * jnp.dot(hidden, w_fc2, preferred_element_type=jnp.float32)
    normed_three = modulate(second_res, modulation[:, 6], modulation[:, 7])
    raw_velocity = jnp.dot(normed_three, w_final, preferred_element_type=jnp.float32)
    masked = jnp.where(token_ok[:, None], raw_velocity, 0.0)
    left_side = jnp.where((grid_col > 0)[:, None], jnp.roll(masked, 1, 0), 0.0)
    right_side = jnp.where((grid_col < GRID_W - 1)[:, None], jnp.roll(masked, -1, 0), 0.0)
    velocity = jnp.where(token_ok[:, None], masked + blend * (left_side + right_side - 2.0 * masked), 0.0)
    next_latent = latent + -1.0 / STEPS * velocity
    return (velocity, next_latent)
```

```python
import math

import jax
import jax.numpy as jnp
from jax import lax
from jax.experimental import pallas as pl
from jax.experimental.pallas import tpu as pltpu
from jax.sharding import PartitionSpec as P

REQ = 4
TXT = 256
STEPS = 4


eps_norm = 1e-06
blend = 0.25
mask_floor = -1e30


def with_halo(cells, sides, width):
    for axis, dim in sides:
        count = lax.axis_size(axis)
        ends = count - 1
        head = lax.slice_in_dim(cells, 0, width, axis=dim)
        tail = lax.slice_in_dim(cells, cells.shape[dim] - width, cells.shape[dim], axis=dim)
        cells = jnp.concatenate(
            [
                lax.ppermute(tail, axis, [(i, (i + 1) % count) for i in range(ends)]),
                cells,
                lax.ppermute(head, axis, [((i + 1) % count, i) for i in range(ends)]),
            ],
            axis=dim,
        )
    return cells


def layer_norm(values):
    mean_value = jnp.mean(values, -1, keepdims=True)
    centred = values - mean_value
    return centred * lax.rsqrt(jnp.mean(centred * centred, -1, keepdims=True) + eps_norm)


def modulate(values, shift_vec, scale_vec):
    return (layer_norm(values) * (1.0 + scale_vec) + shift_vec).astype(jnp.bfloat16)


def rope_tables(pos_h, pos_w, head_size):
    time_half = head_size // 16
    axis_dim = (head_size - head_size // 8) // 2
    freq_index = jnp.arange(axis_dim // 2, dtype=jnp.float32)
    frequency = 10000.0 ** (-2.0 * freq_index / axis_dim)
    angles = jnp.concatenate(
        [
            jnp.zeros((pos_h.shape[0], time_half), jnp.float32),
            pos_h[:, None] * frequency[None, :],
            pos_w[:, None] * frequency[None, :],
        ],
        1,
    )
    return (jnp.cos(angles), jnp.sin(angles))


def norm_rope(values, gain_vec, cosine_table, sine_table, head_count, head_size):
    row_total = values.shape[0]
    per_head = values.astype(jnp.float32).reshape(row_total, head_count, head_size)
    per_head = (
        per_head * lax.rsqrt(jnp.mean(per_head * per_head, -1, keepdims=True) + eps_norm) * gain_vec
    )
    paired = per_head.reshape(row_total, head_count, head_size // 2, 2)
    even_part = paired[..., 0]
    odd_part = paired[..., 1]
    cos_wide = cosine_table[:, None, :]
    sin_wide = sine_table[:, None, :]
    turned = jnp.stack(
        [even_part * cos_wide - odd_part * sin_wide, even_part * sin_wide + odd_part * cos_wide], -1
    )
    return turned.reshape(row_total, head_count * head_size).astype(jnp.bfloat16)


def on_device(
    image_states,
    latent,
    text_keys,
    text_values,
    mod_table,
    timestep,
    grid_size,
    rope_offset,
    w_qkv,
    q_gain,
    k_gain,
    w_out,
    w_fc1,
    w_fc2,
    w_final,
):
    col_total = lax.axis_size("col")
    row_pos = lax.axis_index("row")
    col_pos = lax.axis_index("col")
    tile_w = image_states.shape[0]
    width = image_states.shape[1]
    head_size = q_gain.shape[0]
    head_count = width // head_size
    local_heads = head_count // col_total
    request = row_pos % REQ
    grid_row = row_pos // REQ
    grid_col = col_pos * tile_w + jnp.arange(tile_w, dtype=jnp.int32)
    req_slots = jnp.arange(REQ, dtype=jnp.int32)
    req_onehot = req_slots == request
    limits = jnp.sum(jnp.where(req_onehot[:, None], grid_size, 0), 0)
    offsets = jnp.sum(jnp.where(req_onehot[:, None], rope_offset, 0), 0)
    step_now = jnp.sum(jnp.where(req_onehot, timestep, 0))
    token_ok = (grid_row < limits[0]) & (grid_col < limits[1])
    modulation = lax.dynamic_index_in_dim(mod_table, step_now, 0, keepdims=False)
    states = image_states.astype(jnp.float32)
    normed = modulate(states, modulation[0], modulation[1])
    joined_cols = jnp.dot(
        lax.all_gather(normed, "row", axis=0, tiled=True), w_qkv, preferred_element_type=jnp.float32
    ).astype(jnp.bfloat16)
    joined = lax.all_to_all(joined_cols, "row", split_axis=0, concat_axis=1, tiled=True)
    pos_h = jnp.zeros((tile_w,), jnp.float32) + (grid_row + offsets[0]).astype(jnp.float32)
    pos_w = (grid_col + offsets[1]).astype(jnp.float32)
    cosine_table, sine_table = rope_tables(pos_h, pos_w, head_size)
    queries = norm_rope(joined[:, :width], q_gain, cosine_table, sine_table, head_count, head_size)
    image_keys = norm_rope(
        joined[:, width : 2 * width], k_gain, cosine_table, sine_table, head_count, head_size
    )
    q_heads, k_heads, v_heads = (
        lax.all_to_all(queries, "col", split_axis=1, concat_axis=0, tiled=True),
        lax.all_to_all(image_keys, "col", split_axis=1, concat_axis=0, tiled=True),
        lax.all_to_all(joined[:, 2 * width :], "col", split_axis=1, concat_axis=0, tiled=True),
    )
    image_rows = k_heads.shape[0]
    text_rows = text_keys.shape[0]
    shard_rows = image_rows + text_rows
    q_block = q_heads.reshape(image_rows, local_heads, head_size)
    key_rows = jnp.concatenate([k_heads, text_keys], 0)
    value_rows = jnp.concatenate([v_heads, text_values], 0)
    run_max = jnp.full((image_rows, local_heads), mask_floor, jnp.float32)
    key_piece = lax.all_gather(key_rows, "row", axis=0, tiled=True)
    value_piece = lax.all_gather(value_rows, "row", axis=0, tiled=True)
    piece_rows = key_piece.shape[0]
    global_row = jnp.arange(piece_rows, dtype=jnp.int32)
    shard_id = global_row // shard_rows
    within = global_row % shard_rows
    is_image = within < image_rows
    source_col = within // tile_w
    source_cell = within % tile_w
    image_req = shard_id % REQ
    text_req = (shard_id * text_rows + within - image_rows) // TXT
    key_req = jnp.where(is_image, image_req, text_req)
    key_onehot = key_req[:, None] == req_slots[None, :]
    key_height = jnp.sum(jnp.where(key_onehot, grid_size[:, 0][None, :], 0), 1)
    key_width = jnp.sum(jnp.where(key_onehot, grid_size[:, 1][None, :], 0), 1)
    image_ok = (shard_id // REQ < key_height) & (source_col * tile_w + source_cell < key_width)
    key_ok = (key_req == request) & (jnp.logical_not(is_image) | image_ok)
    scores = jnp.einsum(
        "qhd,khd->qhk",
        q_block,
        key_piece.reshape(piece_rows, local_heads, head_size),
        preferred_element_type=jnp.float32,
    ) * head_size ** (-0.5)
    new_max = jnp.maximum(run_max, jnp.max(jnp.where(key_ok, scores, mask_floor), -1))
    weights = jnp.where(key_ok, jnp.exp(scores - new_max[..., None]), 0.0)
    new_sum = jnp.sum(weights, -1)
    new_acc = jnp.einsum(
        "qhk,khd->qhd",
        weights.astype(jnp.bfloat16),
        value_piece.reshape(piece_rows, local_heads, head_size),
        preferred_element_type=jnp.float32,
    )
    mixed = (
        (new_acc / new_sum[..., None])
        .astype(jnp.bfloat16)
        .reshape(image_rows, local_heads * head_size)
    )
    partial_out = jnp.dot(
        mixed, lax.all_gather(w_out, "row", axis=1, tiled=True), preferred_element_type=jnp.float32
    )
    attended = lax.psum_scatter(
        partial_out.astype(jnp.bfloat16), "col", scatter_dimension=0, tiled=True
    ).astype(jnp.float32)
    first_res = (states + modulation[2] * attended).astype(jnp.bfloat16)
    normed_two = modulate(first_res.astype(jnp.float32), modulation[3], modulation[4])
    all_rows = lax.all_gather(normed_two, "row", axis=0, tiled=True)
    hidden = jax.nn.gelu(
        jnp.dot(all_rows, w_fc1, preferred_element_type=jnp.float32), approximate=True
    ).astype(jnp.bfloat16)
    every_term = jnp.dot(hidden, w_fc2, preferred_element_type=jnp.float32)
    every_sum = lax.psum(every_term, "row")
    mlp_out = lax.dynamic_slice_in_dim(every_sum, row_pos * tile_w, tile_w, 0)
    second_res = first_res.astype(jnp.float32) + modulation[5] * mlp_out
    normed_three = modulate(second_res, modulation[6], modulation[7])
    raw_velocity = jnp.dot(normed_three, w_final, preferred_element_type=jnp.float32)
    masked = jnp.where(token_ok[:, None], raw_velocity, 0.0)
    padded = with_halo(masked, (("col", 0),), 1)
    left_side = padded[:-2]
    right_side = padded[2:]
    velocity = jnp.where(
        token_ok[:, None], masked + blend * (left_side + right_side - 2.0 * masked), 0.0
    )
    next_latent = latent + -1.0 / STEPS * velocity
    return (velocity, next_latent)


bf16 = jnp.bfloat16
QKV_CHUNKS = 6
FC_CHUNKS = 6
f32 = jnp.float32
VMEM_SPEC = pl.BlockSpec(memory_space=pltpu.VMEM)
SMEM_SPEC = pl.BlockSpec(memory_space=pltpu.SMEM)
HBM_SPEC = pl.BlockSpec(memory_space=pltpu.HBM)


def start_copies(pairs, sems):
    copies = [pltpu.make_async_copy(source, target, sems.at[i]) for i, (source, target) in enumerate(pairs)]
    for copy in copies:
        copy.start()
    return copies


def row_chunks(source, target, count):
    size = source.shape[0] // count
    return [(source.at[pl.ds(i * size, size), :], target.at[pl.ds(i * size, size), :]) for i in range(count)]


def chunked_dot(values, weights, copies):
    size = weights.shape[0] // len(copies)
    total = None
    for i, copy in enumerate(copies):
        copy.wait()
        term = jnp.dot(
            values[:, i * size : (i + 1) * size], weights[i * size : (i + 1) * size, :], preferred_element_type=f32
        )
        total = term if total is None else total + term
    return total


def lane_mean(values):
    return jnp.mean(values, -1, keepdims=True)


def norm_rows(values):
    centred = values - lane_mean(values)
    return centred * lax.rsqrt(lane_mean(centred * centred) + eps_norm)


def per_request(mod_ref, step_ref, slot, rows_each, start, size):
    pieces = [
        jnp.broadcast_to(mod_ref[step_ref[q], pl.ds(slot, 1), pl.ds(start, size)], (rows_each, size))
        for q in range(REQ)
    ]
    row = lax.broadcasted_iota(jnp.int32, (REQ * rows_each, size), 0) // rows_each
    whole = jnp.concatenate([pieces[0]] * REQ, 0)
    for q in range(1, REQ):
        whole = jnp.where(row == q, jnp.concatenate([pieces[q]] * REQ, 0), whole)
    return whole


def qkv_kernel(step_ref, tokens_ref, mod_hbm, w_hbm, out_ref, order_ref, mod_ref, w_ref, sems):
    row = lax.axis_index("row")
    depth = order_ref.shape[1]
    size = out_ref.shape[2]
    mod_copy, *w_copies = start_copies([(mod_hbm, mod_ref)] + row_chunks(w_hbm, w_ref, QKV_CHUNKS), sems)
    for q in range(REQ):
        for g in range(2):
            order_ref[4 * q + 2 * g : 4 * q + 2 * g + 2, :] = tokens_ref[REQ * g + q].astype(f32)
    out_ref[...] = jnp.zeros_like(out_ref)
    normed = norm_rows(order_ref[...])
    mod_copy.wait()
    shift = per_request(mod_ref, step_ref, 0, 4, 0, depth)
    scale = per_request(mod_ref, step_ref, 1, 4, 0, depth)
    normed = (normed * (1.0 + scale) + shift).astype(bf16)
    whole = chunked_dot(normed, w_ref, w_copies).astype(bf16)
    for piece in range(w_ref.shape[1] // size):
        group = lax.rem(row * 3 + piece, 8)
        place = lax.rem(group, 2) * 4 + group // 2
        for q in range(REQ):
            out_ref[8 * q + place] = whole[4 * q : 4 * q + 4, piece * size : (piece + 1) * size]


def attention_kernel(
    size_ref, offset_ref, rows_ref, own_k_hbm, own_v_hbm, other_k_hbm, other_v_hbm, q_gain_ref, k_gain_ref, out_ref,
    q_ref, k_ref, v_ref, text_k_ref, text_v_ref, sems,
):
    row = lax.axis_index("row")
    col = lax.axis_index("col")
    req = row // 2
    side = lax.rem(row, 2)
    group = 2 * col + side
    width = q_ref.shape[1]
    head = q_gain_ref.shape[1]
    heads = width // head
    count = q_ref.shape[0]
    half_rows = own_k_hbm.shape[0]
    own = pl.ds(pl.multiple_of(side * width, width), width)
    top_rows = pl.ds(0, half_rows)
    low_rows = pl.ds(half_rows, half_rows)
    copies = start_copies(
        [
            (own_k_hbm.at[:, own], text_k_ref.at[top_rows, :]),
            (other_k_hbm, text_k_ref.at[low_rows, :]),
            (own_v_hbm.at[:, own], text_v_ref.at[top_rows, :]),
            (other_v_hbm, text_v_ref.at[low_rows, :]),
        ],
        sems,
    )
    for which, ref in enumerate((q_ref, k_ref, v_ref)):
        source = (8 * which + group) // 3
        for s in range(4):
            ref[4 * s : 4 * s + 4, :] = rows_ref[source, s].astype(f32)
    token = lax.broadcasted_iota(jnp.int32, (count, 1), 0)
    pos_h = lax.rem(token, 4) // 2
    pos_w = (token // 4) * 2 + lax.rem(token, 2)
    lane = lax.broadcasted_iota(jnp.int32, (count, head), 1)
    pair = lane // 2
    time_half = head // 16
    axis_dim = (head - head // 8) // 2
    half = axis_dim // 2
    in_h = (pair >= time_half) & (pair < time_half + half)
    index = jnp.where(in_h, pair - time_half, pair - time_half - half).astype(f32)
    frequency = jnp.exp(index * f32(-2.0 * math.log(10000.0) / axis_dim))
    spot = jnp.where(in_h, pos_h + offset_ref[0, req], pos_w + offset_ref[1, req]).astype(f32)
    angle = jnp.where(pair < time_half, 0.0, spot * frequency)
    cosine = jnp.cos(angle)
    sine = jnp.sin(angle)
    even = lax.rem(lane, 2) == 0
    sine = jnp.where(even, -sine, sine)

    def turned(values, gain):
        values = values * lax.rsqrt(lane_mean(values * values) + eps_norm) * gain
        swapped = jnp.where(even, pltpu.roll(values, head - 1, 1), pltpu.roll(values, 1, 1))
        return (values * cosine + swapped * sine).astype(bf16)

    key = lax.broadcasted_iota(jnp.int32, (count, count), 1)
    key_ok = (lax.rem(key, 4) // 2 < size_ref[0, req]) & ((key // 4) * 2 + lax.rem(key, 2) < size_ref[1, req])
    contract = (((1,), (1,)), ((), ()))
    scale = head ** (-0.5)
    queries = [turned(q_ref[:, h * head : (h + 1) * head], q_gain_ref[...]) for h in range(heads)]
    keys = [turned(k_ref[:, h * head : (h + 1) * head], k_gain_ref[...]) for h in range(heads)]
    for copy in copies:
        copy.wait()
    for h in range(heads):
        cols = slice(h * head, (h + 1) * head)
        v = v_ref[:, cols].astype(bf16)
        s_text = lax.dot_general(queries[h], text_k_ref[:, cols], contract, preferred_element_type=f32) * scale
        s_image = lax.dot_general(queries[h], keys[h], contract, preferred_element_type=f32) * scale
        s_image = jnp.where(key_ok, s_image, mask_floor)
        top = jnp.maximum(jnp.max(s_text, -1, keepdims=True), jnp.max(s_image, -1, keepdims=True))
        w_text = jnp.exp(s_text - top)
        w_image = jnp.where(key_ok, jnp.exp(s_image - top), 0.0)
        total = jnp.sum(w_text, -1, keepdims=True) + jnp.sum(w_image, -1, keepdims=True)
        summed = jnp.dot(w_text.astype(bf16), text_v_ref[:, cols], preferred_element_type=f32) + jnp.dot(
            w_image.astype(bf16), v, preferred_element_type=f32
        )
        mixed = (summed / total).astype(bf16)
        for s in range(4):
            for r in range(8):
                out_ref[4 * r + s, :, cols] = mixed[4 * s : 4 * s + 4, :]


def out_kernel(
    step_ref, mixed_ref, tokens_ref, mod_hbm, w0_hbm, w1_hbm, w2_hbm, w3_hbm, out_ref, rows_ref, states_ref, mod_ref,
    w_ref, sems,
):
    row = lax.axis_index("row")
    col = lax.axis_index("col")
    depth, width = w0_hbm.shape
    piece = mixed_ref.shape[2]
    start = pl.multiple_of(row * width, width)
    mod_copy, *w_copies = start_copies(
        [(mod_hbm, mod_ref)]
        + [
            (w_hbm, w_ref.at[pl.ds(pl.multiple_of(jnp.bitwise_xor(col, d) * depth, depth), depth), :])
            for d, w_hbm in enumerate((w0_hbm, w1_hbm, w2_hbm, w3_hbm))
        ],
        sems,
    )
    for r in range(8):
        for s in range(4):
            at = (2 * s + r % 2) * piece
            rows_ref[4 * (r // 2) : 4 * (r // 2) + 4, at : at + piece] = mixed_ref[4 * r + s].astype(f32)
    for q in range(REQ):
        for g in range(2):
            states_ref[4 * q + 2 * g : 4 * q + 2 * g + 2, :] = tokens_ref[REQ * g + q, :, pl.ds(start, width)].astype(f32)
    mixed = rows_ref[...].astype(bf16)
    mod_copy.wait()
    gate = per_request(mod_ref, step_ref, 2, 4, start, width)
    for copy in w_copies:
        copy.wait()
    attended = jnp.dot(mixed, w_ref[...], preferred_element_type=f32)
    first = (states_ref[...] + gate * attended).astype(bf16)
    for r in range(8):
        out_ref[r] = first


def mlp_kernel(
    step_ref, first_ref, mod_hbm, w1_hbm, w2_hbm, out_ref, rows_ref, mod_ref, w1_ref, w2_ref, sems
):
    row = lax.axis_index("row")
    depth = rows_ref.shape[1]
    piece = first_ref.shape[2]
    mod_copy, *w_copies = start_copies(
        [(mod_hbm, mod_ref)] + row_chunks(w1_hbm, w1_ref, FC_CHUNKS) + row_chunks(w2_hbm, w2_ref, FC_CHUNKS), sems
    )
    for r in range(8):
        rows_ref[:, r * piece : (r + 1) * piece] = first_ref[r].astype(f32)
    normed = norm_rows(rows_ref[...])
    mod_copy.wait()
    shift = per_request(mod_ref, step_ref, 3, 4, 0, depth)
    scale = per_request(mod_ref, step_ref, 4, 4, 0, depth)
    normed = (normed * (1.0 + scale) + shift).astype(bf16)
    hidden = jax.nn.gelu(chunked_dot(normed, w1_ref, w_copies[:FC_CHUNKS]), approximate=True).astype(bf16)
    added = chunked_dot(hidden, w2_ref, w_copies[FC_CHUNKS:])
    gate = per_request(mod_ref, step_ref, 5, 4, 0, depth)
    mine = jnp.where(row == 0, 1.0, 0.0)
    term = gate * added + mine * rows_ref[...]
    for q in range(REQ):
        for g in range(2):
            out_ref[REQ * g + q] = term[4 * q + 2 * g : 4 * q + 2 * g + 2, :]


def final_kernel(step_ref, size_ref, terms_ref, mod_hbm, w_hbm, out_ref, mod_ref, w_ref, sems):
    row = lax.axis_index("row")
    col = lax.axis_index("col")
    req = lax.rem(row, REQ)
    step = step_ref[req]
    mod_copy, w_copy = start_copies([(mod_hbm.at[step], mod_ref), (w_hbm, w_ref)], sems)
    second = terms_ref[0]
    for r in range(1, 8):
        second = second + terms_ref[r]
    normed = norm_rows(second)
    mod_copy.wait()
    normed = (normed * (1.0 + mod_ref[7:8, :]) + mod_ref[6:7, :]).astype(bf16)
    w_copy.wait()
    raw = lax.dot_general(normed, w_ref[...], (((1,), (1,)), ((), ())), preferred_element_type=f32)
    out_ref[...] = jnp.where(live_rows(size_ref, row, col, raw.shape), raw, 0.0)


def live_rows(size_ref, row, col, shape):
    req = lax.rem(row, REQ)
    grid_col = col * shape[0] + lax.broadcasted_iota(jnp.int32, shape, 0)
    return (row // REQ < size_ref[0, req]) & (grid_col < size_ref[1, req])


def blend_kernel(size_ref, masked_ref, before_ref, after_ref, latent_ref, velocity_ref, next_ref):
    masked = masked_ref[...]
    count = masked.shape[0]
    left = jnp.concatenate([before_ref[count - 1 :, :], masked[: count - 1, :]], 0)
    right = jnp.concatenate([masked[1:, :], after_ref[:1, :]], 0)
    live = live_rows(size_ref, lax.axis_index("row"), lax.axis_index("col"), masked.shape)
    velocity = jnp.where(live, masked + blend * (left + right - 2.0 * masked), 0.0)
    velocity_ref[...] = velocity
    next_ref[...] = latent_ref[...] + -1.0 / STEPS * velocity


def call(kernel, shape, dtype, specs, scratch=(), grid=(), out_spec=None, limit=None):
    return pl.pallas_call(
        kernel,
        out_shape=jax.ShapeDtypeStruct(shape, dtype),
        grid_spec=pltpu.PrefetchScalarGridSpec(
            num_scalar_prefetch=0,
            grid=grid,
            in_specs=specs,
            out_specs=out_spec if out_spec is not None else VMEM_SPEC,
            scratch_shapes=list(scratch),
        ),
        compiler_params=pltpu.CompilerParams(vmem_limit_bytes=limit),
    )


def exchange(values, axes):
    return lax.all_to_all(values, axes, split_axis=0, concat_axis=0, tiled=True)


def compact_on_device(
    image_states, latent, text_keys, text_values, mod_table, timestep, grid_size, rope_offset,
    w_qkv, q_gain, k_gain, w_out, w_fc1, w_fc2, w_final,
):
    rows = lax.axis_size("row")
    cols = lax.axis_size("col")
    row = lax.axis_index("row")
    tile_w, width = image_states.shape
    head = q_gain.shape[0]
    piece = width // 8
    tokens = rows * tile_w
    both = ("row", "col")

    gathered = exchange(jnp.broadcast_to(image_states[None], (rows, tile_w, width)), "row")

    give = (1 - row % 2) * piece
    swap = [(i, i ^ 1) for i in range(rows)]
    other_k = lax.ppermute(lax.dynamic_slice_in_dim(text_keys, give, piece, 1), "row", swap)
    other_v = lax.ppermute(lax.dynamic_slice_in_dim(text_values, give, piece, 1), "row", swap)
    w_x = lax.ppermute(w_out, "col", [(i, i ^ 2) for i in range(cols)])
    near = [(i, i ^ 1) for i in range(cols)]
    w_k = lax.ppermute(w_out, "col", near)

    sems = lambda count: pltpu.SemaphoreType.DMA((count,))
    mod_space = pltpu.VMEM(mod_table.shape, f32)
    pieces = call(
        qkv_kernel,
        (rows * cols, 4, piece),
        bf16,
        [SMEM_SPEC, VMEM_SPEC, HBM_SPEC, HBM_SPEC],
        [pltpu.VMEM((tokens, width), f32), mod_space, pltpu.VMEM(w_qkv.shape, bf16), sems(QKV_CHUNKS + 1)],
        limit=16 << 20,
    )(timestep, gathered, mod_table, w_qkv)
    got = exchange(pieces, both).reshape(rows, cols, 4, piece)
    text_space = pltpu.VMEM((2 * text_keys.shape[0], piece), bf16)
    mixed = call(
        attention_kernel,
        (rows * cols, 4, piece),
        bf16,
        [SMEM_SPEC, SMEM_SPEC, VMEM_SPEC] + [HBM_SPEC] * 4 + [VMEM_SPEC] * 2,
        [pltpu.VMEM((tokens, piece), f32)] * 3 + [text_space] * 2 + [sems(4)],
        limit=8 << 20,
    )(
        grid_size.T, rope_offset.T, got, text_keys, text_values, other_k, other_v,
        q_gain.reshape(1, head), k_gain.reshape(1, head),
    )
    mixed, w_x = lax.optimization_barrier((mixed, w_x))
    w_xk = lax.ppermute(w_x, "col", near)
    all_mixed = exchange(mixed, both)
    first = call(
        out_kernel,
        (rows, tokens, piece),
        bf16,
        [SMEM_SPEC, VMEM_SPEC, VMEM_SPEC] + [HBM_SPEC] * 5,
        [
            pltpu.VMEM((tokens, width), f32),
            pltpu.VMEM((tokens, piece), f32),
            mod_space,
            pltpu.VMEM((width, piece), bf16),
            sems(5),
        ],
        limit=16 << 20,
    )(timestep, all_mixed, gathered, mod_table, w_out, w_k, w_x, w_xk)
    all_first = exchange(first, "row")
    terms = call(
        mlp_kernel,
        (rows, tile_w, width),
        f32,
        [SMEM_SPEC, VMEM_SPEC] + [HBM_SPEC] * 3,
        [
            pltpu.VMEM((tokens, width), f32),
            mod_space,
            pltpu.VMEM(w_fc1.shape, bf16),
            pltpu.VMEM(w_fc2.shape, bf16),
            sems(2 * FC_CHUNKS + 1),
        ],
        limit=40 << 20,
    )(timestep, all_first, mod_table, w_fc1, w_fc2)
    all_terms = exchange(terms, "row")
    masked = call(
        final_kernel,
        (tile_w, w_final.shape[1]),
        f32,
        [SMEM_SPEC, SMEM_SPEC, VMEM_SPEC, HBM_SPEC, HBM_SPEC],
        [pltpu.VMEM(mod_table.shape[1:], f32), pltpu.VMEM(w_final.shape[::-1], bf16), sems(2)],
        limit=8 << 20,
    )(timestep, grid_size.T, all_terms, mod_table, w_final.T)
    before = lax.ppermute(masked, "col", [(i, i + 1) for i in range(cols - 1)])
    after = lax.ppermute(masked, "col", [(i + 1, i) for i in range(cols - 1)])
    result = jax.ShapeDtypeStruct(latent.shape, f32)
    return pl.pallas_call(
        blend_kernel,
        out_shape=(result, result),
        in_specs=[SMEM_SPEC] + [VMEM_SPEC] * 4,
        out_specs=(VMEM_SPEC, VMEM_SPEC),
        compiler_params=pltpu.CompilerParams(vmem_limit_bytes=8 << 20),
    )(grid_size.T, masked, before, after, latent)


def solution(mesh):
    placed = (
        P(("row", "col"), None),
        P(("row", "col"), None),
        P("row", "col"),
        P("row", "col"),
        P(),
        P(),
        P(),
        P(),
        P(None, "row"),
        P(),
        P(),
        P("col", "row"),
        P(None, "row"),
        P("row", None),
        P(),
    )
    compact = mesh.shape["row"] == 2 * REQ and mesh.shape["col"] == 4
    return jax.shard_map(
        compact_on_device if compact else on_device,
        mesh=mesh,
        in_specs=placed,
        out_specs=(P(("row", "col"), None), P(("row", "col"), None)),
        check_vma=False,
    )
```

```python
import math

import jax
import jax.numpy as jnp
from jax import lax
from jax.experimental import pallas as pl
from jax.experimental.pallas import tpu as pltpu
from jax.sharding import PartitionSpec as P

REQ = 4
TXT = 256
STEPS = 4


eps_norm = 1e-06
blend = 0.25
mask_floor = -1e30


def with_halo(cells, sides, width):
    for axis, dim in sides:
        count = lax.axis_size(axis)
        ends = count - 1
        head = lax.slice_in_dim(cells, 0, width, axis=dim)
        tail = lax.slice_in_dim(cells, cells.shape[dim] - width, cells.shape[dim], axis=dim)
        cells = jnp.concatenate(
            [
                lax.ppermute(tail, axis, [(i, (i + 1) % count) for i in range(ends)]),
                cells,
                lax.ppermute(head, axis, [((i + 1) % count, i) for i in range(ends)]),
            ],
            axis=dim,
        )
    return cells


def layer_norm(values):
    mean_value = jnp.mean(values, -1, keepdims=True)
    centred = values - mean_value
    return centred * lax.rsqrt(jnp.mean(centred * centred, -1, keepdims=True) + eps_norm)


def modulate(values, shift_vec, scale_vec):
    return (layer_norm(values) * (1.0 + scale_vec) + shift_vec).astype(jnp.bfloat16)


def rope_tables(pos_h, pos_w, head_size):
    time_half = head_size // 16
    axis_dim = (head_size - head_size // 8) // 2
    freq_index = jnp.arange(axis_dim // 2, dtype=jnp.float32)
    frequency = 10000.0 ** (-2.0 * freq_index / axis_dim)
    angles = jnp.concatenate(
        [
            jnp.zeros((pos_h.shape[0], time_half), jnp.float32),
            pos_h[:, None] * frequency[None, :],
            pos_w[:, None] * frequency[None, :],
        ],
        1,
    )
    return (jnp.cos(angles), jnp.sin(angles))


def norm_rope(values, gain_vec, cosine_table, sine_table, head_count, head_size):
    row_total = values.shape[0]
    per_head = values.astype(jnp.float32).reshape(row_total, head_count, head_size)
    per_head = (
        per_head * lax.rsqrt(jnp.mean(per_head * per_head, -1, keepdims=True) + eps_norm) * gain_vec
    )
    paired = per_head.reshape(row_total, head_count, head_size // 2, 2)
    even_part = paired[..., 0]
    odd_part = paired[..., 1]
    cos_wide = cosine_table[:, None, :]
    sin_wide = sine_table[:, None, :]
    turned = jnp.stack(
        [even_part * cos_wide - odd_part * sin_wide, even_part * sin_wide + odd_part * cos_wide], -1
    )
    return turned.reshape(row_total, head_count * head_size).astype(jnp.bfloat16)


def on_device(
    image_states,
    latent,
    text_keys,
    text_values,
    mod_table,
    timestep,
    grid_size,
    rope_offset,
    w_qkv,
    q_gain,
    k_gain,
    w_out,
    w_fc1,
    w_fc2,
    w_final,
):
    col_total = lax.axis_size("col")
    row_pos = lax.axis_index("row")
    col_pos = lax.axis_index("col")
    tile_w = image_states.shape[0]
    width = image_states.shape[1]
    head_size = q_gain.shape[0]
    head_count = width // head_size
    local_heads = head_count // col_total
    request = row_pos % REQ
    grid_row = row_pos // REQ
    grid_col = col_pos * tile_w + jnp.arange(tile_w, dtype=jnp.int32)
    req_slots = jnp.arange(REQ, dtype=jnp.int32)
    req_onehot = req_slots == request
    limits = jnp.sum(jnp.where(req_onehot[:, None], grid_size, 0), 0)
    offsets = jnp.sum(jnp.where(req_onehot[:, None], rope_offset, 0), 0)
    step_now = jnp.sum(jnp.where(req_onehot, timestep, 0))
    token_ok = (grid_row < limits[0]) & (grid_col < limits[1])
    modulation = lax.dynamic_index_in_dim(mod_table, step_now, 0, keepdims=False)
    states = image_states.astype(jnp.float32)
    normed = modulate(states, modulation[0], modulation[1])
    joined_cols = jnp.dot(
        lax.all_gather(normed, "row", axis=0, tiled=True), w_qkv, preferred_element_type=jnp.float32
    ).astype(jnp.bfloat16)
    joined = lax.all_to_all(joined_cols, "row", split_axis=0, concat_axis=1, tiled=True)
    pos_h = jnp.zeros((tile_w,), jnp.float32) + (grid_row + offsets[0]).astype(jnp.float32)
    pos_w = (grid_col + offsets[1]).astype(jnp.float32)
    cosine_table, sine_table = rope_tables(pos_h, pos_w, head_size)
    queries = norm_rope(joined[:, :width], q_gain, cosine_table, sine_table, head_count, head_size)
    image_keys = norm_rope(
        joined[:, width : 2 * width], k_gain, cosine_table, sine_table, head_count, head_size
    )
    q_heads, k_heads, v_heads = (
        lax.all_to_all(queries, "col", split_axis=1, concat_axis=0, tiled=True),
        lax.all_to_all(image_keys, "col", split_axis=1, concat_axis=0, tiled=True),
        lax.all_to_all(joined[:, 2 * width :], "col", split_axis=1, concat_axis=0, tiled=True),
    )
    image_rows = k_heads.shape[0]
    text_rows = text_keys.shape[0]
    shard_rows = image_rows + text_rows
    q_block = q_heads.reshape(image_rows, local_heads, head_size)
    key_rows = jnp.concatenate([k_heads, text_keys], 0)
    value_rows = jnp.concatenate([v_heads, text_values], 0)
    run_max = jnp.full((image_rows, local_heads), mask_floor, jnp.float32)
    key_piece = lax.all_gather(key_rows, "row", axis=0, tiled=True)
    value_piece = lax.all_gather(value_rows, "row", axis=0, tiled=True)
    piece_rows = key_piece.shape[0]
    global_row = jnp.arange(piece_rows, dtype=jnp.int32)
    shard_id = global_row // shard_rows
    within = global_row % shard_rows
    is_image = within < image_rows
    source_col = within // tile_w
    source_cell = within % tile_w
    image_req = shard_id % REQ
    text_req = (shard_id * text_rows + within - image_rows) // TXT
    key_req = jnp.where(is_image, image_req, text_req)
    key_onehot = key_req[:, None] == req_slots[None, :]
    key_height = jnp.sum(jnp.where(key_onehot, grid_size[:, 0][None, :], 0), 1)
    key_width = jnp.sum(jnp.where(key_onehot, grid_size[:, 1][None, :], 0), 1)
    image_ok = (shard_id // REQ < key_height) & (source_col * tile_w + source_cell < key_width)
    key_ok = (key_req == request) & (jnp.logical_not(is_image) | image_ok)
    scores = jnp.einsum(
        "qhd,khd->qhk",
        q_block,
        key_piece.reshape(piece_rows, local_heads, head_size),
        preferred_element_type=jnp.float32,
    ) * head_size ** (-0.5)
    new_max = jnp.maximum(run_max, jnp.max(jnp.where(key_ok, scores, mask_floor), -1))
    weights = jnp.where(key_ok, jnp.exp(scores - new_max[..., None]), 0.0)
    new_sum = jnp.sum(weights, -1)
    new_acc = jnp.einsum(
        "qhk,khd->qhd",
        weights.astype(jnp.bfloat16),
        value_piece.reshape(piece_rows, local_heads, head_size),
        preferred_element_type=jnp.float32,
    )
    mixed = (
        (new_acc / new_sum[..., None])
        .astype(jnp.bfloat16)
        .reshape(image_rows, local_heads * head_size)
    )
    partial_out = jnp.dot(
        mixed, lax.all_gather(w_out, "row", axis=1, tiled=True), preferred_element_type=jnp.float32
    )
    attended = lax.psum_scatter(
        partial_out.astype(jnp.bfloat16), "col", scatter_dimension=0, tiled=True
    ).astype(jnp.float32)
    first_res = (states + modulation[2] * attended).astype(jnp.bfloat16)
    normed_two = modulate(first_res.astype(jnp.float32), modulation[3], modulation[4])
    all_rows = lax.all_gather(normed_two, "row", axis=0, tiled=True)
    hidden = jax.nn.gelu(
        jnp.dot(all_rows, w_fc1, preferred_element_type=jnp.float32), approximate=True
    ).astype(jnp.bfloat16)
    every_term = jnp.dot(hidden, w_fc2, preferred_element_type=jnp.float32)
    every_sum = lax.psum(every_term, "row")
    mlp_out = lax.dynamic_slice_in_dim(every_sum, row_pos * tile_w, tile_w, 0)
    second_res = first_res.astype(jnp.float32) + modulation[5] * mlp_out
    normed_three = modulate(second_res, modulation[6], modulation[7])
    raw_velocity = jnp.dot(normed_three, w_final, preferred_element_type=jnp.float32)
    masked = jnp.where(token_ok[:, None], raw_velocity, 0.0)
    padded = with_halo(masked, (("col", 0),), 1)
    left_side = padded[:-2]
    right_side = padded[2:]
    velocity = jnp.where(
        token_ok[:, None], masked + blend * (left_side + right_side - 2.0 * masked), 0.0
    )
    next_latent = latent + -1.0 / STEPS * velocity
    return (velocity, next_latent)


bf16 = jnp.bfloat16
QKV_CHUNKS = 6
FC_CHUNKS = 6
f32 = jnp.float32
VMEM_SPEC = pl.BlockSpec(memory_space=pltpu.VMEM)
SMEM_SPEC = pl.BlockSpec(memory_space=pltpu.SMEM)
HBM_SPEC = pl.BlockSpec(memory_space=pltpu.HBM)


def start_copies(pairs, sems):
    copies = [pltpu.make_async_copy(source, target, sems.at[i]) for i, (source, target) in enumerate(pairs)]
    for copy in copies:
        copy.start()
    return copies


def row_chunks(source, target, count):
    size = source.shape[0] // count
    return [(source.at[pl.ds(i * size, size), :], target.at[pl.ds(i * size, size), :]) for i in range(count)]


def chunked_dot(values, weights, copies):
    size = weights.shape[0] // len(copies)
    total = None
    for i, copy in enumerate(copies):
        copy.wait()
        term = jnp.dot(
            values[:, i * size : (i + 1) * size], weights[i * size : (i + 1) * size, :], preferred_element_type=f32
        )
        total = term if total is None else total + term
    return total


def lane_mean(values):
    return jnp.mean(values, -1, keepdims=True)


def norm_rows(values):
    centred = values - lane_mean(values)
    return centred * lax.rsqrt(lane_mean(centred * centred) + eps_norm)


def per_request(mod_ref, step_ref, slot, rows_each, start, size):
    pieces = [
        jnp.broadcast_to(mod_ref[step_ref[q], pl.ds(slot, 1), pl.ds(start, size)], (rows_each, size))
        for q in range(REQ)
    ]
    row = lax.broadcasted_iota(jnp.int32, (REQ * rows_each, size), 0) // rows_each
    whole = jnp.concatenate([pieces[0]] * REQ, 0)
    for q in range(1, REQ):
        whole = jnp.where(row == q, jnp.concatenate([pieces[q]] * REQ, 0), whole)
    return whole


def qkv_kernel(step_hbm, tokens_ref, mod_hbm, w_hbm, out_ref, step_ref, order_ref, mod_ref, w_ref, sems):
    row = lax.axis_index("row")
    depth = order_ref.shape[1]
    size = out_ref.shape[2]
    step_copy, mod_copy, *w_copies = start_copies(
        [(step_hbm, step_ref), (mod_hbm, mod_ref)] + row_chunks(w_hbm, w_ref, QKV_CHUNKS), sems
    )
    for q in range(REQ):
        for g in range(2):
            order_ref[4 * q + 2 * g : 4 * q + 2 * g + 2, :] = tokens_ref[REQ * g + q].astype(f32)
    out_ref[...] = jnp.zeros_like(out_ref)
    normed = norm_rows(order_ref[...])
    step_copy.wait()
    mod_copy.wait()
    shift = per_request(mod_ref, step_ref, 0, 4, 0, depth)
    scale = per_request(mod_ref, step_ref, 1, 4, 0, depth)
    normed = (normed * (1.0 + scale) + shift).astype(bf16)
    whole = chunked_dot(normed, w_ref, w_copies).astype(bf16)
    for piece in range(w_ref.shape[1] // size):
        group = lax.rem(row * 3 + piece, 8)
        place = lax.rem(group, 2) * 4 + group // 2
        for q in range(REQ):
            out_ref[8 * q + place] = whole[4 * q : 4 * q + 4, piece * size : (piece + 1) * size]


def attention_kernel(
    size_hbm, offset_hbm, rows_ref, own_k_hbm, own_v_hbm, other_k_hbm, other_v_hbm, q_gain_hbm, k_gain_hbm, out_ref,
    size_ref, offset_ref, q_gain_ref, k_gain_ref, q_ref, k_ref, v_ref, text_k_ref, text_v_ref, sems,
):
    row = lax.axis_index("row")
    col = lax.axis_index("col")
    req = row // 2
    side = lax.rem(row, 2)
    group = 2 * col + side
    width = q_ref.shape[1]
    head = q_gain_hbm.shape[1]
    heads = width // head
    count = q_ref.shape[0]
    half_rows = own_k_hbm.shape[0]
    own = pl.ds(pl.multiple_of(side * width, width), width)
    top_rows = pl.ds(0, half_rows)
    low_rows = pl.ds(half_rows, half_rows)
    *small, copy_k0, copy_k1, copy_v0, copy_v1 = start_copies(
        [
            (offset_hbm, offset_ref),
            (size_hbm, size_ref),
            (q_gain_hbm, q_gain_ref),
            (k_gain_hbm, k_gain_ref),
            (own_k_hbm.at[:, own], text_k_ref.at[top_rows, :]),
            (other_k_hbm, text_k_ref.at[low_rows, :]),
            (own_v_hbm.at[:, own], text_v_ref.at[top_rows, :]),
            (other_v_hbm, text_v_ref.at[low_rows, :]),
        ],
        sems,
    )
    for which, ref in enumerate((q_ref, k_ref, v_ref)):
        source = (8 * which + group) // 3
        for s in range(4):
            ref[4 * s : 4 * s + 4, :] = rows_ref[source, s].astype(f32)
    for copy in small:
        copy.wait()
    token = lax.broadcasted_iota(jnp.int32, (count, 1), 0)
    pos_h = lax.rem(token, 4) // 2
    pos_w = (token // 4) * 2 + lax.rem(token, 2)
    lane = lax.broadcasted_iota(jnp.int32, (count, head), 1)
    pair = lane // 2
    time_half = head // 16
    axis_dim = (head - head // 8) // 2
    half = axis_dim // 2
    in_h = (pair >= time_half) & (pair < time_half + half)
    index = jnp.where(in_h, pair - time_half, pair - time_half - half).astype(f32)
    frequency = jnp.exp(index * f32(-2.0 * math.log(10000.0) / axis_dim))
    spot = jnp.where(in_h, pos_h + offset_ref[0, req], pos_w + offset_ref[1, req]).astype(f32)
    angle = jnp.where(pair < time_half, 0.0, spot * frequency)
    cosine = jnp.cos(angle)
    sine = jnp.sin(angle)
    even = lax.rem(lane, 2) == 0
    sine = jnp.where(even, -sine, sine)

    def turned(values, gain):
        values = values * lax.rsqrt(lane_mean(values * values) + eps_norm) * gain
        swapped = jnp.where(even, pltpu.roll(values, head - 1, 1), pltpu.roll(values, 1, 1))
        return (values * cosine + swapped * sine).astype(bf16)

    key = lax.broadcasted_iota(jnp.int32, (count, count), 1)
    key_ok = (lax.rem(key, 4) // 2 < size_ref[0, req]) & ((key // 4) * 2 + lax.rem(key, 2) < size_ref[1, req])
    contract = (((1,), (1,)), ((), ()))
    scale = head ** (-0.5)
    queries = [turned(q_ref[:, h * head : (h + 1) * head], q_gain_ref[...]) for h in range(heads)]
    keys = [turned(k_ref[:, h * head : (h + 1) * head], k_gain_ref[...]) for h in range(heads)]
    for copy in (copy_k0, copy_k1, copy_v0, copy_v1):
        copy.wait()
    for h in range(heads):
        cols = slice(h * head, (h + 1) * head)
        v = v_ref[:, cols].astype(bf16)
        s_text = lax.dot_general(queries[h], text_k_ref[:, cols], contract, preferred_element_type=f32) * scale
        s_image = lax.dot_general(queries[h], keys[h], contract, preferred_element_type=f32) * scale
        s_image = jnp.where(key_ok, s_image, mask_floor)
        top = jnp.maximum(jnp.max(s_text, -1, keepdims=True), jnp.max(s_image, -1, keepdims=True))
        w_text = jnp.exp(s_text - top)
        w_image = jnp.where(key_ok, jnp.exp(s_image - top), 0.0)
        total = jnp.sum(w_text, -1, keepdims=True) + jnp.sum(w_image, -1, keepdims=True)
        summed = jnp.dot(w_text.astype(bf16), text_v_ref[:, cols], preferred_element_type=f32) + jnp.dot(
            w_image.astype(bf16), v, preferred_element_type=f32
        )
        mixed = (summed / total).astype(bf16)
        for s in range(4):
            for r in range(8):
                out_ref[4 * r + s, :, cols] = mixed[4 * s : 4 * s + 4, :]


def out_kernel(
    step_hbm, mixed_ref, tokens_ref, mod_hbm, w0_hbm, w1_hbm, w2_hbm, w3_hbm, out_ref, step_ref, rows_ref, states_ref,
    mod_ref, w_ref, sems,
):
    row = lax.axis_index("row")
    col = lax.axis_index("col")
    depth, width = w0_hbm.shape
    piece = mixed_ref.shape[2]
    start = pl.multiple_of(row * width, width)
    step_copy, mod_copy, *w_copies = start_copies(
        [(step_hbm, step_ref), (mod_hbm, mod_ref)]
        + [
            (w_hbm, w_ref.at[pl.ds(pl.multiple_of(jnp.bitwise_xor(col, d) * depth, depth), depth), :])
            for d, w_hbm in enumerate((w0_hbm, w1_hbm, w2_hbm, w3_hbm))
        ],
        sems,
    )
    for r in range(8):
        for s in range(4):
            at = (2 * s + r % 2) * piece
            rows_ref[4 * (r // 2) : 4 * (r // 2) + 4, at : at + piece] = mixed_ref[4 * r + s].astype(f32)
    for q in range(REQ):
        for g in range(2):
            states_ref[4 * q + 2 * g : 4 * q + 2 * g + 2, :] = tokens_ref[REQ * g + q, :, pl.ds(start, width)].astype(f32)
    mixed = rows_ref[...].astype(bf16)
    step_copy.wait()
    mod_copy.wait()
    gate = per_request(mod_ref, step_ref, 2, 4, start, width)
    for copy in w_copies:
        copy.wait()
    attended = jnp.dot(mixed, w_ref[...], preferred_element_type=f32)
    first = (states_ref[...] + gate * attended).astype(bf16)
    for r in range(8):
        out_ref[r] = first


def mlp_kernel(
    step_hbm, first_ref, mod_hbm, w1_hbm, w2_hbm, out_ref, step_ref, rows_ref, mod_ref, w1_ref, w2_ref, sems
):
    row = lax.axis_index("row")
    depth = rows_ref.shape[1]
    piece = first_ref.shape[2]
    step_copy, mod_copy, *w_copies = start_copies(
        [(step_hbm, step_ref), (mod_hbm, mod_ref)]
        + row_chunks(w1_hbm, w1_ref, FC_CHUNKS)
        + row_chunks(w2_hbm, w2_ref, FC_CHUNKS),
        sems,
    )
    for r in range(8):
        rows_ref[:, r * piece : (r + 1) * piece] = first_ref[r].astype(f32)
    normed = norm_rows(rows_ref[...])
    step_copy.wait()
    mod_copy.wait()
    shift = per_request(mod_ref, step_ref, 3, 4, 0, depth)
    scale = per_request(mod_ref, step_ref, 4, 4, 0, depth)
    normed = (normed * (1.0 + scale) + shift).astype(bf16)
    hidden = jax.nn.gelu(chunked_dot(normed, w1_ref, w_copies[:FC_CHUNKS]), approximate=True).astype(bf16)
    added = chunked_dot(hidden, w2_ref, w_copies[FC_CHUNKS:])
    gate = per_request(mod_ref, step_ref, 5, 4, 0, depth)
    mine = jnp.where(row == 0, 1.0, 0.0)
    term = gate * added + mine * rows_ref[...]
    for q in range(REQ):
        for g in range(2):
            out_ref[REQ * g + q] = term[4 * q + 2 * g : 4 * q + 2 * g + 2, :]


def final_kernel(step_hbm, size_hbm, terms_ref, mod_hbm, w_hbm, out_ref, step_ref, size_ref, mod_ref, w_ref, sems):
    row = lax.axis_index("row")
    col = lax.axis_index("col")
    req = lax.rem(row, REQ)
    step_copy, size_copy, mod_copy, w_copy = start_copies(
        [(step_hbm, step_ref), (size_hbm, size_ref), (mod_hbm, mod_ref), (w_hbm, w_ref)], sems
    )
    second = terms_ref[0]
    for r in range(1, 8):
        second = second + terms_ref[r]
    normed = norm_rows(second)
    step_copy.wait()
    mod_copy.wait()
    step = step_ref[req]
    normed = (normed * (1.0 + mod_ref[step, 7:8, :]) + mod_ref[step, 6:7, :]).astype(bf16)
    size_copy.wait()
    w_copy.wait()
    raw = lax.dot_general(normed, w_ref[...], (((1,), (1,)), ((), ())), preferred_element_type=f32)
    out_ref[...] = jnp.where(live_rows(size_ref, row, col, raw.shape), raw, 0.0)


def live_rows(size_ref, row, col, shape):
    req = lax.rem(row, REQ)
    grid_col = col * shape[0] + lax.broadcasted_iota(jnp.int32, shape, 0)
    return (row // REQ < size_ref[0, req]) & (grid_col < size_ref[1, req])


def blend_kernel(size_hbm, masked_ref, near_ref, far_ref, latent_hbm, velocity_ref, next_ref, size_ref, latent_ref, sems):
    col = lax.axis_index("col")
    size_copy, latent_copy = start_copies([(size_hbm, size_ref), (latent_hbm, latent_ref)], sems)
    masked = masked_ref[...]
    near = near_ref[...]
    far = jnp.where((col == 1) | (col == 2), far_ref[...], 0.0)
    odd = lax.rem(col, 2) == 1
    count = masked.shape[0]
    left = jnp.concatenate([jnp.where(odd, near, far)[count - 1 :, :], masked[: count - 1, :]], 0)
    right = jnp.concatenate([masked[1:, :], jnp.where(odd, far, near)[:1, :]], 0)
    size_copy.wait()
    live = live_rows(size_ref, lax.axis_index("row"), col, masked.shape)
    velocity = jnp.where(live, masked + blend * (left + right - 2.0 * masked), 0.0)
    velocity_ref[...] = velocity
    latent_copy.wait()
    next_ref[...] = latent_ref[...] + -1.0 / STEPS * velocity


def call(kernel, shape, dtype, specs, scratch=(), grid=(), out_spec=None, limit=None):
    return pl.pallas_call(
        kernel,
        out_shape=jax.ShapeDtypeStruct(shape, dtype),
        grid_spec=pltpu.PrefetchScalarGridSpec(
            num_scalar_prefetch=0,
            grid=grid,
            in_specs=specs,
            out_specs=out_spec if out_spec is not None else VMEM_SPEC,
            scratch_shapes=list(scratch),
        ),
        compiler_params=pltpu.CompilerParams(vmem_limit_bytes=limit),
    )


def exchange(values, axes):
    return lax.all_to_all(values, axes, split_axis=0, concat_axis=0, tiled=True)


def compact_on_device(
    image_states, latent, text_keys, text_values, mod_table, timestep, grid_size, rope_offset,
    w_qkv, q_gain, k_gain, w_out, w_fc1, w_fc2, w_final,
):
    rows = lax.axis_size("row")
    cols = lax.axis_size("col")
    row = lax.axis_index("row")
    stay = lambda values: pltpu.with_memory_space_constraint(values, pltpu.HBM)
    tile_w, width = image_states.shape
    head = q_gain.shape[0]
    piece = width // 8
    tokens = rows * tile_w
    both = ("row", "col")

    gathered = exchange(jnp.broadcast_to(image_states[None], (rows, tile_w, width)), "row")

    give = (1 - row % 2) * piece
    swap = [(i, i ^ 1) for i in range(rows)]
    other_k = lax.ppermute(lax.dynamic_slice_in_dim(text_keys, give, piece, 1), "row", swap)
    other_v = lax.ppermute(lax.dynamic_slice_in_dim(text_values, give, piece, 1), "row", swap)
    gathered, other_k, other_v = lax.optimization_barrier((gathered, other_k, other_v))
    w_x = lax.ppermute(w_out, "col", [(i, i ^ 2) for i in range(cols)])
    near = [(i, i ^ 1) for i in range(cols)]
    w_k = lax.ppermute(w_out, "col", near)

    sems = lambda count: pltpu.SemaphoreType.DMA((count,))
    mod_space = pltpu.VMEM(mod_table.shape, f32)
    steps_space = pltpu.SMEM(timestep.shape, jnp.int32)
    sizes_space = pltpu.SMEM(grid_size.shape[::-1], jnp.int32)
    gain_space = pltpu.VMEM((1, head), f32)
    steps = stay(timestep)
    sizes = stay(grid_size.T)
    mods = stay(mod_table)
    pieces = call(
        qkv_kernel,
        (rows * cols, 4, piece),
        bf16,
        [HBM_SPEC, VMEM_SPEC, HBM_SPEC, HBM_SPEC],
        [steps_space, pltpu.VMEM((tokens, width), f32), mod_space, pltpu.VMEM(w_qkv.shape, bf16), sems(QKV_CHUNKS + 2)],
        limit=16 << 20,
    )(steps, gathered, mods, stay(w_qkv))
    got = exchange(pieces, both).reshape(rows, cols, 4, piece)
    text_space = pltpu.VMEM((2 * text_keys.shape[0], piece), bf16)
    mixed = call(
        attention_kernel,
        (rows * cols, 4, piece),
        bf16,
        [HBM_SPEC, HBM_SPEC, VMEM_SPEC] + [HBM_SPEC] * 6,
        [sizes_space] * 2 + [gain_space] * 2 + [pltpu.VMEM((tokens, piece), f32)] * 3 + [text_space] * 2 + [sems(8)],
        limit=8 << 20,
    )(
        sizes, stay(rope_offset.T), got, stay(text_keys), stay(text_values), other_k, other_v,
        stay(q_gain.reshape(1, head)), stay(k_gain.reshape(1, head)),
    )
    mixed, w_x = lax.optimization_barrier((mixed, w_x))
    w_xk = lax.ppermute(w_x, "col", near)
    all_mixed = exchange(mixed, both)
    first = call(
        out_kernel,
        (rows, tokens, piece),
        bf16,
        [HBM_SPEC, VMEM_SPEC, VMEM_SPEC] + [HBM_SPEC] * 5,
        [
            steps_space,
            pltpu.VMEM((tokens, width), f32),
            pltpu.VMEM((tokens, piece), f32),
            mod_space,
            pltpu.VMEM((width, piece), bf16),
            sems(6),
        ],
        limit=16 << 20,
    )(steps, all_mixed, gathered, mods, stay(w_out), w_k, w_x, w_xk)
    all_first = exchange(first, "row")
    terms = call(
        mlp_kernel,
        (rows, tile_w, width),
        f32,
        [HBM_SPEC, VMEM_SPEC] + [HBM_SPEC] * 3,
        [
            steps_space,
            pltpu.VMEM((tokens, width), f32),
            mod_space,
            pltpu.VMEM(w_fc1.shape, bf16),
            pltpu.VMEM(w_fc2.shape, bf16),
            sems(2 * FC_CHUNKS + 2),
        ],
        limit=40 << 20,
    )(steps, all_first, mods, stay(w_fc1), stay(w_fc2))
    all_terms = exchange(terms, "row")
    masked = call(
        final_kernel,
        (tile_w, w_final.shape[1]),
        f32,
        [HBM_SPEC, HBM_SPEC, VMEM_SPEC, HBM_SPEC, HBM_SPEC],
        [steps_space, sizes_space, mod_space, pltpu.VMEM(w_final.shape[::-1], bf16), sems(4)],
        limit=8 << 20,
    )(steps, sizes, all_terms, mods, stay(w_final.T))
    beside = lax.ppermute(masked, "col", near)
    across = lax.ppermute(masked, "col", [(i, i ^ 3) for i in range(cols)])
    result = jax.ShapeDtypeStruct(latent.shape, f32)
    return pl.pallas_call(
        blend_kernel,
        out_shape=(result, result),
        in_specs=[HBM_SPEC] + [VMEM_SPEC] * 3 + [HBM_SPEC],
        out_specs=(VMEM_SPEC, VMEM_SPEC),
        scratch_shapes=[sizes_space, pltpu.VMEM(latent.shape, f32), sems(2)],
        compiler_params=pltpu.CompilerParams(vmem_limit_bytes=8 << 20),
    )(sizes, masked, beside, across, stay(latent))


def solution(mesh):
    placed = (
        P(("row", "col"), None),
        P(("row", "col"), None),
        P("row", "col"),
        P("row", "col"),
        P(),
        P(),
        P(),
        P(),
        P(None, "row"),
        P(),
        P(),
        P("col", "row"),
        P(None, "row"),
        P("row", None),
        P(),
    )
    compact = mesh.shape["row"] == 2 * REQ and mesh.shape["col"] == 4
    return jax.shard_map(
        compact_on_device if compact else on_device,
        mesh=mesh,
        in_specs=placed,
        out_specs=(P(("row", "col"), None), P(("row", "col"), None)),
        check_vma=False,
    )
```

```python
import math

import jax
import jax.numpy as jnp
from jax import lax
from jax.experimental import pallas as pl
from jax.experimental.pallas import tpu as pltpu
from jax.sharding import PartitionSpec as P

REQ = 4
TXT = 256
STEPS = 4


eps_norm = 1e-06
blend = 0.25
mask_floor = -1e30


def with_halo(cells, sides, width):
    for axis, dim in sides:
        count = lax.axis_size(axis)
        ends = count - 1
        head = lax.slice_in_dim(cells, 0, width, axis=dim)
        tail = lax.slice_in_dim(cells, cells.shape[dim] - width, cells.shape[dim], axis=dim)
        cells = jnp.concatenate(
            [
                lax.ppermute(tail, axis, [(i, (i + 1) % count) for i in range(ends)]),
                cells,
                lax.ppermute(head, axis, [((i + 1) % count, i) for i in range(ends)]),
            ],
            axis=dim,
        )
    return cells


def layer_norm(values):
    mean_value = jnp.mean(values, -1, keepdims=True)
    centred = values - mean_value
    return centred * lax.rsqrt(jnp.mean(centred * centred, -1, keepdims=True) + eps_norm)


def modulate(values, shift_vec, scale_vec):
    return (layer_norm(values) * (1.0 + scale_vec) + shift_vec).astype(jnp.bfloat16)


def rope_tables(pos_h, pos_w, head_size):
    time_half = head_size // 16
    axis_dim = (head_size - head_size // 8) // 2
    freq_index = jnp.arange(axis_dim // 2, dtype=jnp.float32)
    frequency = 10000.0 ** (-2.0 * freq_index / axis_dim)
    angles = jnp.concatenate(
        [
            jnp.zeros((pos_h.shape[0], time_half), jnp.float32),
            pos_h[:, None] * frequency[None, :],
            pos_w[:, None] * frequency[None, :],
        ],
        1,
    )
    return (jnp.cos(angles), jnp.sin(angles))


def norm_rope(values, gain_vec, cosine_table, sine_table, head_count, head_size):
    row_total = values.shape[0]
    per_head = values.astype(jnp.float32).reshape(row_total, head_count, head_size)
    per_head = (
        per_head * lax.rsqrt(jnp.mean(per_head * per_head, -1, keepdims=True) + eps_norm) * gain_vec
    )
    paired = per_head.reshape(row_total, head_count, head_size // 2, 2)
    even_part = paired[..., 0]
    odd_part = paired[..., 1]
    cos_wide = cosine_table[:, None, :]
    sin_wide = sine_table[:, None, :]
    turned = jnp.stack(
        [even_part * cos_wide - odd_part * sin_wide, even_part * sin_wide + odd_part * cos_wide], -1
    )
    return turned.reshape(row_total, head_count * head_size).astype(jnp.bfloat16)


def on_device(
    image_states,
    latent,
    text_keys,
    text_values,
    mod_table,
    timestep,
    grid_size,
    rope_offset,
    w_qkv,
    q_gain,
    k_gain,
    w_out,
    w_fc1,
    w_fc2,
    w_final,
):
    col_total = lax.axis_size("col")
    row_pos = lax.axis_index("row")
    col_pos = lax.axis_index("col")
    tile_w = image_states.shape[0]
    width = image_states.shape[1]
    head_size = q_gain.shape[0]
    head_count = width // head_size
    local_heads = head_count // col_total
    request = row_pos % REQ
    grid_row = row_pos // REQ
    grid_col = col_pos * tile_w + jnp.arange(tile_w, dtype=jnp.int32)
    req_slots = jnp.arange(REQ, dtype=jnp.int32)
    req_onehot = req_slots == request
    limits = jnp.sum(jnp.where(req_onehot[:, None], grid_size, 0), 0)
    offsets = jnp.sum(jnp.where(req_onehot[:, None], rope_offset, 0), 0)
    step_now = jnp.sum(jnp.where(req_onehot, timestep, 0))
    token_ok = (grid_row < limits[0]) & (grid_col < limits[1])
    modulation = lax.dynamic_index_in_dim(mod_table, step_now, 0, keepdims=False)
    states = image_states.astype(jnp.float32)
    normed = modulate(states, modulation[0], modulation[1])
    joined_cols = jnp.dot(
        lax.all_gather(normed, "row", axis=0, tiled=True), w_qkv, preferred_element_type=jnp.float32
    ).astype(jnp.bfloat16)
    joined = lax.all_to_all(joined_cols, "row", split_axis=0, concat_axis=1, tiled=True)
    pos_h = jnp.zeros((tile_w,), jnp.float32) + (grid_row + offsets[0]).astype(jnp.float32)
    pos_w = (grid_col + offsets[1]).astype(jnp.float32)
    cosine_table, sine_table = rope_tables(pos_h, pos_w, head_size)
    queries = norm_rope(joined[:, :width], q_gain, cosine_table, sine_table, head_count, head_size)
    image_keys = norm_rope(
        joined[:, width : 2 * width], k_gain, cosine_table, sine_table, head_count, head_size
    )
    q_heads, k_heads, v_heads = (
        lax.all_to_all(queries, "col", split_axis=1, concat_axis=0, tiled=True),
        lax.all_to_all(image_keys, "col", split_axis=1, concat_axis=0, tiled=True),
        lax.all_to_all(joined[:, 2 * width :], "col", split_axis=1, concat_axis=0, tiled=True),
    )
    image_rows = k_heads.shape[0]
    text_rows = text_keys.shape[0]
    shard_rows = image_rows + text_rows
    q_block = q_heads.reshape(image_rows, local_heads, head_size)
    key_rows = jnp.concatenate([k_heads, text_keys], 0)
    value_rows = jnp.concatenate([v_heads, text_values], 0)
    run_max = jnp.full((image_rows, local_heads), mask_floor, jnp.float32)
    key_piece = lax.all_gather(key_rows, "row", axis=0, tiled=True)
    value_piece = lax.all_gather(value_rows, "row", axis=0, tiled=True)
    piece_rows = key_piece.shape[0]
    global_row = jnp.arange(piece_rows, dtype=jnp.int32)
    shard_id = global_row // shard_rows
    within = global_row % shard_rows
    is_image = within < image_rows
    source_col = within // tile_w
    source_cell = within % tile_w
    image_req = shard_id % REQ
    text_req = (shard_id * text_rows + within - image_rows) // TXT
    key_req = jnp.where(is_image, image_req, text_req)
    key_onehot = key_req[:, None] == req_slots[None, :]
    key_height = jnp.sum(jnp.where(key_onehot, grid_size[:, 0][None, :], 0), 1)
    key_width = jnp.sum(jnp.where(key_onehot, grid_size[:, 1][None, :], 0), 1)
    image_ok = (shard_id // REQ < key_height) & (source_col * tile_w + source_cell < key_width)
    key_ok = (key_req == request) & (jnp.logical_not(is_image) | image_ok)
    scores = jnp.einsum(
        "qhd,khd->qhk",
        q_block,
        key_piece.reshape(piece_rows, local_heads, head_size),
        preferred_element_type=jnp.float32,
    ) * head_size ** (-0.5)
    new_max = jnp.maximum(run_max, jnp.max(jnp.where(key_ok, scores, mask_floor), -1))
    weights = jnp.where(key_ok, jnp.exp(scores - new_max[..., None]), 0.0)
    new_sum = jnp.sum(weights, -1)
    new_acc = jnp.einsum(
        "qhk,khd->qhd",
        weights.astype(jnp.bfloat16),
        value_piece.reshape(piece_rows, local_heads, head_size),
        preferred_element_type=jnp.float32,
    )
    mixed = (
        (new_acc / new_sum[..., None])
        .astype(jnp.bfloat16)
        .reshape(image_rows, local_heads * head_size)
    )
    partial_out = jnp.dot(
        mixed, lax.all_gather(w_out, "row", axis=1, tiled=True), preferred_element_type=jnp.float32
    )
    attended = lax.psum_scatter(
        partial_out.astype(jnp.bfloat16), "col", scatter_dimension=0, tiled=True
    ).astype(jnp.float32)
    first_res = (states + modulation[2] * attended).astype(jnp.bfloat16)
    normed_two = modulate(first_res.astype(jnp.float32), modulation[3], modulation[4])
    all_rows = lax.all_gather(normed_two, "row", axis=0, tiled=True)
    hidden = jax.nn.gelu(
        jnp.dot(all_rows, w_fc1, preferred_element_type=jnp.float32), approximate=True
    ).astype(jnp.bfloat16)
    every_term = jnp.dot(hidden, w_fc2, preferred_element_type=jnp.float32)
    every_sum = lax.psum(every_term, "row")
    mlp_out = lax.dynamic_slice_in_dim(every_sum, row_pos * tile_w, tile_w, 0)
    second_res = first_res.astype(jnp.float32) + modulation[5] * mlp_out
    normed_three = modulate(second_res, modulation[6], modulation[7])
    raw_velocity = jnp.dot(normed_three, w_final, preferred_element_type=jnp.float32)
    masked = jnp.where(token_ok[:, None], raw_velocity, 0.0)
    padded = with_halo(masked, (("col", 0),), 1)
    left_side = padded[:-2]
    right_side = padded[2:]
    velocity = jnp.where(
        token_ok[:, None], masked + blend * (left_side + right_side - 2.0 * masked), 0.0
    )
    next_latent = latent + -1.0 / STEPS * velocity
    return (velocity, next_latent)


bf16 = jnp.bfloat16
QKV_CHUNKS = 6
FC_CHUNKS = 6
f32 = jnp.float32
VMEM_SPEC = pl.BlockSpec(memory_space=pltpu.VMEM)
SMEM_SPEC = pl.BlockSpec(memory_space=pltpu.SMEM)
HBM_SPEC = pl.BlockSpec(memory_space=pltpu.HBM)


def start_copies(pairs, sems):
    copies = [pltpu.make_async_copy(source, target, sems.at[i]) for i, (source, target) in enumerate(pairs)]
    for copy in copies:
        copy.start()
    return copies


def row_chunks(source, target, count):
    size = source.shape[0] // count
    return [(source.at[pl.ds(i * size, size), :], target.at[pl.ds(i * size, size), :]) for i in range(count)]


def chunked_dot(values, weights, copies):
    size = weights.shape[0] // len(copies)
    total = None
    for i, copy in enumerate(copies):
        copy.wait()
        term = jnp.dot(
            values[:, i * size : (i + 1) * size], weights[i * size : (i + 1) * size, :], preferred_element_type=f32
        )
        total = term if total is None else total + term
    return total


def lane_mean(values):
    return jnp.mean(values, -1, keepdims=True)


def norm_rows(values):
    centred = values - lane_mean(values)
    return centred * lax.rsqrt(lane_mean(centred * centred) + eps_norm)


def per_request(mod_ref, step_ref, slot, rows_each, start, size):
    pieces = [
        jnp.broadcast_to(mod_ref[step_ref[q], pl.ds(slot, 1), pl.ds(start, size)], (rows_each, size))
        for q in range(REQ)
    ]
    row = lax.broadcasted_iota(jnp.int32, (REQ * rows_each, size), 0) // rows_each
    whole = jnp.concatenate([pieces[0]] * REQ, 0)
    for q in range(1, REQ):
        whole = jnp.where(row == q, jnp.concatenate([pieces[q]] * REQ, 0), whole)
    return whole


def qkv_kernel(step_hbm, tokens_ref, mod_hbm, w_hbm, out_ref, step_ref, order_ref, mod_ref, w_ref, sems):
    row = lax.axis_index("row")
    depth = order_ref.shape[1]
    size = out_ref.shape[2]
    step_copy, mod_copy, *w_copies = start_copies(
        [(step_hbm, step_ref), (mod_hbm, mod_ref)] + row_chunks(w_hbm, w_ref, QKV_CHUNKS), sems
    )
    for q in range(REQ):
        for g in range(2):
            order_ref[4 * q + 2 * g : 4 * q + 2 * g + 2, :] = tokens_ref[REQ * g + q].astype(f32)
    out_ref[...] = jnp.zeros_like(out_ref)
    normed = norm_rows(order_ref[...])
    step_copy.wait()
    mod_copy.wait()
    shift = per_request(mod_ref, step_ref, 0, 4, 0, depth)
    scale = per_request(mod_ref, step_ref, 1, 4, 0, depth)
    normed = (normed * (1.0 + scale) + shift).astype(bf16)
    whole = chunked_dot(normed, w_ref, w_copies).astype(bf16)
    for piece in range(w_ref.shape[1] // size):
        group = lax.rem(row * 3 + piece, 8)
        place = lax.rem(group, 2) * 4 + group // 2
        for q in range(REQ):
            out_ref[8 * q + place] = whole[4 * q : 4 * q + 4, piece * size : (piece + 1) * size]


def give_kernel(k_hbm, v_hbm, out_ref, sems):
    size = out_ref.shape[2]
    start = (1 - lax.rem(lax.axis_index("row"), 2)) * size
    part = pl.ds(pl.multiple_of(start, size), size)
    for copy in start_copies([(k_hbm.at[:, part], out_ref.at[0]), (v_hbm.at[:, part], out_ref.at[1])], sems):
        copy.wait()


def attention_kernel(
    size_hbm, offset_hbm, rows_ref, own_k_hbm, own_v_hbm, other_hbm, q_gain_hbm, k_gain_hbm, out_ref,
    size_ref, offset_ref, q_gain_ref, k_gain_ref, q_ref, k_ref, v_ref, text_k_ref, text_v_ref, sems,
):
    row = lax.axis_index("row")
    col = lax.axis_index("col")
    req = row // 2
    side = lax.rem(row, 2)
    group = 2 * col + side
    width = q_ref.shape[1]
    head = q_gain_hbm.shape[1]
    heads = width // head
    count = q_ref.shape[0]
    half_rows = own_k_hbm.shape[0]
    own = pl.ds(pl.multiple_of(side * width, width), width)
    top_rows = pl.ds(0, half_rows)
    low_rows = pl.ds(half_rows, half_rows)
    *small, copy_k0, copy_k1, copy_v0, copy_v1 = start_copies(
        [
            (offset_hbm, offset_ref),
            (size_hbm, size_ref),
            (q_gain_hbm, q_gain_ref),
            (k_gain_hbm, k_gain_ref),
            (own_k_hbm.at[:, own], text_k_ref.at[top_rows, :]),
            (other_hbm.at[0], text_k_ref.at[low_rows, :]),
            (own_v_hbm.at[:, own], text_v_ref.at[top_rows, :]),
            (other_hbm.at[1], text_v_ref.at[low_rows, :]),
        ],
        sems,
    )
    for which, ref in enumerate((q_ref, k_ref, v_ref)):
        source = (8 * which + group) // 3
        for s in range(4):
            ref[4 * s : 4 * s + 4, :] = rows_ref[source, s].astype(f32)
    for copy in small:
        copy.wait()
    token = lax.broadcasted_iota(jnp.int32, (count, 1), 0)
    pos_h = lax.rem(token, 4) // 2
    pos_w = (token // 4) * 2 + lax.rem(token, 2)
    lane = lax.broadcasted_iota(jnp.int32, (count, head), 1)
    pair = lane // 2
    time_half = head // 16
    axis_dim = (head - head // 8) // 2
    half = axis_dim // 2
    in_h = (pair >= time_half) & (pair < time_half + half)
    index = jnp.where(in_h, pair - time_half, pair - time_half - half).astype(f32)
    frequency = jnp.exp(index * f32(-2.0 * math.log(10000.0) / axis_dim))
    spot = jnp.where(in_h, pos_h + offset_ref[0, req], pos_w + offset_ref[1, req]).astype(f32)
    angle = jnp.where(pair < time_half, 0.0, spot * frequency)
    cosine = jnp.cos(angle)
    sine = jnp.sin(angle)
    even = lax.rem(lane, 2) == 0
    sine = jnp.where(even, -sine, sine)

    def turned(values, gain):
        values = values * lax.rsqrt(lane_mean(values * values) + eps_norm) * gain
        swapped = jnp.where(even, pltpu.roll(values, head - 1, 1), pltpu.roll(values, 1, 1))
        return (values * cosine + swapped * sine).astype(bf16)

    key = lax.broadcasted_iota(jnp.int32, (count, count), 1)
    key_ok = (lax.rem(key, 4) // 2 < size_ref[0, req]) & ((key // 4) * 2 + lax.rem(key, 2) < size_ref[1, req])
    contract = (((1,), (1,)), ((), ()))
    scale = head ** (-0.5)
    queries = [turned(q_ref[:, h * head : (h + 1) * head], q_gain_ref[...]) for h in range(heads)]
    keys = [turned(k_ref[:, h * head : (h + 1) * head], k_gain_ref[...]) for h in range(heads)]
    for copy in (copy_k0, copy_k1, copy_v0, copy_v1):
        copy.wait()
    for h in range(heads):
        cols = slice(h * head, (h + 1) * head)
        v = v_ref[:, cols].astype(bf16)
        s_text = lax.dot_general(queries[h], text_k_ref[:, cols], contract, preferred_element_type=f32) * scale
        s_image = lax.dot_general(queries[h], keys[h], contract, preferred_element_type=f32) * scale
        s_image = jnp.where(key_ok, s_image, mask_floor)
        top = jnp.maximum(jnp.max(s_text, -1, keepdims=True), jnp.max(s_image, -1, keepdims=True))
        w_text = jnp.exp(s_text - top)
        w_image = jnp.where(key_ok, jnp.exp(s_image - top), 0.0)
        total = jnp.sum(w_text, -1, keepdims=True) + jnp.sum(w_image, -1, keepdims=True)
        summed = jnp.dot(w_text.astype(bf16), text_v_ref[:, cols], preferred_element_type=f32) + jnp.dot(
            w_image.astype(bf16), v, preferred_element_type=f32
        )
        mixed = (summed / total).astype(bf16)
        for s in range(4):
            for r in range(8):
                out_ref[4 * r + s, :, cols] = mixed[4 * s : 4 * s + 4, :]


def out_kernel(
    step_hbm, mixed_ref, tokens_ref, mod_hbm, w0_hbm, w1_hbm, w2_hbm, w3_hbm, out_ref, step_ref, rows_ref, states_ref,
    mod_ref, w_ref, sems,
):
    row = lax.axis_index("row")
    col = lax.axis_index("col")
    depth, width = w0_hbm.shape
    piece = mixed_ref.shape[2]
    start = pl.multiple_of(row * width, width)
    step_copy, mod_copy, *w_copies = start_copies(
        [(step_hbm, step_ref), (mod_hbm, mod_ref)]
        + [
            (w_hbm, w_ref.at[pl.ds(pl.multiple_of(jnp.bitwise_xor(col, d) * depth, depth), depth), :])
            for d, w_hbm in enumerate((w0_hbm, w1_hbm, w2_hbm, w3_hbm))
        ],
        sems,
    )
    for r in range(8):
        for s in range(4):
            at = (2 * s + r % 2) * piece
            rows_ref[4 * (r // 2) : 4 * (r // 2) + 4, at : at + piece] = mixed_ref[4 * r + s].astype(f32)
    for q in range(REQ):
        for g in range(2):
            states_ref[4 * q + 2 * g : 4 * q + 2 * g + 2, :] = tokens_ref[REQ * g + q, :, pl.ds(start, width)].astype(f32)
    mixed = rows_ref[...].astype(bf16)
    step_copy.wait()
    mod_copy.wait()
    gate = per_request(mod_ref, step_ref, 2, 4, start, width)
    for copy in w_copies:
        copy.wait()
    attended = jnp.dot(mixed, w_ref[...], preferred_element_type=f32)
    first = (states_ref[...] + gate * attended).astype(bf16)
    for r in range(8):
        out_ref[r] = first


def mlp_kernel(
    step_hbm, first_ref, mod_hbm, w1_hbm, w2_hbm, out_ref, step_ref, rows_ref, mod_ref, w1_ref, w2_ref, sems
):
    row = lax.axis_index("row")
    depth = rows_ref.shape[1]
    piece = first_ref.shape[2]
    step_copy, mod_copy, *w_copies = start_copies(
        [(step_hbm, step_ref), (mod_hbm, mod_ref)]
        + row_chunks(w1_hbm, w1_ref, FC_CHUNKS)
        + row_chunks(w2_hbm, w2_ref, FC_CHUNKS),
        sems,
    )
    for r in range(8):
        rows_ref[:, r * piece : (r + 1) * piece] = first_ref[r].astype(f32)
    normed = norm_rows(rows_ref[...])
    step_copy.wait()
    mod_copy.wait()
    shift = per_request(mod_ref, step_ref, 3, 4, 0, depth)
    scale = per_request(mod_ref, step_ref, 4, 4, 0, depth)
    normed = (normed * (1.0 + scale) + shift).astype(bf16)
    hidden = jax.nn.gelu(chunked_dot(normed, w1_ref, w_copies[:FC_CHUNKS]), approximate=True).astype(bf16)
    added = chunked_dot(hidden, w2_ref, w_copies[FC_CHUNKS:])
    gate = per_request(mod_ref, step_ref, 5, 4, 0, depth)
    mine = jnp.where(row == 0, 1.0, 0.0)
    term = gate * added + mine * rows_ref[...]
    for q in range(REQ):
        for g in range(2):
            out_ref[REQ * g + q] = term[4 * q + 2 * g : 4 * q + 2 * g + 2, :]


def final_kernel(
    step_hbm, size_hbm, terms_ref, mod_hbm, w_hbm, out_ref, live_ref, step_ref, size_ref, mod_ref, w_ref, sems
):
    row = lax.axis_index("row")
    col = lax.axis_index("col")
    req = lax.rem(row, REQ)
    step_copy, size_copy, mod_copy, w_copy = start_copies(
        [(step_hbm, step_ref), (size_hbm, size_ref), (mod_hbm, mod_ref), (w_hbm, w_ref)], sems
    )
    second = terms_ref[0]
    for r in range(1, 8):
        second = second + terms_ref[r]
    normed = norm_rows(second)
    step_copy.wait()
    mod_copy.wait()
    step = step_ref[req]
    normed = (normed * (1.0 + mod_ref[step, 7:8, :]) + mod_ref[step, 6:7, :]).astype(bf16)
    size_copy.wait()
    grid_col = col * out_ref.shape[0] + lax.broadcasted_iota(jnp.int32, out_ref.shape, 0)
    live = (row // REQ < size_ref[0, req]) & (grid_col < size_ref[1, req])
    live_ref[...] = jnp.where(live, 1.0, 0.0)
    w_copy.wait()
    raw = lax.dot_general(normed, w_ref[...], (((1,), (1,)), ((), ())), preferred_element_type=f32)
    out_ref[...] = jnp.where(live, raw, 0.0)


def blend_kernel(masked_ref, live_ref, near_ref, far_ref, latent_ref, velocity_ref, next_ref):
    col = lax.axis_index("col")
    masked = masked_ref[...]
    near = near_ref[...]
    far = jnp.where((col == 1) | (col == 2), far_ref[...], 0.0)
    odd = lax.rem(col, 2) == 1
    count = masked.shape[0]
    left = jnp.concatenate([jnp.where(odd, near, far)[count - 1 :, :], masked[: count - 1, :]], 0)
    right = jnp.concatenate([masked[1:, :], jnp.where(odd, far, near)[:1, :]], 0)
    velocity = jnp.where(live_ref[...] > 0.0, masked + blend * (left + right - 2.0 * masked), 0.0)
    velocity_ref[...] = velocity
    next_ref[...] = latent_ref[...] + -1.0 / STEPS * velocity


def call(kernel, shape, dtype, specs, scratch=(), grid=(), out_spec=None, limit=None):
    return pl.pallas_call(
        kernel,
        out_shape=jax.ShapeDtypeStruct(shape, dtype),
        grid_spec=pltpu.PrefetchScalarGridSpec(
            num_scalar_prefetch=0,
            grid=grid,
            in_specs=specs,
            out_specs=out_spec if out_spec is not None else VMEM_SPEC,
            scratch_shapes=list(scratch),
        ),
        compiler_params=pltpu.CompilerParams(vmem_limit_bytes=limit),
    )


def exchange(values, axes):
    return lax.all_to_all(values, axes, split_axis=0, concat_axis=0, tiled=True)


def compact_on_device(
    image_states, latent, text_keys, text_values, mod_table, timestep, grid_size, rope_offset,
    w_qkv, q_gain, k_gain, w_out, w_fc1, w_fc2, w_final,
):
    rows = lax.axis_size("row")
    cols = lax.axis_size("col")
    stay = lambda values: pltpu.with_memory_space_constraint(values, pltpu.HBM)
    tile_w, width = image_states.shape
    head = q_gain.shape[0]
    piece = width // 8
    tokens = rows * tile_w
    both = ("row", "col")

    spread, w_out = lax.optimization_barrier((jnp.broadcast_to(image_states[None], (rows, tile_w, width)), w_out))
    gathered = exchange(spread, "row")
    given = call(
        give_kernel, (2, text_keys.shape[0], piece), bf16, [HBM_SPEC] * 2, [pltpu.SemaphoreType.DMA((2,))], limit=4 << 20
    )(stay(text_keys), stay(text_values))
    other = lax.ppermute(given, "row", [(i, i ^ 1) for i in range(rows)])
    near = [(i, i ^ 1) for i in range(cols)]
    w_x = lax.ppermute(w_out, "col", [(i, i ^ 2) for i in range(cols)])
    w_k = lax.ppermute(w_out, "col", near)

    sems = lambda count: pltpu.SemaphoreType.DMA((count,))
    mod_space = pltpu.VMEM(mod_table.shape, f32)
    steps_space = pltpu.SMEM(timestep.shape, jnp.int32)
    sizes_space = pltpu.SMEM(grid_size.shape[::-1], jnp.int32)
    gain_space = pltpu.VMEM((1, head), f32)
    steps = stay(timestep)
    sizes = stay(grid_size.T)
    mods = stay(mod_table)
    pieces = call(
        qkv_kernel,
        (rows * cols, 4, piece),
        bf16,
        [HBM_SPEC, VMEM_SPEC, HBM_SPEC, HBM_SPEC],
        [steps_space, pltpu.VMEM((tokens, width), f32), mod_space, pltpu.VMEM(w_qkv.shape, bf16), sems(QKV_CHUNKS + 2)],
        limit=16 << 20,
    )(steps, gathered, mods, stay(w_qkv))
    pieces, other, w_k = lax.optimization_barrier((pieces, other, w_k))
    got = exchange(pieces, both).reshape(rows, cols, 4, piece)
    text_space = pltpu.VMEM((2 * text_keys.shape[0], piece), bf16)
    mixed = call(
        attention_kernel,
        (rows * cols, 4, piece),
        bf16,
        [HBM_SPEC, HBM_SPEC, VMEM_SPEC] + [HBM_SPEC] * 5,
        [sizes_space] * 2 + [gain_space] * 2 + [pltpu.VMEM((tokens, piece), f32)] * 3 + [text_space] * 2 + [sems(8)],
        limit=8 << 20,
    )(
        sizes, stay(rope_offset.T), got, stay(text_keys), stay(text_values), other,
        stay(q_gain.reshape(1, head)), stay(k_gain.reshape(1, head)),
    )
    mixed, w_x = lax.optimization_barrier((mixed, w_x))
    w_xk = lax.ppermute(w_x, "col", near)
    all_mixed = exchange(mixed, both)
    first = call(
        out_kernel,
        (rows, tokens, piece),
        bf16,
        [HBM_SPEC, VMEM_SPEC, VMEM_SPEC] + [HBM_SPEC] * 5,
        [
            steps_space,
            pltpu.VMEM((tokens, width), f32),
            pltpu.VMEM((tokens, piece), f32),
            mod_space,
            pltpu.VMEM((width, piece), bf16),
            sems(6),
        ],
        limit=16 << 20,
    )(steps, all_mixed, gathered, mods, stay(w_out), w_k, w_x, w_xk)
    all_first = exchange(first, "row")
    terms = call(
        mlp_kernel,
        (rows, tile_w, width),
        f32,
        [HBM_SPEC, VMEM_SPEC] + [HBM_SPEC] * 3,
        [
            steps_space,
            pltpu.VMEM((tokens, width), f32),
            mod_space,
            pltpu.VMEM(w_fc1.shape, bf16),
            pltpu.VMEM(w_fc2.shape, bf16),
            sems(2 * FC_CHUNKS + 2),
        ],
        limit=40 << 20,
    )(steps, all_first, mods, stay(w_fc1), stay(w_fc2))
    all_terms = exchange(terms, "row")
    result = jax.ShapeDtypeStruct(latent.shape, f32)
    masked, live = pl.pallas_call(
        final_kernel,
        out_shape=(result, result),
        in_specs=[HBM_SPEC, HBM_SPEC, VMEM_SPEC, HBM_SPEC, HBM_SPEC],
        out_specs=(VMEM_SPEC, VMEM_SPEC),
        scratch_shapes=[steps_space, sizes_space, mod_space, pltpu.VMEM(w_final.shape[::-1], bf16), sems(4)],
        compiler_params=pltpu.CompilerParams(vmem_limit_bytes=8 << 20),
    )(steps, sizes, all_terms, mods, stay(w_final.T))
    beside = lax.ppermute(masked, "col", near)
    across = lax.ppermute(masked, "col", [(i, i ^ 3) for i in range(cols)])
    return pl.pallas_call(
        blend_kernel,
        out_shape=(result, result),
        in_specs=[VMEM_SPEC] * 5,
        out_specs=(VMEM_SPEC, VMEM_SPEC),
        compiler_params=pltpu.CompilerParams(vmem_limit_bytes=8 << 20),
    )(masked, live, beside, across, latent)


def solution(mesh):
    placed = (
        P(("row", "col"), None),
        P(("row", "col"), None),
        P("row", "col"),
        P("row", "col"),
        P(),
        P(),
        P(),
        P(),
        P(None, "row"),
        P(),
        P(),
        P("col", "row"),
        P(None, "row"),
        P("row", None),
        P(),
    )
    compact = mesh.shape["row"] == 2 * REQ and mesh.shape["col"] == 4
    return jax.shard_map(
        compact_on_device if compact else on_device,
        mesh=mesh,
        in_specs=placed,
        out_specs=(P(("row", "col"), None), P(("row", "col"), None)),
        check_vma=False,
    )
```

```python
import math

import jax
import jax.numpy as jnp
from jax import lax
from jax.experimental import pallas as pl
from jax.experimental.pallas import tpu as pltpu
from jax.sharding import PartitionSpec as P

REQ = 4
TXT = 256
STEPS = 4


eps_norm = 1e-06
blend = 0.25
mask_floor = -1e30


def with_halo(cells, sides, width):
    for axis, dim in sides:
        count = lax.axis_size(axis)
        ends = count - 1
        head = lax.slice_in_dim(cells, 0, width, axis=dim)
        tail = lax.slice_in_dim(cells, cells.shape[dim] - width, cells.shape[dim], axis=dim)
        cells = jnp.concatenate(
            [
                lax.ppermute(tail, axis, [(i, (i + 1) % count) for i in range(ends)]),
                cells,
                lax.ppermute(head, axis, [((i + 1) % count, i) for i in range(ends)]),
            ],
            axis=dim,
        )
    return cells


def layer_norm(values):
    mean_value = jnp.mean(values, -1, keepdims=True)
    centred = values - mean_value
    return centred * lax.rsqrt(jnp.mean(centred * centred, -1, keepdims=True) + eps_norm)


def modulate(values, shift_vec, scale_vec):
    return (layer_norm(values) * (1.0 + scale_vec) + shift_vec).astype(jnp.bfloat16)


def rope_tables(pos_h, pos_w, head_size):
    time_half = head_size // 16
    axis_dim = (head_size - head_size // 8) // 2
    freq_index = jnp.arange(axis_dim // 2, dtype=jnp.float32)
    frequency = 10000.0 ** (-2.0 * freq_index / axis_dim)
    angles = jnp.concatenate(
        [
            jnp.zeros((pos_h.shape[0], time_half), jnp.float32),
            pos_h[:, None] * frequency[None, :],
            pos_w[:, None] * frequency[None, :],
        ],
        1,
    )
    return (jnp.cos(angles), jnp.sin(angles))


def norm_rope(values, gain_vec, cosine_table, sine_table, head_count, head_size):
    row_total = values.shape[0]
    per_head = values.astype(jnp.float32).reshape(row_total, head_count, head_size)
    per_head = (
        per_head * lax.rsqrt(jnp.mean(per_head * per_head, -1, keepdims=True) + eps_norm) * gain_vec
    )
    paired = per_head.reshape(row_total, head_count, head_size // 2, 2)
    even_part = paired[..., 0]
    odd_part = paired[..., 1]
    cos_wide = cosine_table[:, None, :]
    sin_wide = sine_table[:, None, :]
    turned = jnp.stack(
        [even_part * cos_wide - odd_part * sin_wide, even_part * sin_wide + odd_part * cos_wide], -1
    )
    return turned.reshape(row_total, head_count * head_size).astype(jnp.bfloat16)


def on_device(
    image_states,
    latent,
    text_keys,
    text_values,
    mod_table,
    timestep,
    grid_size,
    rope_offset,
    w_qkv,
    q_gain,
    k_gain,
    w_out,
    w_fc1,
    w_fc2,
    w_final,
):
    col_total = lax.axis_size("col")
    row_pos = lax.axis_index("row")
    col_pos = lax.axis_index("col")
    tile_w = image_states.shape[0]
    width = image_states.shape[1]
    head_size = q_gain.shape[0]
    head_count = width // head_size
    local_heads = head_count // col_total
    request = row_pos % REQ
    grid_row = row_pos // REQ
    grid_col = col_pos * tile_w + jnp.arange(tile_w, dtype=jnp.int32)
    req_slots = jnp.arange(REQ, dtype=jnp.int32)
    req_onehot = req_slots == request
    limits = jnp.sum(jnp.where(req_onehot[:, None], grid_size, 0), 0)
    offsets = jnp.sum(jnp.where(req_onehot[:, None], rope_offset, 0), 0)
    step_now = jnp.sum(jnp.where(req_onehot, timestep, 0))
    token_ok = (grid_row < limits[0]) & (grid_col < limits[1])
    modulation = lax.dynamic_index_in_dim(mod_table, step_now, 0, keepdims=False)
    states = image_states.astype(jnp.float32)
    normed = modulate(states, modulation[0], modulation[1])
    joined_cols = jnp.dot(
        lax.all_gather(normed, "row", axis=0, tiled=True), w_qkv, preferred_element_type=jnp.float32
    ).astype(jnp.bfloat16)
    joined = lax.all_to_all(joined_cols, "row", split_axis=0, concat_axis=1, tiled=True)
    pos_h = jnp.zeros((tile_w,), jnp.float32) + (grid_row + offsets[0]).astype(jnp.float32)
    pos_w = (grid_col + offsets[1]).astype(jnp.float32)
    cosine_table, sine_table = rope_tables(pos_h, pos_w, head_size)
    queries = norm_rope(joined[:, :width], q_gain, cosine_table, sine_table, head_count, head_size)
    image_keys = norm_rope(
        joined[:, width : 2 * width], k_gain, cosine_table, sine_table, head_count, head_size
    )
    q_heads, k_heads, v_heads = (
        lax.all_to_all(queries, "col", split_axis=1, concat_axis=0, tiled=True),
        lax.all_to_all(image_keys, "col", split_axis=1, concat_axis=0, tiled=True),
        lax.all_to_all(joined[:, 2 * width :], "col", split_axis=1, concat_axis=0, tiled=True),
    )
    image_rows = k_heads.shape[0]
    text_rows = text_keys.shape[0]
    shard_rows = image_rows + text_rows
    q_block = q_heads.reshape(image_rows, local_heads, head_size)
    key_rows = jnp.concatenate([k_heads, text_keys], 0)
    value_rows = jnp.concatenate([v_heads, text_values], 0)
    run_max = jnp.full((image_rows, local_heads), mask_floor, jnp.float32)
    key_piece = lax.all_gather(key_rows, "row", axis=0, tiled=True)
    value_piece = lax.all_gather(value_rows, "row", axis=0, tiled=True)
    piece_rows = key_piece.shape[0]
    global_row = jnp.arange(piece_rows, dtype=jnp.int32)
    shard_id = global_row // shard_rows
    within = global_row % shard_rows
    is_image = within < image_rows
    source_col = within // tile_w
    source_cell = within % tile_w
    image_req = shard_id % REQ
    text_req = (shard_id * text_rows + within - image_rows) // TXT
    key_req = jnp.where(is_image, image_req, text_req)
    key_onehot = key_req[:, None] == req_slots[None, :]
    key_height = jnp.sum(jnp.where(key_onehot, grid_size[:, 0][None, :], 0), 1)
    key_width = jnp.sum(jnp.where(key_onehot, grid_size[:, 1][None, :], 0), 1)
    image_ok = (shard_id // REQ < key_height) & (source_col * tile_w + source_cell < key_width)
    key_ok = (key_req == request) & (jnp.logical_not(is_image) | image_ok)
    scores = jnp.einsum(
        "qhd,khd->qhk",
        q_block,
        key_piece.reshape(piece_rows, local_heads, head_size),
        preferred_element_type=jnp.float32,
    ) * head_size ** (-0.5)
    new_max = jnp.maximum(run_max, jnp.max(jnp.where(key_ok, scores, mask_floor), -1))
    weights = jnp.where(key_ok, jnp.exp(scores - new_max[..., None]), 0.0)
    new_sum = jnp.sum(weights, -1)
    new_acc = jnp.einsum(
        "qhk,khd->qhd",
        weights.astype(jnp.bfloat16),
        value_piece.reshape(piece_rows, local_heads, head_size),
        preferred_element_type=jnp.float32,
    )
    mixed = (
        (new_acc / new_sum[..., None])
        .astype(jnp.bfloat16)
        .reshape(image_rows, local_heads * head_size)
    )
    partial_out = jnp.dot(
        mixed, lax.all_gather(w_out, "row", axis=1, tiled=True), preferred_element_type=jnp.float32
    )
    attended = lax.psum_scatter(
        partial_out.astype(jnp.bfloat16), "col", scatter_dimension=0, tiled=True
    ).astype(jnp.float32)
    first_res = (states + modulation[2] * attended).astype(jnp.bfloat16)
    normed_two = modulate(first_res.astype(jnp.float32), modulation[3], modulation[4])
    all_rows = lax.all_gather(normed_two, "row", axis=0, tiled=True)
    hidden = jax.nn.gelu(
        jnp.dot(all_rows, w_fc1, preferred_element_type=jnp.float32), approximate=True
    ).astype(jnp.bfloat16)
    every_term = jnp.dot(hidden, w_fc2, preferred_element_type=jnp.float32)
    every_sum = lax.psum(every_term, "row")
    mlp_out = lax.dynamic_slice_in_dim(every_sum, row_pos * tile_w, tile_w, 0)
    second_res = first_res.astype(jnp.float32) + modulation[5] * mlp_out
    normed_three = modulate(second_res, modulation[6], modulation[7])
    raw_velocity = jnp.dot(normed_three, w_final, preferred_element_type=jnp.float32)
    masked = jnp.where(token_ok[:, None], raw_velocity, 0.0)
    padded = with_halo(masked, (("col", 0),), 1)
    left_side = padded[:-2]
    right_side = padded[2:]
    velocity = jnp.where(
        token_ok[:, None], masked + blend * (left_side + right_side - 2.0 * masked), 0.0
    )
    next_latent = latent + -1.0 / STEPS * velocity
    return (velocity, next_latent)


bf16 = jnp.bfloat16
QKV_CHUNKS = 6
FC_CHUNKS = 6
f32 = jnp.float32
VMEM_SPEC = pl.BlockSpec(memory_space=pltpu.VMEM)
SMEM_SPEC = pl.BlockSpec(memory_space=pltpu.SMEM)
HBM_SPEC = pl.BlockSpec(memory_space=pltpu.HBM)


def start_copies(pairs, sems):
    copies = [pltpu.make_async_copy(source, target, sems.at[i]) for i, (source, target) in enumerate(pairs)]
    for copy in copies:
        copy.start()
    return copies


def row_chunks(source, target, count):
    size = source.shape[0] // count
    return [(source.at[pl.ds(i * size, size), :], target.at[pl.ds(i * size, size), :]) for i in range(count)]


def chunked_dot(values, weights, copies):
    size = weights.shape[0] // len(copies)
    total = None
    for i, copy in enumerate(copies):
        copy.wait()
        term = jnp.dot(
            values[:, i * size : (i + 1) * size], weights[i * size : (i + 1) * size, :], preferred_element_type=f32
        )
        total = term if total is None else total + term
    return total


def lane_mean(values):
    return jnp.mean(values, -1, keepdims=True)


def norm_rows(values):
    centred = values - lane_mean(values)
    return centred * lax.rsqrt(lane_mean(centred * centred) + eps_norm)


def per_request(mod_ref, step_ref, slot, rows_each, start, size):
    pieces = [
        jnp.broadcast_to(mod_ref[step_ref[q], pl.ds(slot, 1), pl.ds(start, size)], (rows_each, size))
        for q in range(REQ)
    ]
    row = lax.broadcasted_iota(jnp.int32, (REQ * rows_each, size), 0) // rows_each
    whole = jnp.concatenate([pieces[0]] * REQ, 0)
    for q in range(1, REQ):
        whole = jnp.where(row == q, jnp.concatenate([pieces[q]] * REQ, 0), whole)
    return whole


def qkv_kernel(step_hbm, tokens_ref, mod_hbm, w_ref, out_ref, step_ref, order_ref, mod_ref, sems):
    row = lax.axis_index("row")
    depth = order_ref.shape[1]
    size = out_ref.shape[2]
    step_copy, mod_copy = start_copies([(step_hbm, step_ref), (mod_hbm, mod_ref)], sems)
    for q in range(REQ):
        for g in range(2):
            order_ref[4 * q + 2 * g : 4 * q + 2 * g + 2, :] = tokens_ref[REQ * g + q].astype(f32)
    out_ref[...] = jnp.zeros_like(out_ref)
    normed = norm_rows(order_ref[...])
    step_copy.wait()
    mod_copy.wait()
    shift = per_request(mod_ref, step_ref, 0, 4, 0, depth)
    scale = per_request(mod_ref, step_ref, 1, 4, 0, depth)
    normed = (normed * (1.0 + scale) + shift).astype(bf16)
    whole = jnp.dot(normed, w_ref[...], preferred_element_type=f32).astype(bf16)
    for piece in range(w_ref.shape[1] // size):
        group = lax.rem(row * 3 + piece, 8)
        place = lax.rem(group, 2) * 4 + group // 2
        for q in range(REQ):
            out_ref[8 * q + place] = whole[4 * q : 4 * q + 4, piece * size : (piece + 1) * size]


def opening_kernel(states_hbm, k_hbm, v_hbm, spread_ref, given_ref, sems):
    size = given_ref.shape[2]
    start = (1 - lax.rem(lax.axis_index("row"), 2)) * size
    part = pl.ds(pl.multiple_of(start, size), size)
    pairs = [(k_hbm.at[:, part], given_ref.at[0]), (v_hbm.at[:, part], given_ref.at[1])]
    pairs += [(states_hbm, spread_ref.at[r]) for r in range(spread_ref.shape[0])]
    for copy in start_copies(pairs, sems):
        copy.wait()


def attention_kernel(
    size_hbm, offset_hbm, rows_ref, own_k_hbm, own_v_hbm, other_hbm, q_gain_hbm, k_gain_hbm, out_ref,
    size_ref, offset_ref, q_gain_ref, k_gain_ref, q_ref, k_ref, v_ref, text_k_ref, text_v_ref, sems,
):
    row = lax.axis_index("row")
    col = lax.axis_index("col")
    req = row // 2
    side = lax.rem(row, 2)
    group = 2 * col + side
    width = q_ref.shape[1]
    head = q_gain_hbm.shape[1]
    heads = width // head
    count = q_ref.shape[0]
    half_rows = own_k_hbm.shape[0]
    own = pl.ds(pl.multiple_of(side * width, width), width)
    top_rows = pl.ds(0, half_rows)
    low_rows = pl.ds(half_rows, half_rows)
    *small, copy_k0, copy_k1, copy_v0, copy_v1 = start_copies(
        [
            (offset_hbm, offset_ref),
            (size_hbm, size_ref),
            (q_gain_hbm, q_gain_ref),
            (k_gain_hbm, k_gain_ref),
            (own_k_hbm.at[:, own], text_k_ref.at[top_rows, :]),
            (other_hbm.at[0], text_k_ref.at[low_rows, :]),
            (own_v_hbm.at[:, own], text_v_ref.at[top_rows, :]),
            (other_hbm.at[1], text_v_ref.at[low_rows, :]),
        ],
        sems,
    )
    for which, ref in enumerate((q_ref, k_ref, v_ref)):
        source = (8 * which + group) // 3
        for s in range(4):
            ref[4 * s : 4 * s + 4, :] = rows_ref[source, s].astype(f32)
    for copy in small:
        copy.wait()
    token = lax.broadcasted_iota(jnp.int32, (count, 1), 0)
    pos_h = lax.rem(token, 4) // 2
    pos_w = (token // 4) * 2 + lax.rem(token, 2)
    lane = lax.broadcasted_iota(jnp.int32, (count, head), 1)
    pair = lane // 2
    time_half = head // 16
    axis_dim = (head - head // 8) // 2
    half = axis_dim // 2
    in_h = (pair >= time_half) & (pair < time_half + half)
    index = jnp.where(in_h, pair - time_half, pair - time_half - half).astype(f32)
    frequency = jnp.exp(index * f32(-2.0 * math.log(10000.0) / axis_dim))
    spot = jnp.where(in_h, pos_h + offset_ref[0, req], pos_w + offset_ref[1, req]).astype(f32)
    angle = jnp.where(pair < time_half, 0.0, spot * frequency)
    cosine = jnp.cos(angle)
    sine = jnp.sin(angle)
    even = lax.rem(lane, 2) == 0
    sine = jnp.where(even, -sine, sine)

    def turned(values, gain):
        values = values * lax.rsqrt(lane_mean(values * values) + eps_norm) * gain
        swapped = jnp.where(even, pltpu.roll(values, head - 1, 1), pltpu.roll(values, 1, 1))
        return (values * cosine + swapped * sine).astype(bf16)

    key = lax.broadcasted_iota(jnp.int32, (count, count), 1)
    key_ok = (lax.rem(key, 4) // 2 < size_ref[0, req]) & ((key // 4) * 2 + lax.rem(key, 2) < size_ref[1, req])
    contract = (((1,), (1,)), ((), ()))
    scale = head ** (-0.5)
    queries = [turned(q_ref[:, h * head : (h + 1) * head], q_gain_ref[...]) for h in range(heads)]
    keys = [turned(k_ref[:, h * head : (h + 1) * head], k_gain_ref[...]) for h in range(heads)]
    for copy in (copy_k0, copy_k1, copy_v0, copy_v1):
        copy.wait()
    for h in range(heads):
        cols = slice(h * head, (h + 1) * head)
        v = v_ref[:, cols].astype(bf16)
        s_text = lax.dot_general(queries[h], text_k_ref[:, cols], contract, preferred_element_type=f32) * scale
        s_image = lax.dot_general(queries[h], keys[h], contract, preferred_element_type=f32) * scale
        s_image = jnp.where(key_ok, s_image, mask_floor)
        top = jnp.maximum(jnp.max(s_text, -1, keepdims=True), jnp.max(s_image, -1, keepdims=True))
        w_text = jnp.exp(s_text - top)
        w_image = jnp.where(key_ok, jnp.exp(s_image - top), 0.0)
        total = jnp.sum(w_text, -1, keepdims=True) + jnp.sum(w_image, -1, keepdims=True)
        summed = jnp.dot(w_text.astype(bf16), text_v_ref[:, cols], preferred_element_type=f32) + jnp.dot(
            w_image.astype(bf16), v, preferred_element_type=f32
        )
        mixed = (summed / total).astype(bf16)
        for s in range(4):
            for r in range(8):
                out_ref[4 * r + s, :, cols] = mixed[4 * s : 4 * s + 4, :]


def out_kernel(
    step_hbm, mixed_ref, tokens_ref, mod_hbm, own_hbm, w1_ref, w2_ref, w3_ref, out_ref, step_ref, rows_ref, states_ref,
    mod_ref, w0_ref, sems,
):
    row = lax.axis_index("row")
    col = lax.axis_index("col")
    depth, width = own_hbm.shape
    piece = mixed_ref.shape[2]
    start = pl.multiple_of(row * width, width)
    w_copy, step_copy, mod_copy = start_copies([(own_hbm, w0_ref), (step_hbm, step_ref), (mod_hbm, mod_ref)], sems)
    for r in range(8):
        for s in range(4):
            at = (2 * s + r % 2) * piece
            rows_ref[4 * (r // 2) : 4 * (r // 2) + 4, at : at + piece] = mixed_ref[4 * r + s].astype(f32)
    for q in range(REQ):
        for g in range(2):
            states_ref[4 * q + 2 * g : 4 * q + 2 * g + 2, :] = tokens_ref[REQ * g + q, :, pl.ds(start, width)].astype(f32)

    def share(d, w_ref):
        at = pl.multiple_of(jnp.bitwise_xor(col, d) * depth, depth)
        return jnp.dot(rows_ref[:, pl.ds(at, depth)].astype(bf16), w_ref[...], preferred_element_type=f32)

    attended = share(1, w1_ref) + share(2, w2_ref) + share(3, w3_ref)
    w_copy.wait()
    attended = attended + share(0, w0_ref)
    step_copy.wait()
    mod_copy.wait()
    gate = per_request(mod_ref, step_ref, 2, 4, start, width)
    first = (states_ref[...] + gate * attended).astype(bf16)
    for r in range(8):
        out_ref[r] = first


def mlp_kernel(
    step_hbm, first_ref, mod_hbm, w1_ref, w2_hbm, out_ref, own_ref, step_ref, rows_ref, mod_ref, w2_ref, sems
):
    row = lax.axis_index("row")
    depth = rows_ref.shape[1]
    piece = first_ref.shape[2]
    step_copy, mod_copy, *w_copies = start_copies(
        [(step_hbm, step_ref), (mod_hbm, mod_ref)]
        + row_chunks(w2_hbm, w2_ref, FC_CHUNKS),
        sems,
    )
    for r in range(8):
        rows_ref[:, r * piece : (r + 1) * piece] = first_ref[r].astype(f32)
    normed = norm_rows(rows_ref[...])
    step_copy.wait()
    mod_copy.wait()
    shift = per_request(mod_ref, step_ref, 3, 4, 0, depth)
    scale = per_request(mod_ref, step_ref, 4, 4, 0, depth)
    normed = (normed * (1.0 + scale) + shift).astype(bf16)
    own = rows_ref[0:2, :]
    for q in range(REQ):
        for g in range(2):
            own = jnp.where(row == REQ * g + q, rows_ref[4 * q + 2 * g : 4 * q + 2 * g + 2, :], own)
    own_ref[...] = own
    hidden = jax.nn.gelu(
        jnp.dot(normed, w1_ref[...], preferred_element_type=f32), approximate=True
    ).astype(bf16)
    added = chunked_dot(hidden, w2_ref, w_copies)
    gate = per_request(mod_ref, step_ref, 5, 4, 0, depth)
    term = (gate * added).astype(out_ref.dtype)
    for q in range(REQ):
        for g in range(2):
            out_ref[REQ * g + q] = term[4 * q + 2 * g : 4 * q + 2 * g + 2, :]


def final_kernel(
    step_hbm, size_hbm, terms_ref, first_ref, mod_hbm, w_hbm, out_ref, live_ref, step_ref, size_ref, mod_ref, w_ref, sems
):
    row = lax.axis_index("row")
    col = lax.axis_index("col")
    req = lax.rem(row, REQ)
    step_copy, size_copy, mod_copy, w_copy = start_copies(
        [(step_hbm, step_ref), (size_hbm, size_ref), (mod_hbm, mod_ref), (w_hbm, w_ref)], sems
    )
    second = first_ref[...]
    for r in range(8):
        second = second + terms_ref[r].astype(f32)
    normed = norm_rows(second)
    step_copy.wait()
    mod_copy.wait()
    step = step_ref[req]
    normed = (normed * (1.0 + mod_ref[step, 7:8, :]) + mod_ref[step, 6:7, :]).astype(bf16)
    size_copy.wait()
    grid_col = col * out_ref.shape[0] + lax.broadcasted_iota(jnp.int32, out_ref.shape, 0)
    live = (row // REQ < size_ref[0, req]) & (grid_col < size_ref[1, req])
    live_ref[...] = jnp.where(live, 1.0, 0.0)
    w_copy.wait()
    raw = lax.dot_general(normed, w_ref[...], (((1,), (1,)), ((), ())), preferred_element_type=f32)
    out_ref[...] = jnp.where(live, raw, 0.0)


def blend_kernel(masked_ref, live_ref, near_ref, far_ref, latent_ref, velocity_ref, next_ref):
    col = lax.axis_index("col")
    masked = masked_ref[...]
    near = near_ref[...]
    far = jnp.where((col == 1) | (col == 2), far_ref[...], 0.0)
    odd = lax.rem(col, 2) == 1
    count = masked.shape[0]
    left = jnp.concatenate([jnp.where(odd, near, far)[count - 1 :, :], masked[: count - 1, :]], 0)
    right = jnp.concatenate([masked[1:, :], jnp.where(odd, far, near)[:1, :]], 0)
    velocity = jnp.where(live_ref[...] > 0.0, masked + blend * (left + right - 2.0 * masked), 0.0)
    velocity_ref[...] = velocity
    next_ref[...] = latent_ref[...] + -1.0 / STEPS * velocity


def call(kernel, shape, dtype, specs, scratch=(), grid=(), out_spec=None, limit=None):
    return pl.pallas_call(
        kernel,
        out_shape=jax.ShapeDtypeStruct(shape, dtype),
        grid_spec=pltpu.PrefetchScalarGridSpec(
            num_scalar_prefetch=0,
            grid=grid,
            in_specs=specs,
            out_specs=out_spec if out_spec is not None else VMEM_SPEC,
            scratch_shapes=list(scratch),
        ),
        compiler_params=pltpu.CompilerParams(vmem_limit_bytes=limit),
    )


def exchange(values, axes):
    return lax.all_to_all(values, axes, split_axis=0, concat_axis=0, tiled=True)


def compact_on_device(
    image_states, latent, text_keys, text_values, mod_table, timestep, grid_size, rope_offset,
    w_qkv, q_gain, k_gain, w_out, w_fc1, w_fc2, w_final,
):
    rows = lax.axis_size("row")
    cols = lax.axis_size("col")
    stay = lambda values: pltpu.with_memory_space_constraint(values, pltpu.HBM)
    tile_w, width = image_states.shape
    head = q_gain.shape[0]
    piece = width // 8
    tokens = rows * tile_w
    both = ("row", "col")

    near = [(i, i ^ 1) for i in range(cols)]
    spread, given = pl.pallas_call(
        opening_kernel,
        out_shape=(
            jax.ShapeDtypeStruct((rows, tile_w, width), bf16),
            jax.ShapeDtypeStruct((2, text_keys.shape[0], piece), bf16),
        ),
        in_specs=[HBM_SPEC] * 3,
        out_specs=(VMEM_SPEC, VMEM_SPEC),
        scratch_shapes=[pltpu.SemaphoreType.DMA((rows + 2,))],
        compiler_params=pltpu.CompilerParams(vmem_limit_bytes=4 << 20),
    )(stay(image_states), stay(text_keys), stay(text_values))
    other = lax.ppermute(given, "row", [(i, i ^ 1) for i in range(rows)])
    w_x = lax.ppermute(w_out, "col", [(i, i ^ 2) for i in range(cols)])
    w_k = lax.ppermute(w_out, "col", near)
    gathered = exchange(spread, "row")

    sems = lambda count: pltpu.SemaphoreType.DMA((count,))
    mod_space = pltpu.VMEM(mod_table.shape, f32)
    steps_space = pltpu.SMEM(timestep.shape, jnp.int32)
    sizes_space = pltpu.SMEM(grid_size.shape[::-1], jnp.int32)
    gain_space = pltpu.VMEM((1, head), f32)
    steps = stay(timestep)
    sizes = stay(grid_size.T)
    mods = stay(mod_table)
    pieces = call(
        qkv_kernel,
        (rows * cols, 4, piece),
        bf16,
        [HBM_SPEC, VMEM_SPEC, HBM_SPEC, VMEM_SPEC],
        [steps_space, pltpu.VMEM((tokens, width), f32), mod_space, sems(2)],
        limit=8 << 20,
    )(steps, gathered, mods, lax.ppermute(w_qkv, "col", near))
    pieces, other, w_k = lax.optimization_barrier((pieces, other, w_k))
    got = exchange(pieces, both).reshape(rows, cols, 4, piece)
    text_space = pltpu.VMEM((2 * text_keys.shape[0], piece), bf16)
    mixed = call(
        attention_kernel,
        (rows * cols, 4, piece),
        bf16,
        [HBM_SPEC, HBM_SPEC, VMEM_SPEC] + [HBM_SPEC] * 5,
        [sizes_space] * 2 + [gain_space] * 2 + [pltpu.VMEM((tokens, piece), f32)] * 3 + [text_space] * 2 + [sems(8)],
        limit=8 << 20,
    )(
        sizes, stay(rope_offset.T), got, stay(text_keys), stay(text_values), other,
        stay(q_gain.reshape(1, head)), stay(k_gain.reshape(1, head)),
    )
    mixed, w_x = lax.optimization_barrier((mixed, w_x))
    w_xk = lax.ppermute(w_x, "col", near)
    all_mixed = exchange(mixed, both)
    first = call(
        out_kernel,
        (rows, tokens, piece),
        bf16,
        [HBM_SPEC, VMEM_SPEC, VMEM_SPEC, HBM_SPEC, HBM_SPEC] + [VMEM_SPEC] * 3,
        [
            steps_space,
            pltpu.VMEM((tokens, width), f32),
            pltpu.VMEM((tokens, piece), f32),
            mod_space,
            pltpu.VMEM(w_out.shape, bf16),
            sems(3),
        ],
        limit=8 << 20,
    )(steps, all_mixed, gathered, mods, stay(w_out), w_k, w_x, w_xk)
    all_first = exchange(first, "row")
    terms, first_own = pl.pallas_call(
        mlp_kernel,
        out_shape=(
            jax.ShapeDtypeStruct((rows, tile_w, width), bf16),
            jax.ShapeDtypeStruct((tile_w, width), f32),
        ),
        in_specs=[HBM_SPEC, VMEM_SPEC, HBM_SPEC, VMEM_SPEC, HBM_SPEC],
        out_specs=(VMEM_SPEC, VMEM_SPEC),
        scratch_shapes=[
            steps_space,
            pltpu.VMEM((tokens, width), f32),
            mod_space,
            pltpu.VMEM(w_fc2.shape, bf16),
            sems(FC_CHUNKS + 2),
        ],
        compiler_params=pltpu.CompilerParams(vmem_limit_bytes=16 << 20),
    )(steps, all_first, mods, w_fc1, stay(w_fc2))
    all_terms = exchange(terms, "row")
    result = jax.ShapeDtypeStruct(latent.shape, f32)
    masked, live = pl.pallas_call(
        final_kernel,
        out_shape=(result, result),
        in_specs=[HBM_SPEC, HBM_SPEC, VMEM_SPEC, VMEM_SPEC, HBM_SPEC, HBM_SPEC],
        out_specs=(VMEM_SPEC, VMEM_SPEC),
        scratch_shapes=[steps_space, sizes_space, mod_space, pltpu.VMEM(w_final.shape[::-1], bf16), sems(4)],
        compiler_params=pltpu.CompilerParams(vmem_limit_bytes=8 << 20),
    )(steps, sizes, all_terms, first_own, mods, stay(w_final.T))
    beside = lax.ppermute(masked, "col", near)
    across = lax.ppermute(masked, "col", [(i, i ^ 3) for i in range(cols)])
    return pl.pallas_call(
        blend_kernel,
        out_shape=(result, result),
        in_specs=[VMEM_SPEC] * 5,
        out_specs=(VMEM_SPEC, VMEM_SPEC),
        compiler_params=pltpu.CompilerParams(vmem_limit_bytes=8 << 20),
    )(masked, live, beside, across, latent)


def solution(mesh):
    placed = (
        P(("row", "col"), None),
        P(("row", "col"), None),
        P("row", "col"),
        P("row", "col"),
        P(),
        P(),
        P(),
        P(),
        P(None, "row"),
        P(),
        P(),
        P("col", "row"),
        P(None, "row"),
        P("row", None),
        P(),
    )
    compact = mesh.shape["row"] == 2 * REQ and mesh.shape["col"] == 4
    return jax.shard_map(
        compact_on_device if compact else on_device,
        mesh=mesh,
        in_specs=placed,
        out_specs=(P(("row", "col"), None), P(("row", "col"), None)),
        check_vma=False,
    )
```

```python
import math

import jax
import jax.numpy as jnp
from jax import lax
from jax.experimental import pallas as pl
from jax.experimental.pallas import tpu as pltpu
from jax.sharding import PartitionSpec as P

REQ = 4
TXT = 256
STEPS = 4


eps_norm = 1e-06
blend = 0.25
mask_floor = -1e30


def with_halo(cells, sides, width):
    for axis, dim in sides:
        count = lax.axis_size(axis)
        ends = count - 1
        head = lax.slice_in_dim(cells, 0, width, axis=dim)
        tail = lax.slice_in_dim(cells, cells.shape[dim] - width, cells.shape[dim], axis=dim)
        cells = jnp.concatenate(
            [
                lax.ppermute(tail, axis, [(i, (i + 1) % count) for i in range(ends)]),
                cells,
                lax.ppermute(head, axis, [((i + 1) % count, i) for i in range(ends)]),
            ],
            axis=dim,
        )
    return cells


def layer_norm(values):
    mean_value = jnp.mean(values, -1, keepdims=True)
    centred = values - mean_value
    return centred * lax.rsqrt(jnp.mean(centred * centred, -1, keepdims=True) + eps_norm)


def modulate(values, shift_vec, scale_vec):
    return (layer_norm(values) * (1.0 + scale_vec) + shift_vec).astype(jnp.bfloat16)


def rope_tables(pos_h, pos_w, head_size):
    time_half = head_size // 16
    axis_dim = (head_size - head_size // 8) // 2
    freq_index = jnp.arange(axis_dim // 2, dtype=jnp.float32)
    frequency = 10000.0 ** (-2.0 * freq_index / axis_dim)
    angles = jnp.concatenate(
        [
            jnp.zeros((pos_h.shape[0], time_half), jnp.float32),
            pos_h[:, None] * frequency[None, :],
            pos_w[:, None] * frequency[None, :],
        ],
        1,
    )
    return (jnp.cos(angles), jnp.sin(angles))


def norm_rope(values, gain_vec, cosine_table, sine_table, head_count, head_size):
    row_total = values.shape[0]
    per_head = values.astype(jnp.float32).reshape(row_total, head_count, head_size)
    per_head = (
        per_head * lax.rsqrt(jnp.mean(per_head * per_head, -1, keepdims=True) + eps_norm) * gain_vec
    )
    paired = per_head.reshape(row_total, head_count, head_size // 2, 2)
    even_part = paired[..., 0]
    odd_part = paired[..., 1]
    cos_wide = cosine_table[:, None, :]
    sin_wide = sine_table[:, None, :]
    turned = jnp.stack(
        [even_part * cos_wide - odd_part * sin_wide, even_part * sin_wide + odd_part * cos_wide], -1
    )
    return turned.reshape(row_total, head_count * head_size).astype(jnp.bfloat16)


def on_device(
    image_states,
    latent,
    text_keys,
    text_values,
    mod_table,
    timestep,
    grid_size,
    rope_offset,
    w_qkv,
    q_gain,
    k_gain,
    w_out,
    w_fc1,
    w_fc2,
    w_final,
):
    col_total = lax.axis_size("col")
    row_pos = lax.axis_index("row")
    col_pos = lax.axis_index("col")
    tile_w = image_states.shape[0]
    width = image_states.shape[1]
    head_size = q_gain.shape[0]
    head_count = width // head_size
    local_heads = head_count // col_total
    request = row_pos % REQ
    grid_row = row_pos // REQ
    grid_col = col_pos * tile_w + jnp.arange(tile_w, dtype=jnp.int32)
    req_slots = jnp.arange(REQ, dtype=jnp.int32)
    req_onehot = req_slots == request
    limits = jnp.sum(jnp.where(req_onehot[:, None], grid_size, 0), 0)
    offsets = jnp.sum(jnp.where(req_onehot[:, None], rope_offset, 0), 0)
    step_now = jnp.sum(jnp.where(req_onehot, timestep, 0))
    token_ok = (grid_row < limits[0]) & (grid_col < limits[1])
    modulation = lax.dynamic_index_in_dim(mod_table, step_now, 0, keepdims=False)
    states = image_states.astype(jnp.float32)
    normed = modulate(states, modulation[0], modulation[1])
    joined_cols = jnp.dot(
        lax.all_gather(normed, "row", axis=0, tiled=True), w_qkv, preferred_element_type=jnp.float32
    ).astype(jnp.bfloat16)
    joined = lax.all_to_all(joined_cols, "row", split_axis=0, concat_axis=1, tiled=True)
    pos_h = jnp.zeros((tile_w,), jnp.float32) + (grid_row + offsets[0]).astype(jnp.float32)
    pos_w = (grid_col + offsets[1]).astype(jnp.float32)
    cosine_table, sine_table = rope_tables(pos_h, pos_w, head_size)
    queries = norm_rope(joined[:, :width], q_gain, cosine_table, sine_table, head_count, head_size)
    image_keys = norm_rope(
        joined[:, width : 2 * width], k_gain, cosine_table, sine_table, head_count, head_size
    )
    q_heads, k_heads, v_heads = (
        lax.all_to_all(queries, "col", split_axis=1, concat_axis=0, tiled=True),
        lax.all_to_all(image_keys, "col", split_axis=1, concat_axis=0, tiled=True),
        lax.all_to_all(joined[:, 2 * width :], "col", split_axis=1, concat_axis=0, tiled=True),
    )
    image_rows = k_heads.shape[0]
    text_rows = text_keys.shape[0]
    shard_rows = image_rows + text_rows
    q_block = q_heads.reshape(image_rows, local_heads, head_size)
    key_rows = jnp.concatenate([k_heads, text_keys], 0)
    value_rows = jnp.concatenate([v_heads, text_values], 0)
    run_max = jnp.full((image_rows, local_heads), mask_floor, jnp.float32)
    key_piece = lax.all_gather(key_rows, "row", axis=0, tiled=True)
    value_piece = lax.all_gather(value_rows, "row", axis=0, tiled=True)
    piece_rows = key_piece.shape[0]
    global_row = jnp.arange(piece_rows, dtype=jnp.int32)
    shard_id = global_row // shard_rows
    within = global_row % shard_rows
    is_image = within < image_rows
    source_col = within // tile_w
    source_cell = within % tile_w
    image_req = shard_id % REQ
    text_req = (shard_id * text_rows + within - image_rows) // TXT
    key_req = jnp.where(is_image, image_req, text_req)
    key_onehot = key_req[:, None] == req_slots[None, :]
    key_height = jnp.sum(jnp.where(key_onehot, grid_size[:, 0][None, :], 0), 1)
    key_width = jnp.sum(jnp.where(key_onehot, grid_size[:, 1][None, :], 0), 1)
    image_ok = (shard_id // REQ < key_height) & (source_col * tile_w + source_cell < key_width)
    key_ok = (key_req == request) & (jnp.logical_not(is_image) | image_ok)
    scores = jnp.einsum(
        "qhd,khd->qhk",
        q_block,
        key_piece.reshape(piece_rows, local_heads, head_size),
        preferred_element_type=jnp.float32,
    ) * head_size ** (-0.5)
    new_max = jnp.maximum(run_max, jnp.max(jnp.where(key_ok, scores, mask_floor), -1))
    weights = jnp.where(key_ok, jnp.exp(scores - new_max[..., None]), 0.0)
    new_sum = jnp.sum(weights, -1)
    new_acc = jnp.einsum(
        "qhk,khd->qhd",
        weights.astype(jnp.bfloat16),
        value_piece.reshape(piece_rows, local_heads, head_size),
        preferred_element_type=jnp.float32,
    )
    mixed = (
        (new_acc / new_sum[..., None])
        .astype(jnp.bfloat16)
        .reshape(image_rows, local_heads * head_size)
    )
    partial_out = jnp.dot(
        mixed, lax.all_gather(w_out, "row", axis=1, tiled=True), preferred_element_type=jnp.float32
    )
    attended = lax.psum_scatter(
        partial_out.astype(jnp.bfloat16), "col", scatter_dimension=0, tiled=True
    ).astype(jnp.float32)
    first_res = (states + modulation[2] * attended).astype(jnp.bfloat16)
    normed_two = modulate(first_res.astype(jnp.float32), modulation[3], modulation[4])
    all_rows = lax.all_gather(normed_two, "row", axis=0, tiled=True)
    hidden = jax.nn.gelu(
        jnp.dot(all_rows, w_fc1, preferred_element_type=jnp.float32), approximate=True
    ).astype(jnp.bfloat16)
    every_term = jnp.dot(hidden, w_fc2, preferred_element_type=jnp.float32)
    every_sum = lax.psum(every_term, "row")
    mlp_out = lax.dynamic_slice_in_dim(every_sum, row_pos * tile_w, tile_w, 0)
    second_res = first_res.astype(jnp.float32) + modulation[5] * mlp_out
    normed_three = modulate(second_res, modulation[6], modulation[7])
    raw_velocity = jnp.dot(normed_three, w_final, preferred_element_type=jnp.float32)
    masked = jnp.where(token_ok[:, None], raw_velocity, 0.0)
    padded = with_halo(masked, (("col", 0),), 1)
    left_side = padded[:-2]
    right_side = padded[2:]
    velocity = jnp.where(
        token_ok[:, None], masked + blend * (left_side + right_side - 2.0 * masked), 0.0
    )
    next_latent = latent + -1.0 / STEPS * velocity
    return (velocity, next_latent)


bf16 = jnp.bfloat16
FC_PARTS = 3
f32 = jnp.float32
VMEM_SPEC = pl.BlockSpec(memory_space=pltpu.VMEM)
HBM_SPEC = pl.BlockSpec(memory_space=pltpu.HBM)


def start_copies(pairs, sems):
    copies = [pltpu.make_async_copy(source, target, sems.at[i]) for i, (source, target) in enumerate(pairs)]
    for copy in copies:
        copy.start()
    return copies


def part_rows(hbm, index):
    size = hbm.shape[0] // FC_PARTS
    return hbm.at[pl.ds(index * size, size), :]


def lane_mean(values):
    return jnp.mean(values, -1, keepdims=True)


def norm_rows(values):
    centred = values - lane_mean(values)
    return centred * lax.rsqrt(lane_mean(centred * centred) + eps_norm)


def per_request(mod_ref, step_ref, slot, rows_each, start, size):
    pieces = [
        jnp.broadcast_to(mod_ref[step_ref[q], pl.ds(slot, 1), pl.ds(start, size)], (rows_each, size))
        for q in range(REQ)
    ]
    row = lax.broadcasted_iota(jnp.int32, (REQ * rows_each, size), 0) // rows_each
    whole = jnp.concatenate([pieces[0]] * REQ, 0)
    for q in range(1, REQ):
        whole = jnp.where(row == q, jnp.concatenate([pieces[q]] * REQ, 0), whole)
    return whole


def qkv_kernel(
    step_hbm, size_hbm, offset_hbm, tokens_ref, mod_hbm, w_ref, fc2_hbm, text_k_hbm, text_v_hbm, q_gain_hbm, k_gain_hbm,
    out_ref, fc2_ref, text_ref, turn_ref, mask_ref, states_ref, gate_ref,
    step_ref, size_ref, offset_ref, q_gain_ref, k_gain_ref, order_ref, mod_ref, sems,
):
    row = lax.axis_index("row")
    depth = order_ref.shape[1]
    size = out_ref.shape[2]
    here = pl.ds(pl.multiple_of(lax.rem(row, 2) * size, size), size)
    copies = start_copies(
        [
            (step_hbm, step_ref),
            (size_hbm, size_ref),
            (offset_hbm, offset_ref),
            (q_gain_hbm, q_gain_ref),
            (k_gain_hbm, k_gain_ref),
            (mod_hbm, mod_ref),
            (text_k_hbm.at[:, here], text_ref.at[0]),
            (text_v_hbm.at[:, here], text_ref.at[1]),
            (part_rows(fc2_hbm, 0), fc2_ref),
        ],
        sems,
    )
    for q in range(REQ):
        for g in range(2):
            order_ref[4 * q + 2 * g : 4 * q + 2 * g + 2, :] = tokens_ref[REQ * g + q].astype(f32)
    out_ref[...] = jnp.zeros_like(out_ref)
    normed = norm_rows(order_ref[...])
    for copy in copies[:6]:
        copy.wait()
    shift = per_request(mod_ref, step_ref, 0, 4, 0, depth)
    scale = per_request(mod_ref, step_ref, 1, 4, 0, depth)
    normed = (normed * (1.0 + scale) + shift).astype(bf16)
    whole = jnp.dot(normed, w_ref[...], preferred_element_type=f32).astype(bf16)
    start = pl.multiple_of(row * size, size)
    states_ref[...] = order_ref[:, pl.ds(start, size)]
    gate_ref[...] = per_request(mod_ref, step_ref, 2, 4, start, size)
    turn_tables(row // 2, size_ref, offset_ref, q_gain_ref, k_gain_ref, turn_ref, mask_ref)
    for piece in range(w_ref.shape[1] // size):
        group = lax.rem(row * 3 + piece, 8)
        place = lax.rem(group, 2) * 4 + group // 2
        for q in range(REQ):
            out_ref[8 * q + place] = whole[4 * q : 4 * q + 4, piece * size : (piece + 1) * size]
    for copy in copies[6:]:
        copy.wait()


def swap_pairs(values):
    count = values.shape[-1]
    even = lax.rem(lax.broadcasted_iota(jnp.int32, values.shape, 1), 2) == 0
    return jnp.where(even, pltpu.roll(values, count - 1, 1), pltpu.roll(values, 1, 1))


def turn_tables(req, size_ref, offset_ref, q_gain_ref, k_gain_ref, turn_ref, mask_ref):
    _, count, head = turn_ref.shape
    token = lax.broadcasted_iota(jnp.int32, (count, 1), 0)
    pos_h = lax.rem(token, 4) // 2
    pos_w = (token // 4) * 2 + lax.rem(token, 2)
    lane = lax.broadcasted_iota(jnp.int32, (count, head), 1)
    pair = lane // 2
    time_half = head // 16
    axis_dim = (head - head // 8) // 2
    half = axis_dim // 2
    in_h = (pair >= time_half) & (pair < time_half + half)
    index = jnp.where(in_h, pair - time_half, pair - time_half - half).astype(f32)
    frequency = jnp.exp(index * f32(-2.0 * math.log(10000.0) / axis_dim))
    spot = jnp.where(in_h, pos_h + offset_ref[0, req], pos_w + offset_ref[1, req]).astype(f32)
    angle = jnp.where(pair < time_half, 0.0, spot * frequency)
    cosine = jnp.cos(angle)
    sine = jnp.sin(angle)
    sine = jnp.where(lax.rem(lane, 2) == 0, -sine, sine)
    for i, gain_ref in enumerate((q_gain_ref, k_gain_ref)):
        gain = jnp.broadcast_to(gain_ref[...], (count, head))
        turn_ref[2 * i] = gain * cosine
        turn_ref[2 * i + 1] = swap_pairs(gain) * sine
    key = lax.broadcasted_iota(jnp.int32, (count, count), 1)
    live = (lax.rem(key, 4) // 2 < size_ref[0, req]) & ((key // 4) * 2 + lax.rem(key, 2) < size_ref[1, req])
    mask_ref[...] = jnp.where(live, 1.0, 0.0)


def opening_kernel(states_hbm, k_hbm, v_hbm, spread_ref, given_ref, sems):
    size = given_ref.shape[2]
    start = (1 - lax.rem(lax.axis_index("row"), 2)) * size
    part = pl.ds(pl.multiple_of(start, size), size)
    states_copy, *text_copies = start_copies(
        [(states_hbm, spread_ref.at[0]), (k_hbm.at[:, part], given_ref.at[0]), (v_hbm.at[:, part], given_ref.at[1])], sems
    )
    states_copy.wait()
    states = spread_ref[0]
    for r in range(1, spread_ref.shape[0]):
        spread_ref[r] = states
    for copy in text_copies:
        copy.wait()


def attention_kernel(
    rows_ref, text_ref, other_ref, turn_ref, mask_ref, w_hbm, out_ref, w_ref, q_ref, k_ref, v_ref, sems
):
    (w_copy,) = start_copies([(w_hbm, w_ref)], sems)
    group = 2 * lax.axis_index("col") + lax.rem(lax.axis_index("row"), 2)
    count, width = q_ref.shape
    head = turn_ref.shape[2]
    for which, ref in enumerate((q_ref, k_ref, v_ref)):
        source = (8 * which + group) // 3
        for s in range(4):
            ref[4 * s : 4 * s + 4, :] = rows_ref[source, s].astype(f32)

    def turned(values, which):
        values = values * lax.rsqrt(lane_mean(values * values) + eps_norm)
        return (values * turn_ref[2 * which] + swap_pairs(values) * turn_ref[2 * which + 1]).astype(bf16)

    key_ok = mask_ref[...] > 0.0
    contract = (((1,), (1,)), ((), ()))
    scale = head ** (-0.5)
    for h in range(width // head):
        cols = slice(h * head, (h + 1) * head)
        q = turned(q_ref[:, cols], 0)
        k = turned(k_ref[:, cols], 1)
        v = v_ref[:, cols].astype(bf16)
        s_own = lax.dot_general(q, text_ref[0, :, cols], contract, preferred_element_type=f32) * scale
        s_other = lax.dot_general(q, other_ref[0, :, cols], contract, preferred_element_type=f32) * scale
        s_image = lax.dot_general(q, k, contract, preferred_element_type=f32) * scale
        s_image = jnp.where(key_ok, s_image, mask_floor)
        top = jnp.maximum(
            jnp.max(jnp.maximum(s_own, s_other), -1, keepdims=True), jnp.max(s_image, -1, keepdims=True)
        )
        w_own = jnp.exp(s_own - top)
        w_other = jnp.exp(s_other - top)
        w_image = jnp.where(key_ok, jnp.exp(s_image - top), 0.0)
        total = jnp.sum(w_own + w_other, -1, keepdims=True) + jnp.sum(w_image, -1, keepdims=True)
        summed = (
            jnp.dot(w_own.astype(bf16), text_ref[1, :, cols], preferred_element_type=f32)
            + jnp.dot(w_other.astype(bf16), other_ref[1, :, cols], preferred_element_type=f32)
            + jnp.dot(w_image.astype(bf16), v, preferred_element_type=f32)
        )
        mixed = (summed / total).astype(bf16)
        for s in range(4):
            for r in range(8):
                out_ref[4 * r + s, :, cols] = mixed[4 * s : 4 * s + 4, :]
    w_copy.wait()


def out_kernel(mixed_ref, states_ref, gate_ref, w0_ref, w1_ref, w2_ref, w3_ref, out_ref, rows_ref):
    col = lax.axis_index("col")
    depth = w0_ref.shape[0]
    piece = mixed_ref.shape[2]
    for r in range(8):
        for s in range(4):
            at = (2 * s + r % 2) * piece
            rows_ref[4 * (r // 2) : 4 * (r // 2) + 4, at : at + piece] = mixed_ref[4 * r + s].astype(f32)
    attended = 0.0
    for d, w_ref in enumerate((w0_ref, w1_ref, w2_ref, w3_ref)):
        at = pl.multiple_of(jnp.bitwise_xor(col, d) * depth, depth)
        share = rows_ref[:, pl.ds(at, depth)].astype(bf16)
        attended = attended + jnp.dot(share, w_ref[...], preferred_element_type=f32)
    first = (states_ref[...] + gate_ref[...] * attended).astype(bf16)
    for r in range(8):
        out_ref[r] = first


def mlp_kernel(
    step_hbm, size_hbm, first_ref, mod_hbm, w1_ref, w2a_ref, w2_hbm, final_hbm, out_ref, own_ref, final_ref, last_ref,
    live_ref, step_ref, size_ref, rows_ref, mod_ref, w2b_ref, w2c_ref, sems,
):
    row = lax.axis_index("row")
    depth = rows_ref.shape[1]
    piece = first_ref.shape[2]
    step_copy, size_copy, mod_copy, *w_copies = start_copies(
        [
            (step_hbm, step_ref),
            (size_hbm, size_ref),
            (mod_hbm, mod_ref),
            (part_rows(w2_hbm, 1), w2b_ref),
            (part_rows(w2_hbm, 2), w2c_ref),
            (final_hbm, final_ref),
        ],
        sems,
    )
    for r in range(8):
        rows_ref[:, r * piece : (r + 1) * piece] = first_ref[r].astype(f32)
    normed = norm_rows(rows_ref[...])
    step_copy.wait()
    size_copy.wait()
    mod_copy.wait()
    shift = per_request(mod_ref, step_ref, 3, 4, 0, depth)
    scale = per_request(mod_ref, step_ref, 4, 4, 0, depth)
    normed = (normed * (1.0 + scale) + shift).astype(bf16)
    own = rows_ref[0:2, :]
    for q in range(REQ):
        for g in range(2):
            own = jnp.where(row == REQ * g + q, rows_ref[4 * q + 2 * g : 4 * q + 2 * g + 2, :], own)
    own_ref[...] = own
    req = lax.rem(row, REQ)
    last_ref[...] = mod_ref[step_ref[req], 6:8, :]
    grid_col = lax.axis_index("col") * live_ref.shape[0] + lax.broadcasted_iota(jnp.int32, live_ref.shape, 0)
    live = (row // REQ < size_ref[0, req]) & (grid_col < size_ref[1, req])
    live_ref[...] = jnp.where(live, 1.0, 0.0)
    hidden = jax.nn.gelu(
        jnp.dot(normed, w1_ref[...], preferred_element_type=f32), approximate=True
    ).astype(bf16)
    size = w2a_ref.shape[0]
    added = 0.0
    for i, w_ref in enumerate((w2a_ref, w2b_ref, w2c_ref)):
        if i > 0:
            w_copies[i - 1].wait()
        added = added + jnp.dot(hidden[:, i * size : (i + 1) * size], w_ref[...], preferred_element_type=f32)
    gate = per_request(mod_ref, step_ref, 5, 4, 0, depth)
    term = (gate * added).astype(out_ref.dtype)
    for q in range(REQ):
        for g in range(2):
            out_ref[REQ * g + q] = term[4 * q + 2 * g : 4 * q + 2 * g + 2, :]
    w_copies[2].wait()


def final_kernel(terms_ref, first_ref, last_ref, w_ref, live_ref, out_ref):
    second = first_ref[...]
    for r in range(8):
        second = second + terms_ref[r].astype(f32)
    normed = (norm_rows(second) * (1.0 + last_ref[1:2, :]) + last_ref[0:1, :]).astype(bf16)
    raw = lax.dot_general(normed, w_ref[...], (((1,), (1,)), ((), ())), preferred_element_type=f32)
    out_ref[...] = jnp.where(live_ref[...] > 0.0, raw, 0.0)


def blend_kernel(masked_ref, live_ref, near_ref, far_ref, latent_ref, velocity_ref, next_ref):
    col = lax.axis_index("col")
    masked = masked_ref[...]
    near = near_ref[...]
    far = jnp.where((col == 1) | (col == 2), far_ref[...], 0.0)
    odd = lax.rem(col, 2) == 1
    count = masked.shape[0]
    left = jnp.concatenate([jnp.where(odd, near, far)[count - 1 :, :], masked[: count - 1, :]], 0)
    right = jnp.concatenate([masked[1:, :], jnp.where(odd, far, near)[:1, :]], 0)
    velocity = jnp.where(live_ref[...] > 0.0, masked + blend * (left + right - 2.0 * masked), 0.0)
    velocity_ref[...] = velocity
    next_ref[...] = latent_ref[...] + -1.0 / STEPS * velocity


def call(kernel, outs, specs, scratch=(), limit=8 << 20):
    return pl.pallas_call(
        kernel,
        out_shape=tuple(jax.ShapeDtypeStruct(shape, dtype) for shape, dtype in outs),
        in_specs=specs,
        out_specs=(VMEM_SPEC,) * len(outs),
        scratch_shapes=list(scratch),
        compiler_params=pltpu.CompilerParams(vmem_limit_bytes=limit),
    )


def exchange(values, axes):
    return lax.all_to_all(values, axes, split_axis=0, concat_axis=0, tiled=True)


def compact_on_device(
    image_states, latent, text_keys, text_values, mod_table, timestep, grid_size, rope_offset,
    w_qkv, q_gain, k_gain, w_out, w_fc1, w_fc2, w_final,
):
    rows = lax.axis_size("row")
    cols = lax.axis_size("col")
    stay = lambda values: pltpu.with_memory_space_constraint(values, pltpu.HBM)
    tile_w, width = image_states.shape
    head = q_gain.shape[0]
    piece = width // 8
    tokens = rows * tile_w
    both = ("row", "col")

    near = [(i, i ^ 1) for i in range(cols)]
    steps = stay(timestep)
    sizes = stay(grid_size.T)
    mods = stay(mod_table)
    fc2 = stay(w_fc2)
    sems = lambda count: pltpu.SemaphoreType.DMA((count,))
    mod_space = pltpu.VMEM(mod_table.shape, f32)
    steps_space = pltpu.SMEM(timestep.shape, jnp.int32)
    sizes_space = pltpu.SMEM(grid_size.shape[::-1], jnp.int32)
    gain_space = pltpu.VMEM((1, head), f32)
    fc2_part = ((w_fc2.shape[0] // FC_PARTS, width), bf16)

    spread, given = call(
        opening_kernel,
        [((rows, tile_w, width), bf16), ((2, text_keys.shape[0], piece), bf16)],
        [HBM_SPEC] * 3,
        [sems(3)],
    )(stay(image_states), stay(text_keys), stay(text_values))
    other = lax.ppermute(given, "row", [(i, i ^ 1) for i in range(rows)])
    w_x = lax.ppermute(w_out, "col", [(i, i ^ 2) for i in range(cols)])
    w_k = lax.ppermute(w_out, "col", near)
    gathered = exchange(spread, "row")
    half_rows = text_keys.shape[0]
    pieces, fc2_a, text, turn, mask, states, gate = call(
        qkv_kernel,
        [
            ((rows * cols, 4, piece), bf16),
            fc2_part,
            ((2, half_rows, piece), bf16),
            ((4, tokens, head), f32),
            ((tokens, tokens), f32),
            ((tokens, piece), f32),
            ((tokens, piece), f32),
        ],
        [HBM_SPEC] * 3 + [VMEM_SPEC, HBM_SPEC, VMEM_SPEC] + [HBM_SPEC] * 5,
        [
            steps_space,
            sizes_space,
            sizes_space,
            gain_space,
            gain_space,
            pltpu.VMEM((tokens, width), f32),
            mod_space,
            sems(9),
        ],
    )(
        steps, sizes, stay(rope_offset.T), gathered, mods, lax.ppermute(w_qkv, "col", near), fc2, stay(text_keys),
        stay(text_values), stay(q_gain.reshape(1, head)), stay(k_gain.reshape(1, head)),
    )
    pieces, other, w_k = lax.optimization_barrier((pieces, other, w_k))
    got = exchange(pieces, both).reshape(rows, cols, 4, piece)
    mixed, w_own = call(
        attention_kernel,
        [((rows * cols, 4, piece), bf16), (w_out.shape, bf16)],
        [VMEM_SPEC] * 5 + [HBM_SPEC],
        [pltpu.VMEM((tokens, piece), f32)] * 3 + [sems(1)],
    )(got, text, other, turn, mask, stay(w_out))
    mixed, w_x = lax.optimization_barrier((mixed, w_x))
    w_xk = lax.ppermute(w_x, "col", near)
    all_mixed = exchange(mixed, both)
    (first,) = call(
        out_kernel, [((rows, tokens, piece), bf16)], [VMEM_SPEC] * 7, [pltpu.VMEM((tokens, width), f32)]
    )(all_mixed, states, gate, w_own, w_k, w_x, w_xk)
    all_first = exchange(first, "row")
    terms, first_own, final_here, last, live = call(
        mlp_kernel,
        [
            ((rows, tile_w, width), bf16),
            ((tile_w, width), f32),
            (w_final.shape[::-1], bf16),
            ((2, width), f32),
            (latent.shape, f32),
        ],
        [HBM_SPEC, HBM_SPEC, VMEM_SPEC, HBM_SPEC, VMEM_SPEC, VMEM_SPEC, HBM_SPEC, HBM_SPEC],
        [steps_space, sizes_space, pltpu.VMEM((tokens, width), f32), mod_space]
        + [pltpu.VMEM(*fc2_part)] * 2
        + [sems(6)],
        limit=16 << 20,
    )(steps, sizes, all_first, mods, w_fc1, fc2_a, fc2, stay(w_final.T))
    all_terms = exchange(terms, "row")
    (masked,) = call(final_kernel, [(latent.shape, f32)], [VMEM_SPEC] * 5)(all_terms, first_own, last, final_here, live)
    beside = lax.ppermute(masked, "col", near)
    across = lax.ppermute(masked, "col", [(i, i ^ 3) for i in range(cols)])
    return call(blend_kernel, [(latent.shape, f32)] * 2, [VMEM_SPEC] * 5)(masked, live, beside, across, latent)


def solution(mesh):
    placed = (
        P(("row", "col"), None),
        P(("row", "col"), None),
        P("row", "col"),
        P("row", "col"),
        P(),
        P(),
        P(),
        P(),
        P(None, "row"),
        P(),
        P(),
        P("col", "row"),
        P(None, "row"),
        P("row", None),
        P(),
    )
    compact = mesh.shape["row"] == 2 * REQ and mesh.shape["col"] == 4
    return jax.shard_map(
        compact_on_device if compact else on_device,
        mesh=mesh,
        in_specs=placed,
        out_specs=(P(("row", "col"), None), P(("row", "col"), None)),
        check_vma=False,
    )
```

```python
import math

import jax
import jax.numpy as jnp
from jax import lax
from jax.experimental import pallas as pl
from jax.experimental.pallas import tpu as pltpu
from jax.sharding import PartitionSpec as P

REQ = 4
TXT = 256
STEPS = 4


eps_norm = 1e-06
blend = 0.25
mask_floor = -1e30


def with_halo(cells, sides, width):
    for axis, dim in sides:
        count = lax.axis_size(axis)
        ends = count - 1
        head = lax.slice_in_dim(cells, 0, width, axis=dim)
        tail = lax.slice_in_dim(cells, cells.shape[dim] - width, cells.shape[dim], axis=dim)
        cells = jnp.concatenate(
            [
                lax.ppermute(tail, axis, [(i, (i + 1) % count) for i in range(ends)]),
                cells,
                lax.ppermute(head, axis, [((i + 1) % count, i) for i in range(ends)]),
            ],
            axis=dim,
        )
    return cells


def layer_norm(values):
    mean_value = jnp.mean(values, -1, keepdims=True)
    centred = values - mean_value
    return centred * lax.rsqrt(jnp.mean(centred * centred, -1, keepdims=True) + eps_norm)


def modulate(values, shift_vec, scale_vec):
    return (layer_norm(values) * (1.0 + scale_vec) + shift_vec).astype(jnp.bfloat16)


def rope_tables(pos_h, pos_w, head_size):
    time_half = head_size // 16
    axis_dim = (head_size - head_size // 8) // 2
    freq_index = jnp.arange(axis_dim // 2, dtype=jnp.float32)
    frequency = 10000.0 ** (-2.0 * freq_index / axis_dim)
    angles = jnp.concatenate(
        [
            jnp.zeros((pos_h.shape[0], time_half), jnp.float32),
            pos_h[:, None] * frequency[None, :],
            pos_w[:, None] * frequency[None, :],
        ],
        1,
    )
    return (jnp.cos(angles), jnp.sin(angles))


def norm_rope(values, gain_vec, cosine_table, sine_table, head_count, head_size):
    row_total = values.shape[0]
    per_head = values.astype(jnp.float32).reshape(row_total, head_count, head_size)
    per_head = (
        per_head * lax.rsqrt(jnp.mean(per_head * per_head, -1, keepdims=True) + eps_norm) * gain_vec
    )
    paired = per_head.reshape(row_total, head_count, head_size // 2, 2)
    even_part = paired[..., 0]
    odd_part = paired[..., 1]
    cos_wide = cosine_table[:, None, :]
    sin_wide = sine_table[:, None, :]
    turned = jnp.stack(
        [even_part * cos_wide - odd_part * sin_wide, even_part * sin_wide + odd_part * cos_wide], -1
    )
    return turned.reshape(row_total, head_count * head_size).astype(jnp.bfloat16)


def on_device(
    image_states,
    latent,
    text_keys,
    text_values,
    mod_table,
    timestep,
    grid_size,
    rope_offset,
    w_qkv,
    q_gain,
    k_gain,
    w_out,
    w_fc1,
    w_fc2,
    w_final,
):
    col_total = lax.axis_size("col")
    row_pos = lax.axis_index("row")
    col_pos = lax.axis_index("col")
    tile_w = image_states.shape[0]
    width = image_states.shape[1]
    head_size = q_gain.shape[0]
    head_count = width // head_size
    local_heads = head_count // col_total
    request = row_pos % REQ
    grid_row = row_pos // REQ
    grid_col = col_pos * tile_w + jnp.arange(tile_w, dtype=jnp.int32)
    req_slots = jnp.arange(REQ, dtype=jnp.int32)
    req_onehot = req_slots == request
    limits = jnp.sum(jnp.where(req_onehot[:, None], grid_size, 0), 0)
    offsets = jnp.sum(jnp.where(req_onehot[:, None], rope_offset, 0), 0)
    step_now = jnp.sum(jnp.where(req_onehot, timestep, 0))
    token_ok = (grid_row < limits[0]) & (grid_col < limits[1])
    modulation = lax.dynamic_index_in_dim(mod_table, step_now, 0, keepdims=False)
    states = image_states.astype(jnp.float32)
    normed = modulate(states, modulation[0], modulation[1])
    joined_cols = jnp.dot(
        lax.all_gather(normed, "row", axis=0, tiled=True), w_qkv, preferred_element_type=jnp.float32
    ).astype(jnp.bfloat16)
    joined = lax.all_to_all(joined_cols, "row", split_axis=0, concat_axis=1, tiled=True)
    pos_h = jnp.zeros((tile_w,), jnp.float32) + (grid_row + offsets[0]).astype(jnp.float32)
    pos_w = (grid_col + offsets[1]).astype(jnp.float32)
    cosine_table, sine_table = rope_tables(pos_h, pos_w, head_size)
    queries = norm_rope(joined[:, :width], q_gain, cosine_table, sine_table, head_count, head_size)
    image_keys = norm_rope(
        joined[:, width : 2 * width], k_gain, cosine_table, sine_table, head_count, head_size
    )
    q_heads, k_heads, v_heads = (
        lax.all_to_all(queries, "col", split_axis=1, concat_axis=0, tiled=True),
        lax.all_to_all(image_keys, "col", split_axis=1, concat_axis=0, tiled=True),
        lax.all_to_all(joined[:, 2 * width :], "col", split_axis=1, concat_axis=0, tiled=True),
    )
    image_rows = k_heads.shape[0]
    text_rows = text_keys.shape[0]
    shard_rows = image_rows + text_rows
    q_block = q_heads.reshape(image_rows, local_heads, head_size)
    key_rows = jnp.concatenate([k_heads, text_keys], 0)
    value_rows = jnp.concatenate([v_heads, text_values], 0)
    run_max = jnp.full((image_rows, local_heads), mask_floor, jnp.float32)
    key_piece = lax.all_gather(key_rows, "row", axis=0, tiled=True)
    value_piece = lax.all_gather(value_rows, "row", axis=0, tiled=True)
    piece_rows = key_piece.shape[0]
    global_row = jnp.arange(piece_rows, dtype=jnp.int32)
    shard_id = global_row // shard_rows
    within = global_row % shard_rows
    is_image = within < image_rows
    source_col = within // tile_w
    source_cell = within % tile_w
    image_req = shard_id % REQ
    text_req = (shard_id * text_rows + within - image_rows) // TXT
    key_req = jnp.where(is_image, image_req, text_req)
    key_onehot = key_req[:, None] == req_slots[None, :]
    key_height = jnp.sum(jnp.where(key_onehot, grid_size[:, 0][None, :], 0), 1)
    key_width = jnp.sum(jnp.where(key_onehot, grid_size[:, 1][None, :], 0), 1)
    image_ok = (shard_id // REQ < key_height) & (source_col * tile_w + source_cell < key_width)
    key_ok = (key_req == request) & (jnp.logical_not(is_image) | image_ok)
    scores = jnp.einsum(
        "qhd,khd->qhk",
        q_block,
        key_piece.reshape(piece_rows, local_heads, head_size),
        preferred_element_type=jnp.float32,
    ) * head_size ** (-0.5)
    new_max = jnp.maximum(run_max, jnp.max(jnp.where(key_ok, scores, mask_floor), -1))
    weights = jnp.where(key_ok, jnp.exp(scores - new_max[..., None]), 0.0)
    new_sum = jnp.sum(weights, -1)
    new_acc = jnp.einsum(
        "qhk,khd->qhd",
        weights.astype(jnp.bfloat16),
        value_piece.reshape(piece_rows, local_heads, head_size),
        preferred_element_type=jnp.float32,
    )
    mixed = (
        (new_acc / new_sum[..., None])
        .astype(jnp.bfloat16)
        .reshape(image_rows, local_heads * head_size)
    )
    partial_out = jnp.dot(
        mixed, lax.all_gather(w_out, "row", axis=1, tiled=True), preferred_element_type=jnp.float32
    )
    attended = lax.psum_scatter(
        partial_out.astype(jnp.bfloat16), "col", scatter_dimension=0, tiled=True
    ).astype(jnp.float32)
    first_res = (states + modulation[2] * attended).astype(jnp.bfloat16)
    normed_two = modulate(first_res.astype(jnp.float32), modulation[3], modulation[4])
    all_rows = lax.all_gather(normed_two, "row", axis=0, tiled=True)
    hidden = jax.nn.gelu(
        jnp.dot(all_rows, w_fc1, preferred_element_type=jnp.float32), approximate=True
    ).astype(jnp.bfloat16)
    every_term = jnp.dot(hidden, w_fc2, preferred_element_type=jnp.float32)
    every_sum = lax.psum(every_term, "row")
    mlp_out = lax.dynamic_slice_in_dim(every_sum, row_pos * tile_w, tile_w, 0)
    second_res = first_res.astype(jnp.float32) + modulation[5] * mlp_out
    normed_three = modulate(second_res, modulation[6], modulation[7])
    raw_velocity = jnp.dot(normed_three, w_final, preferred_element_type=jnp.float32)
    masked = jnp.where(token_ok[:, None], raw_velocity, 0.0)
    padded = with_halo(masked, (("col", 0),), 1)
    left_side = padded[:-2]
    right_side = padded[2:]
    velocity = jnp.where(
        token_ok[:, None], masked + blend * (left_side + right_side - 2.0 * masked), 0.0
    )
    next_latent = latent + -1.0 / STEPS * velocity
    return (velocity, next_latent)


bf16 = jnp.bfloat16
FC_PARTS = 3
f32 = jnp.float32
VMEM_SPEC = pl.BlockSpec(memory_space=pltpu.VMEM)
HBM_SPEC = pl.BlockSpec(memory_space=pltpu.HBM)


def start_copies(pairs, sems):
    copies = [pltpu.make_async_copy(source, target, sems.at[i]) for i, (source, target) in enumerate(pairs)]
    for copy in copies:
        copy.start()
    return copies


def part_rows(hbm, index):
    size = hbm.shape[0] // FC_PARTS
    return hbm.at[pl.ds(index * size, size), :]


def lane_mean(values):
    return jnp.mean(values, -1, keepdims=True)


def norm_rows(values):
    centred = values - lane_mean(values)
    return centred * lax.rsqrt(lane_mean(centred * centred) + eps_norm)


def per_request(mod_ref, step_ref, slot, rows_each, start, size):
    pieces = [
        jnp.broadcast_to(mod_ref[step_ref[q], pl.ds(slot, 1), pl.ds(start, size)], (rows_each, size))
        for q in range(REQ)
    ]
    row = lax.broadcasted_iota(jnp.int32, (REQ * rows_each, size), 0) // rows_each
    whole = jnp.concatenate([pieces[0]] * REQ, 0)
    for q in range(1, REQ):
        whole = jnp.where(row == q, jnp.concatenate([pieces[q]] * REQ, 0), whole)
    return whole


def qkv_kernel(
    step_hbm, tokens_ref, mod_ref, w_ref, fc2_hbm, text_k_hbm, text_v_hbm, out_ref, fc2_ref, text_ref, states_ref, gate_ref,
    step_ref, order_ref, sems,
):
    row = lax.axis_index("row")
    depth = order_ref.shape[1]
    size = out_ref.shape[2]
    here = pl.ds(pl.multiple_of(lax.rem(row, 2) * size, size), size)
    copies = start_copies(
        [
            (step_hbm, step_ref),
            (text_k_hbm.at[:, here], text_ref.at[0]),
            (text_v_hbm.at[:, here], text_ref.at[1]),
            (part_rows(fc2_hbm, 0), fc2_ref),
        ],
        sems,
    )
    for q in range(REQ):
        for g in range(2):
            order_ref[4 * q + 2 * g : 4 * q + 2 * g + 2, :] = tokens_ref[REQ * g + q].astype(f32)
    out_ref[...] = jnp.zeros_like(out_ref)
    normed = norm_rows(order_ref[...])
    for copy in copies[:1]:
        copy.wait()
    shift = per_request(mod_ref, step_ref, 0, 4, 0, depth)
    scale = per_request(mod_ref, step_ref, 1, 4, 0, depth)
    normed = (normed * (1.0 + scale) + shift).astype(bf16)
    whole = jnp.dot(normed, w_ref[...], preferred_element_type=f32).astype(bf16)
    start = pl.multiple_of(row * size, size)
    states_ref[...] = order_ref[:, pl.ds(start, size)]
    gate_ref[...] = per_request(mod_ref, step_ref, 2, 4, start, size)
    for piece in range(w_ref.shape[1] // size):
        group = lax.rem(row * 3 + piece, 8)
        place = lax.rem(group, 2) * 4 + group // 2
        for q in range(REQ):
            out_ref[8 * q + place] = whole[4 * q : 4 * q + 4, piece * size : (piece + 1) * size]
    for copy in copies[1:]:
        copy.wait()


def swap_pairs(values):
    count = values.shape[-1]
    even = lax.rem(lax.broadcasted_iota(jnp.int32, values.shape, 1), 2) == 0
    return jnp.where(even, pltpu.roll(values, count - 1, 1), pltpu.roll(values, 1, 1))


def turn_tables(req, size_ref, offset_ref, q_gain_ref, k_gain_ref, turn_ref, mask_ref):
    _, count, head = turn_ref.shape
    token = lax.broadcasted_iota(jnp.int32, (count, 1), 0)
    pos_h = lax.rem(token, 4) // 2
    pos_w = (token // 4) * 2 + lax.rem(token, 2)
    lane = lax.broadcasted_iota(jnp.int32, (count, head), 1)
    pair = lane // 2
    time_half = head // 16
    axis_dim = (head - head // 8) // 2
    half = axis_dim // 2
    in_h = (pair >= time_half) & (pair < time_half + half)
    index = jnp.where(in_h, pair - time_half, pair - time_half - half).astype(f32)
    frequency = jnp.exp(index * f32(-2.0 * math.log(10000.0) / axis_dim))
    spot = jnp.where(in_h, pos_h + offset_ref[0, req], pos_w + offset_ref[1, req]).astype(f32)
    angle = jnp.where(pair < time_half, 0.0, spot * frequency)
    cosine = jnp.cos(angle)
    sine = jnp.sin(angle)
    sine = jnp.where(lax.rem(lane, 2) == 0, -sine, sine)
    for i, gain_ref in enumerate((q_gain_ref, k_gain_ref)):
        gain = jnp.broadcast_to(gain_ref[...], (count, head))
        turn_ref[2 * i] = gain * cosine
        turn_ref[2 * i + 1] = swap_pairs(gain) * sine
    key = lax.broadcasted_iota(jnp.int32, (count, count), 1)
    live = (lax.rem(key, 4) // 2 < size_ref[0, req]) & ((key // 4) * 2 + lax.rem(key, 2) < size_ref[1, req])
    mask_ref[...] = jnp.where(live, 1.0, 0.0)


def opening_kernel(
    states_hbm, k_hbm, v_hbm, mod_hbm, size_hbm, offset_hbm, q_gain_hbm, k_gain_hbm,
    spread_ref, given_ref, mod_ref, turn_ref, mask_ref, size_ref, offset_ref, q_gain_ref, k_gain_ref, sems,
):
    size = given_ref.shape[2]
    start = (1 - lax.rem(lax.axis_index("row"), 2)) * size
    part = pl.ds(pl.multiple_of(start, size), size)
    states_copy, *text_copies = start_copies(
        [
            (states_hbm, spread_ref.at[0]),
            (k_hbm.at[:, part], given_ref.at[0]),
            (v_hbm.at[:, part], given_ref.at[1]),
            (mod_hbm, mod_ref),
            (size_hbm, size_ref),
            (offset_hbm, offset_ref),
            (q_gain_hbm, q_gain_ref),
            (k_gain_hbm, k_gain_ref),
        ],
        sems,
    )
    states_copy.wait()
    states = spread_ref[0]
    for r in range(1, spread_ref.shape[0]):
        spread_ref[r] = states
    for copy in text_copies:
        copy.wait()
    turn_tables(lax.axis_index("row") // 2, size_ref, offset_ref, q_gain_ref, k_gain_ref, turn_ref, mask_ref)


def attention_kernel(
    rows_ref, text_ref, other_ref, turn_ref, mask_ref, w_hbm, out_ref, w_ref, q_ref, k_ref, v_ref, sems
):
    (w_copy,) = start_copies([(w_hbm, w_ref)], sems)
    group = 2 * lax.axis_index("col") + lax.rem(lax.axis_index("row"), 2)
    count, width = q_ref.shape
    head = turn_ref.shape[2]
    for which, ref in enumerate((q_ref, k_ref, v_ref)):
        source = (8 * which + group) // 3
        for s in range(4):
            ref[4 * s : 4 * s + 4, :] = rows_ref[source, s].astype(f32)

    def turned(values, which):
        values = values * lax.rsqrt(lane_mean(values * values) + eps_norm)
        return (values * turn_ref[2 * which] + swap_pairs(values) * turn_ref[2 * which + 1]).astype(bf16)

    key_ok = mask_ref[...] > 0.0
    contract = (((1,), (1,)), ((), ()))
    scale = head ** (-0.5)
    for h in range(width // head):
        cols = slice(h * head, (h + 1) * head)
        q = turned(q_ref[:, cols], 0)
        k = turned(k_ref[:, cols], 1)
        v = v_ref[:, cols].astype(bf16)
        s_own = lax.dot_general(q, text_ref[0, :, cols], contract, preferred_element_type=f32) * scale
        s_other = lax.dot_general(q, other_ref[0, :, cols], contract, preferred_element_type=f32) * scale
        s_image = lax.dot_general(q, k, contract, preferred_element_type=f32) * scale
        s_image = jnp.where(key_ok, s_image, mask_floor)
        top = jnp.maximum(
            jnp.max(jnp.maximum(s_own, s_other), -1, keepdims=True), jnp.max(s_image, -1, keepdims=True)
        )
        w_own = jnp.exp(s_own - top)
        w_other = jnp.exp(s_other - top)
        w_image = jnp.where(key_ok, jnp.exp(s_image - top), 0.0)
        total = jnp.sum(w_own + w_other, -1, keepdims=True) + jnp.sum(w_image, -1, keepdims=True)
        summed = (
            jnp.dot(w_own.astype(bf16), text_ref[1, :, cols], preferred_element_type=f32)
            + jnp.dot(w_other.astype(bf16), other_ref[1, :, cols], preferred_element_type=f32)
            + jnp.dot(w_image.astype(bf16), v, preferred_element_type=f32)
        )
        mixed = (summed / total).astype(bf16)
        for s in range(4):
            for r in range(8):
                out_ref[4 * r + s, :, cols] = mixed[4 * s : 4 * s + 4, :]
    w_copy.wait()


def out_kernel(mixed_ref, states_ref, gate_ref, w0_ref, w1_ref, w2_ref, w3_ref, out_ref, rows_ref):
    col = lax.axis_index("col")
    depth = w0_ref.shape[0]
    piece = mixed_ref.shape[2]
    for r in range(8):
        for s in range(4):
            at = (2 * s + r % 2) * piece
            rows_ref[4 * (r // 2) : 4 * (r // 2) + 4, at : at + piece] = mixed_ref[4 * r + s].astype(f32)
    attended = 0.0
    for d, w_ref in enumerate((w0_ref, w1_ref, w2_ref, w3_ref)):
        at = pl.multiple_of(jnp.bitwise_xor(col, d) * depth, depth)
        share = rows_ref[:, pl.ds(at, depth)].astype(bf16)
        attended = attended + jnp.dot(share, w_ref[...], preferred_element_type=f32)
    first = (states_ref[...] + gate_ref[...] * attended).astype(bf16)
    for r in range(8):
        out_ref[r] = first


def mlp_kernel(
    step_hbm, size_hbm, first_ref, mod_ref, w1_ref, w2a_ref, w2_hbm, final_hbm, out_ref, own_ref, final_ref, last_ref,
    live_ref, step_ref, size_ref, rows_ref, w2b_ref, w2c_ref, sems,
):
    row = lax.axis_index("row")
    depth = rows_ref.shape[1]
    piece = first_ref.shape[2]
    step_copy, size_copy, *w_copies = start_copies(
        [
            (step_hbm, step_ref),
            (size_hbm, size_ref),
            (part_rows(w2_hbm, 1), w2b_ref),
            (part_rows(w2_hbm, 2), w2c_ref),
            (final_hbm, final_ref),
        ],
        sems,
    )
    for r in range(8):
        rows_ref[:, r * piece : (r + 1) * piece] = first_ref[r].astype(f32)
    normed = norm_rows(rows_ref[...])
    step_copy.wait()
    size_copy.wait()
    shift = per_request(mod_ref, step_ref, 3, 4, 0, depth)
    scale = per_request(mod_ref, step_ref, 4, 4, 0, depth)
    normed = (normed * (1.0 + scale) + shift).astype(bf16)
    own = rows_ref[0:2, :]
    for q in range(REQ):
        for g in range(2):
            own = jnp.where(row == REQ * g + q, rows_ref[4 * q + 2 * g : 4 * q + 2 * g + 2, :], own)
    own_ref[...] = own
    req = lax.rem(row, REQ)
    last_ref[...] = mod_ref[step_ref[req], 6:8, :]
    grid_col = lax.axis_index("col") * live_ref.shape[0] + lax.broadcasted_iota(jnp.int32, live_ref.shape, 0)
    live = (row // REQ < size_ref[0, req]) & (grid_col < size_ref[1, req])
    live_ref[...] = jnp.where(live, 1.0, 0.0)
    hidden = jax.nn.gelu(
        jnp.dot(normed, w1_ref[...], preferred_element_type=f32), approximate=True
    ).astype(bf16)
    size = w2a_ref.shape[0]
    added = 0.0
    for i, w_ref in enumerate((w2a_ref, w2b_ref, w2c_ref)):
        if i > 0:
            w_copies[i - 1].wait()
        added = added + jnp.dot(hidden[:, i * size : (i + 1) * size], w_ref[...], preferred_element_type=f32)
    gate = per_request(mod_ref, step_ref, 5, 4, 0, depth)
    term = (gate * added).astype(out_ref.dtype)
    for q in range(REQ):
        for g in range(2):
            out_ref[REQ * g + q] = term[4 * q + 2 * g : 4 * q + 2 * g + 2, :]
    w_copies[2].wait()


def final_kernel(terms_ref, first_ref, last_ref, w_ref, live_ref, out_ref):
    second = first_ref[...]
    for r in range(8):
        second = second + terms_ref[r].astype(f32)
    normed = (norm_rows(second) * (1.0 + last_ref[1:2, :]) + last_ref[0:1, :]).astype(bf16)
    raw = lax.dot_general(normed, w_ref[...], (((1,), (1,)), ((), ())), preferred_element_type=f32)
    out_ref[...] = jnp.where(live_ref[...] > 0.0, raw, 0.0)


def blend_kernel(masked_ref, live_ref, near_ref, far_ref, latent_ref, velocity_ref, next_ref):
    col = lax.axis_index("col")
    masked = masked_ref[...]
    near = near_ref[...]
    far = jnp.where((col == 1) | (col == 2), far_ref[...], 0.0)
    odd = lax.rem(col, 2) == 1
    count = masked.shape[0]
    left = jnp.concatenate([jnp.where(odd, near, far)[count - 1 :, :], masked[: count - 1, :]], 0)
    right = jnp.concatenate([masked[1:, :], jnp.where(odd, far, near)[:1, :]], 0)
    velocity = jnp.where(live_ref[...] > 0.0, masked + blend * (left + right - 2.0 * masked), 0.0)
    velocity_ref[...] = velocity
    next_ref[...] = latent_ref[...] + -1.0 / STEPS * velocity


def call(kernel, outs, specs, scratch=(), limit=8 << 20):
    return pl.pallas_call(
        kernel,
        out_shape=tuple(jax.ShapeDtypeStruct(shape, dtype) for shape, dtype in outs),
        in_specs=specs,
        out_specs=(VMEM_SPEC,) * len(outs),
        scratch_shapes=list(scratch),
        compiler_params=pltpu.CompilerParams(vmem_limit_bytes=limit),
    )


def exchange(values, axes):
    return lax.all_to_all(values, axes, split_axis=0, concat_axis=0, tiled=True)


def compact_on_device(
    image_states, latent, text_keys, text_values, mod_table, timestep, grid_size, rope_offset,
    w_qkv, q_gain, k_gain, w_out, w_fc1, w_fc2, w_final,
):
    rows = lax.axis_size("row")
    cols = lax.axis_size("col")
    stay = lambda values: pltpu.with_memory_space_constraint(values, pltpu.HBM)
    tile_w, width = image_states.shape
    head = q_gain.shape[0]
    piece = width // 8
    tokens = rows * tile_w
    both = ("row", "col")

    near = [(i, i ^ 1) for i in range(cols)]
    steps = stay(timestep)
    sizes = stay(grid_size.T)
    fc2 = stay(w_fc2)
    sems = lambda count: pltpu.SemaphoreType.DMA((count,))
    steps_space = pltpu.SMEM(timestep.shape, jnp.int32)
    sizes_space = pltpu.SMEM(grid_size.shape[::-1], jnp.int32)
    gain_space = pltpu.VMEM((1, head), f32)
    fc2_part = ((w_fc2.shape[0] // FC_PARTS, width), bf16)

    spread, given, mods, turn, mask = call(
        opening_kernel,
        [
            ((rows, tile_w, width), bf16),
            ((2, text_keys.shape[0], piece), bf16),
            (mod_table.shape, f32),
            ((4, tokens, head), f32),
            ((tokens, tokens), f32),
        ],
        [HBM_SPEC] * 8,
        [sizes_space, sizes_space, gain_space, gain_space, sems(8)],
    )(
        stay(image_states), stay(text_keys), stay(text_values), stay(mod_table), sizes, stay(rope_offset.T),
        stay(q_gain.reshape(1, head)), stay(k_gain.reshape(1, head)),
    )
    other = lax.ppermute(given, "row", [(i, i ^ 1) for i in range(rows)])
    w_x = lax.ppermute(w_out, "col", [(i, i ^ 2) for i in range(cols)])
    w_k = lax.ppermute(w_out, "col", near)
    gathered = exchange(spread, "row")
    half_rows = text_keys.shape[0]
    pieces, fc2_a, text, states, gate = call(
        qkv_kernel,
        [
            ((rows * cols, 4, piece), bf16),
            fc2_part,
            ((2, half_rows, piece), bf16),
            ((tokens, piece), f32),
            ((tokens, piece), f32),
        ],
        [HBM_SPEC] + [VMEM_SPEC] * 3 + [HBM_SPEC] * 3,
        [
            steps_space,
            pltpu.VMEM((tokens, width), f32),
            sems(4),
        ],
    )(
        steps, gathered, mods, lax.ppermute(w_qkv, "col", near), fc2, stay(text_keys), stay(text_values),
    )
    pieces, other, w_k = lax.optimization_barrier((pieces, other, w_k))
    got = exchange(pieces, both).reshape(rows, cols, 4, piece)
    mixed, w_own = call(
        attention_kernel,
        [((rows * cols, 4, piece), bf16), (w_out.shape, bf16)],
        [VMEM_SPEC] * 5 + [HBM_SPEC],
        [pltpu.VMEM((tokens, piece), f32)] * 3 + [sems(1)],
    )(got, text, other, turn, mask, stay(w_out))
    mixed, w_x = lax.optimization_barrier((mixed, w_x))
    w_xk = lax.ppermute(w_x, "col", near)
    all_mixed = exchange(mixed, both)
    (first,) = call(
        out_kernel, [((rows, tokens, piece), bf16)], [VMEM_SPEC] * 7, [pltpu.VMEM((tokens, width), f32)]
    )(all_mixed, states, gate, w_own, w_k, w_x, w_xk)
    all_first = exchange(first, "row")
    terms, first_own, final_here, last, live = call(
        mlp_kernel,
        [
            ((rows, tile_w, width), bf16),
            ((tile_w, width), f32),
            (w_final.shape[::-1], bf16),
            ((2, width), f32),
            (latent.shape, f32),
        ],
        [HBM_SPEC, HBM_SPEC] + [VMEM_SPEC] * 4 + [HBM_SPEC, HBM_SPEC],
        [steps_space, sizes_space, pltpu.VMEM((tokens, width), f32)]
        + [pltpu.VMEM(*fc2_part)] * 2
        + [sems(5)],
        limit=16 << 20,
    )(steps, sizes, all_first, mods, w_fc1, fc2_a, fc2, stay(w_final.T))
    all_terms = exchange(terms, "row")
    (masked,) = call(final_kernel, [(latent.shape, f32)], [VMEM_SPEC] * 5)(all_terms, first_own, last, final_here, live)
    beside = lax.ppermute(masked, "col", near)
    across = lax.ppermute(masked, "col", [(i, i ^ 3) for i in range(cols)])
    return call(blend_kernel, [(latent.shape, f32)] * 2, [VMEM_SPEC] * 5)(masked, live, beside, across, latent)


def solution(mesh):
    placed = (
        P(("row", "col"), None),
        P(("row", "col"), None),
        P("row", "col"),
        P("row", "col"),
        P(),
        P(),
        P(),
        P(),
        P(None, "row"),
        P(),
        P(),
        P("col", "row"),
        P(None, "row"),
        P("row", None),
        P(),
    )
    compact = mesh.shape["row"] == 2 * REQ and mesh.shape["col"] == 4
    return jax.shard_map(
        compact_on_device if compact else on_device,
        mesh=mesh,
        in_specs=placed,
        out_specs=(P(("row", "col"), None), P(("row", "col"), None)),
        check_vma=False,
    )
```

```python
import math

import jax
import jax.numpy as jnp
from jax import lax
from jax.experimental import pallas as pl
from jax.experimental.pallas import tpu as pltpu
from jax.sharding import PartitionSpec as P

REQ = 4
TXT = 256
STEPS = 4


eps_norm = 1e-06
blend = 0.25
mask_floor = -1e30


def with_halo(cells, sides, width):
    for axis, dim in sides:
        count = lax.axis_size(axis)
        ends = count - 1
        head = lax.slice_in_dim(cells, 0, width, axis=dim)
        tail = lax.slice_in_dim(cells, cells.shape[dim] - width, cells.shape[dim], axis=dim)
        cells = jnp.concatenate(
            [
                lax.ppermute(tail, axis, [(i, (i + 1) % count) for i in range(ends)]),
                cells,
                lax.ppermute(head, axis, [((i + 1) % count, i) for i in range(ends)]),
            ],
            axis=dim,
        )
    return cells


def layer_norm(values):
    mean_value = jnp.mean(values, -1, keepdims=True)
    centred = values - mean_value
    return centred * lax.rsqrt(jnp.mean(centred * centred, -1, keepdims=True) + eps_norm)


def modulate(values, shift_vec, scale_vec):
    return (layer_norm(values) * (1.0 + scale_vec) + shift_vec).astype(jnp.bfloat16)


def rope_tables(pos_h, pos_w, head_size):
    time_half = head_size // 16
    axis_dim = (head_size - head_size // 8) // 2
    freq_index = jnp.arange(axis_dim // 2, dtype=jnp.float32)
    frequency = 10000.0 ** (-2.0 * freq_index / axis_dim)
    angles = jnp.concatenate(
        [
            jnp.zeros((pos_h.shape[0], time_half), jnp.float32),
            pos_h[:, None] * frequency[None, :],
            pos_w[:, None] * frequency[None, :],
        ],
        1,
    )
    return (jnp.cos(angles), jnp.sin(angles))


def norm_rope(values, gain_vec, cosine_table, sine_table, head_count, head_size):
    row_total = values.shape[0]
    per_head = values.astype(jnp.float32).reshape(row_total, head_count, head_size)
    per_head = (
        per_head * lax.rsqrt(jnp.mean(per_head * per_head, -1, keepdims=True) + eps_norm) * gain_vec
    )
    paired = per_head.reshape(row_total, head_count, head_size // 2, 2)
    even_part = paired[..., 0]
    odd_part = paired[..., 1]
    cos_wide = cosine_table[:, None, :]
    sin_wide = sine_table[:, None, :]
    turned = jnp.stack(
        [even_part * cos_wide - odd_part * sin_wide, even_part * sin_wide + odd_part * cos_wide], -1
    )
    return turned.reshape(row_total, head_count * head_size).astype(jnp.bfloat16)


def on_device(
    image_states,
    latent,
    text_keys,
    text_values,
    mod_table,
    timestep,
    grid_size,
    rope_offset,
    w_qkv,
    q_gain,
    k_gain,
    w_out,
    w_fc1,
    w_fc2,
    w_final,
):
    col_total = lax.axis_size("col")
    row_pos = lax.axis_index("row")
    col_pos = lax.axis_index("col")
    tile_w = image_states.shape[0]
    width = image_states.shape[1]
    head_size = q_gain.shape[0]
    head_count = width // head_size
    local_heads = head_count // col_total
    request = row_pos % REQ
    grid_row = row_pos // REQ
    grid_col = col_pos * tile_w + jnp.arange(tile_w, dtype=jnp.int32)
    req_slots = jnp.arange(REQ, dtype=jnp.int32)
    req_onehot = req_slots == request
    limits = jnp.sum(jnp.where(req_onehot[:, None], grid_size, 0), 0)
    offsets = jnp.sum(jnp.where(req_onehot[:, None], rope_offset, 0), 0)
    step_now = jnp.sum(jnp.where(req_onehot, timestep, 0))
    token_ok = (grid_row < limits[0]) & (grid_col < limits[1])
    modulation = lax.dynamic_index_in_dim(mod_table, step_now, 0, keepdims=False)
    states = image_states.astype(jnp.float32)
    normed = modulate(states, modulation[0], modulation[1])
    joined_cols = jnp.dot(
        lax.all_gather(normed, "row", axis=0, tiled=True), w_qkv, preferred_element_type=jnp.float32
    ).astype(jnp.bfloat16)
    joined = lax.all_to_all(joined_cols, "row", split_axis=0, concat_axis=1, tiled=True)
    pos_h = jnp.zeros((tile_w,), jnp.float32) + (grid_row + offsets[0]).astype(jnp.float32)
    pos_w = (grid_col + offsets[1]).astype(jnp.float32)
    cosine_table, sine_table = rope_tables(pos_h, pos_w, head_size)
    queries = norm_rope(joined[:, :width], q_gain, cosine_table, sine_table, head_count, head_size)
    image_keys = norm_rope(
        joined[:, width : 2 * width], k_gain, cosine_table, sine_table, head_count, head_size
    )
    q_heads, k_heads, v_heads = (
        lax.all_to_all(queries, "col", split_axis=1, concat_axis=0, tiled=True),
        lax.all_to_all(image_keys, "col", split_axis=1, concat_axis=0, tiled=True),
        lax.all_to_all(joined[:, 2 * width :], "col", split_axis=1, concat_axis=0, tiled=True),
    )
    image_rows = k_heads.shape[0]
    text_rows = text_keys.shape[0]
    shard_rows = image_rows + text_rows
    q_block = q_heads.reshape(image_rows, local_heads, head_size)
    key_rows = jnp.concatenate([k_heads, text_keys], 0)
    value_rows = jnp.concatenate([v_heads, text_values], 0)
    run_max = jnp.full((image_rows, local_heads), mask_floor, jnp.float32)
    key_piece = lax.all_gather(key_rows, "row", axis=0, tiled=True)
    value_piece = lax.all_gather(value_rows, "row", axis=0, tiled=True)
    piece_rows = key_piece.shape[0]
    global_row = jnp.arange(piece_rows, dtype=jnp.int32)
    shard_id = global_row // shard_rows
    within = global_row % shard_rows
    is_image = within < image_rows
    source_col = within // tile_w
    source_cell = within % tile_w
    image_req = shard_id % REQ
    text_req = (shard_id * text_rows + within - image_rows) // TXT
    key_req = jnp.where(is_image, image_req, text_req)
    key_onehot = key_req[:, None] == req_slots[None, :]
    key_height = jnp.sum(jnp.where(key_onehot, grid_size[:, 0][None, :], 0), 1)
    key_width = jnp.sum(jnp.where(key_onehot, grid_size[:, 1][None, :], 0), 1)
    image_ok = (shard_id // REQ < key_height) & (source_col * tile_w + source_cell < key_width)
    key_ok = (key_req == request) & (jnp.logical_not(is_image) | image_ok)
    scores = jnp.einsum(
        "qhd,khd->qhk",
        q_block,
        key_piece.reshape(piece_rows, local_heads, head_size),
        preferred_element_type=jnp.float32,
    ) * head_size ** (-0.5)
    new_max = jnp.maximum(run_max, jnp.max(jnp.where(key_ok, scores, mask_floor), -1))
    weights = jnp.where(key_ok, jnp.exp(scores - new_max[..., None]), 0.0)
    new_sum = jnp.sum(weights, -1)
    new_acc = jnp.einsum(
        "qhk,khd->qhd",
        weights.astype(jnp.bfloat16),
        value_piece.reshape(piece_rows, local_heads, head_size),
        preferred_element_type=jnp.float32,
    )
    mixed = (
        (new_acc / new_sum[..., None])
        .astype(jnp.bfloat16)
        .reshape(image_rows, local_heads * head_size)
    )
    partial_out = jnp.dot(
        mixed, lax.all_gather(w_out, "row", axis=1, tiled=True), preferred_element_type=jnp.float32
    )
    attended = lax.psum_scatter(
        partial_out.astype(jnp.bfloat16), "col", scatter_dimension=0, tiled=True
    ).astype(jnp.float32)
    first_res = (states + modulation[2] * attended).astype(jnp.bfloat16)
    normed_two = modulate(first_res.astype(jnp.float32), modulation[3], modulation[4])
    all_rows = lax.all_gather(normed_two, "row", axis=0, tiled=True)
    hidden = jax.nn.gelu(
        jnp.dot(all_rows, w_fc1, preferred_element_type=jnp.float32), approximate=True
    ).astype(jnp.bfloat16)
    every_term = jnp.dot(hidden, w_fc2, preferred_element_type=jnp.float32)
    every_sum = lax.psum(every_term, "row")
    mlp_out = lax.dynamic_slice_in_dim(every_sum, row_pos * tile_w, tile_w, 0)
    second_res = first_res.astype(jnp.float32) + modulation[5] * mlp_out
    normed_three = modulate(second_res, modulation[6], modulation[7])
    raw_velocity = jnp.dot(normed_three, w_final, preferred_element_type=jnp.float32)
    masked = jnp.where(token_ok[:, None], raw_velocity, 0.0)
    padded = with_halo(masked, (("col", 0),), 1)
    left_side = padded[:-2]
    right_side = padded[2:]
    velocity = jnp.where(
        token_ok[:, None], masked + blend * (left_side + right_side - 2.0 * masked), 0.0
    )
    next_latent = latent + -1.0 / STEPS * velocity
    return (velocity, next_latent)


bf16 = jnp.bfloat16
FC_PARTS = 3
f32 = jnp.float32
VMEM_SPEC = pl.BlockSpec(memory_space=pltpu.VMEM)
HBM_SPEC = pl.BlockSpec(memory_space=pltpu.HBM)


def start_copies(pairs, sems):
    copies = [pltpu.make_async_copy(source, target, sems.at[i]) for i, (source, target) in enumerate(pairs)]
    for copy in copies:
        copy.start()
    return copies


def part_rows(hbm, index):
    size = hbm.shape[0] // FC_PARTS
    return hbm.at[pl.ds(index * size, size), :]


def lane_mean(values):
    return jnp.mean(values, -1, keepdims=True)


def norm_rows(values):
    centred = values - lane_mean(values)
    return centred * lax.rsqrt(lane_mean(centred * centred) + eps_norm)


def per_request(mod_ref, step_ref, slot, rows_each, start, size):
    pieces = [
        jnp.broadcast_to(mod_ref[step_ref[q], pl.ds(slot, 1), pl.ds(start, size)], (rows_each, size))
        for q in range(REQ)
    ]
    row = lax.broadcasted_iota(jnp.int32, (REQ * rows_each, size), 0) // rows_each
    whole = jnp.concatenate([pieces[0]] * REQ, 0)
    for q in range(1, REQ):
        whole = jnp.where(row == q, jnp.concatenate([pieces[q]] * REQ, 0), whole)
    return whole


def qkv_kernel(
    step_hbm, tokens_ref, mod_ref, w_ref, fc2_hbm, text_k_hbm, text_v_hbm, out_ref, fc2_ref, text_ref, states_ref, gate_ref,
    step_ref, order_ref, sems,
):
    row = lax.axis_index("row")
    depth = order_ref.shape[1]
    size = out_ref.shape[2]
    here = pl.ds(pl.multiple_of(lax.rem(row, 2) * size, size), size)
    copies = start_copies(
        [
            (step_hbm, step_ref),
            (text_k_hbm.at[:, here], text_ref.at[0]),
            (text_v_hbm.at[:, here], text_ref.at[1]),
            (part_rows(fc2_hbm, 0), fc2_ref),
        ],
        sems,
    )
    for q in range(REQ):
        for g in range(2):
            order_ref[4 * q + 2 * g : 4 * q + 2 * g + 2, :] = tokens_ref[REQ * g + q].astype(f32)
    out_ref[...] = jnp.zeros_like(out_ref)
    normed = norm_rows(order_ref[...])
    for copy in copies[:1]:
        copy.wait()
    shift = per_request(mod_ref, step_ref, 0, 4, 0, depth)
    scale = per_request(mod_ref, step_ref, 1, 4, 0, depth)
    normed = (normed * (1.0 + scale) + shift).astype(bf16)
    whole = jnp.dot(normed, w_ref[...], preferred_element_type=f32).astype(bf16)
    start = pl.multiple_of(row * size, size)
    states_ref[...] = order_ref[:, pl.ds(start, size)]
    gate_ref[...] = per_request(mod_ref, step_ref, 2, 4, start, size)
    for piece in range(w_ref.shape[1] // size):
        group = lax.rem(row * 3 + piece, 8)
        place = (group // 2) * 8 + lax.rem(group, 2)
        for q in range(REQ):
            out_ref[2 * q + place] = whole[4 * q : 4 * q + 4, piece * size : (piece + 1) * size]
    for copy in copies[1:]:
        copy.wait()


def swap_pairs(values):
    count = values.shape[-1]
    even = lax.rem(lax.broadcasted_iota(jnp.int32, values.shape, 1), 2) == 0
    return jnp.where(even, pltpu.roll(values, count - 1, 1), pltpu.roll(values, 1, 1))


def turn_tables(req, size_ref, offset_ref, q_gain_ref, k_gain_ref, turn_ref, mask_ref):
    _, count, head = turn_ref.shape
    token = lax.broadcasted_iota(jnp.int32, (count, 1), 0)
    pos_h = lax.rem(token, 4) // 2
    pos_w = (token // 4) * 2 + lax.rem(token, 2)
    lane = lax.broadcasted_iota(jnp.int32, (count, head), 1)
    pair = lane // 2
    time_half = head // 16
    axis_dim = (head - head // 8) // 2
    half = axis_dim // 2
    in_h = (pair >= time_half) & (pair < time_half + half)
    index = jnp.where(in_h, pair - time_half, pair - time_half - half).astype(f32)
    frequency = jnp.exp(index * f32(-2.0 * math.log(10000.0) / axis_dim))
    spot = jnp.where(in_h, pos_h + offset_ref[0, req], pos_w + offset_ref[1, req]).astype(f32)
    angle = jnp.where(pair < time_half, 0.0, spot * frequency)
    cosine = jnp.cos(angle)
    sine = jnp.sin(angle)
    sine = jnp.where(lax.rem(lane, 2) == 0, -sine, sine)
    for i, gain_ref in enumerate((q_gain_ref, k_gain_ref)):
        gain = jnp.broadcast_to(gain_ref[...], (count, head))
        turn_ref[2 * i] = gain * cosine
        turn_ref[2 * i + 1] = swap_pairs(gain) * sine
    key = lax.broadcasted_iota(jnp.int32, (count, count), 1)
    live = (lax.rem(key, 4) // 2 < size_ref[0, req]) & ((key // 4) * 2 + lax.rem(key, 2) < size_ref[1, req])
    mask_ref[...] = jnp.where(live, 1.0, 0.0)


def opening_kernel(
    states_hbm, k_hbm, v_hbm, mod_hbm, size_hbm, offset_hbm, q_gain_hbm, k_gain_hbm,
    spread_ref, given_ref, mod_ref, turn_ref, mask_ref, size_ref, offset_ref, q_gain_ref, k_gain_ref, sems,
):
    size = given_ref.shape[2]
    start = (1 - lax.rem(lax.axis_index("row"), 2)) * size
    part = pl.ds(pl.multiple_of(start, size), size)
    states_copy, *text_copies = start_copies(
        [
            (states_hbm, spread_ref.at[0]),
            (k_hbm.at[:, part], given_ref.at[0]),
            (v_hbm.at[:, part], given_ref.at[1]),
            (mod_hbm, mod_ref),
            (size_hbm, size_ref),
            (offset_hbm, offset_ref),
            (q_gain_hbm, q_gain_ref),
            (k_gain_hbm, k_gain_ref),
        ],
        sems,
    )
    states_copy.wait()
    states = spread_ref[0]
    for r in range(1, spread_ref.shape[0]):
        spread_ref[r] = states
    for copy in text_copies:
        copy.wait()
    turn_tables(lax.axis_index("row") // 2, size_ref, offset_ref, q_gain_ref, k_gain_ref, turn_ref, mask_ref)


def attention_kernel(
    rows_ref, text_ref, other_ref, turn_ref, mask_ref, w_hbm, out_ref, w_ref, q_ref, k_ref, v_ref, sems
):
    (w_copy,) = start_copies([(w_hbm, w_ref)], sems)
    group = 2 * lax.axis_index("col") + lax.rem(lax.axis_index("row"), 2)
    count, width = q_ref.shape
    head = turn_ref.shape[2]
    for which, ref in enumerate((q_ref, k_ref, v_ref)):
        source = (8 * which + group) // 3
        for s in range(4):
            ref[4 * s : 4 * s + 4, :] = rows_ref[s, source].astype(f32)

    def turned(values, which):
        values = values * lax.rsqrt(lane_mean(values * values) + eps_norm)
        return (values * turn_ref[2 * which] + swap_pairs(values) * turn_ref[2 * which + 1]).astype(bf16)

    key_ok = mask_ref[...] > 0.0
    contract = (((1,), (1,)), ((), ()))
    scale = head ** (-0.5)
    for h in range(width // head):
        cols = slice(h * head, (h + 1) * head)
        q = turned(q_ref[:, cols], 0)
        k = turned(k_ref[:, cols], 1)
        v = v_ref[:, cols].astype(bf16)
        s_own = lax.dot_general(q, text_ref[0, :, cols], contract, preferred_element_type=f32) * scale
        s_other = lax.dot_general(q, other_ref[0, :, cols], contract, preferred_element_type=f32) * scale
        s_image = lax.dot_general(q, k, contract, preferred_element_type=f32) * scale
        s_image = jnp.where(key_ok, s_image, mask_floor)
        top = jnp.maximum(
            jnp.max(jnp.maximum(s_own, s_other), -1, keepdims=True), jnp.max(s_image, -1, keepdims=True)
        )
        w_own = jnp.exp(s_own - top)
        w_other = jnp.exp(s_other - top)
        w_image = jnp.where(key_ok, jnp.exp(s_image - top), 0.0)
        total = jnp.sum(w_own + w_other, -1, keepdims=True) + jnp.sum(w_image, -1, keepdims=True)
        summed = (
            jnp.dot(w_own.astype(bf16), text_ref[1, :, cols], preferred_element_type=f32)
            + jnp.dot(w_other.astype(bf16), other_ref[1, :, cols], preferred_element_type=f32)
            + jnp.dot(w_image.astype(bf16), v, preferred_element_type=f32)
        )
        mixed = (summed / total).astype(bf16)
        for s in range(4):
            for r in range(8):
                out_ref[8 * s + r, :, cols] = mixed[4 * s : 4 * s + 4, :]
    w_copy.wait()


def out_kernel(mixed_ref, states_ref, gate_ref, w0_ref, w1_ref, w2_ref, w3_ref, out_ref, rows_ref):
    col = lax.axis_index("col")
    depth = w0_ref.shape[0]
    piece = mixed_ref.shape[2]
    for r in range(8):
        for s in range(4):
            at = (2 * s + r % 2) * piece
            rows_ref[4 * (r // 2) : 4 * (r // 2) + 4, at : at + piece] = mixed_ref[8 * s + r].astype(f32)
    attended = 0.0
    for d, w_ref in enumerate((w0_ref, w1_ref, w2_ref, w3_ref)):
        at = pl.multiple_of(jnp.bitwise_xor(col, d) * depth, depth)
        share = rows_ref[:, pl.ds(at, depth)].astype(bf16)
        attended = attended + jnp.dot(share, w_ref[...], preferred_element_type=f32)
    first = (states_ref[...] + gate_ref[...] * attended).astype(bf16)
    for r in range(8):
        out_ref[r] = first


def mlp_kernel(
    step_hbm, size_hbm, first_ref, mod_ref, w1_ref, w2a_ref, w2_hbm, final_hbm, out_ref, own_ref, final_ref, last_ref,
    live_ref, step_ref, size_ref, rows_ref, w2b_ref, w2c_ref, sems,
):
    row = lax.axis_index("row")
    depth = rows_ref.shape[1]
    piece = first_ref.shape[2]
    step_copy, size_copy, *w_copies = start_copies(
        [
            (step_hbm, step_ref),
            (size_hbm, size_ref),
            (part_rows(w2_hbm, 1), w2b_ref),
            (part_rows(w2_hbm, 2), w2c_ref),
            (final_hbm, final_ref),
        ],
        sems,
    )
    for r in range(8):
        rows_ref[:, r * piece : (r + 1) * piece] = first_ref[r].astype(f32)
    normed = norm_rows(rows_ref[...])
    step_copy.wait()
    size_copy.wait()
    shift = per_request(mod_ref, step_ref, 3, 4, 0, depth)
    scale = per_request(mod_ref, step_ref, 4, 4, 0, depth)
    normed = (normed * (1.0 + scale) + shift).astype(bf16)
    own = rows_ref[0:2, :]
    for q in range(REQ):
        for g in range(2):
            own = jnp.where(row == REQ * g + q, rows_ref[4 * q + 2 * g : 4 * q + 2 * g + 2, :], own)
    own_ref[...] = own
    req = lax.rem(row, REQ)
    last_ref[...] = mod_ref[step_ref[req], 6:8, :]
    grid_col = lax.axis_index("col") * live_ref.shape[0] + lax.broadcasted_iota(jnp.int32, live_ref.shape, 0)
    live = (row // REQ < size_ref[0, req]) & (grid_col < size_ref[1, req])
    live_ref[...] = jnp.where(live, 1.0, 0.0)
    hidden = jax.nn.gelu(
        jnp.dot(normed, w1_ref[...], preferred_element_type=f32), approximate=True
    ).astype(bf16)
    size = w2a_ref.shape[0]
    added = 0.0
    for i, w_ref in enumerate((w2a_ref, w2b_ref, w2c_ref)):
        if i > 0:
            w_copies[i - 1].wait()
        added = added + jnp.dot(hidden[:, i * size : (i + 1) * size], w_ref[...], preferred_element_type=f32)
    gate = per_request(mod_ref, step_ref, 5, 4, 0, depth)
    term = (gate * added).astype(out_ref.dtype)
    for q in range(REQ):
        for g in range(2):
            out_ref[REQ * g + q] = term[4 * q + 2 * g : 4 * q + 2 * g + 2, :]
    w_copies[2].wait()


def final_kernel(terms_ref, first_ref, last_ref, w_ref, live_ref, out_ref):
    second = first_ref[...]
    for r in range(8):
        second = second + terms_ref[r].astype(f32)
    normed = (norm_rows(second) * (1.0 + last_ref[1:2, :]) + last_ref[0:1, :]).astype(bf16)
    raw = lax.dot_general(normed, w_ref[...], (((1,), (1,)), ((), ())), preferred_element_type=f32)
    out_ref[...] = jnp.where(live_ref[...] > 0.0, raw, 0.0)


def blend_kernel(masked_ref, live_ref, near_ref, far_ref, latent_ref, velocity_ref, next_ref):
    col = lax.axis_index("col")
    masked = masked_ref[...]
    near = near_ref[...]
    far = jnp.where((col == 1) | (col == 2), far_ref[...], 0.0)
    odd = lax.rem(col, 2) == 1
    count = masked.shape[0]
    left = jnp.concatenate([jnp.where(odd, near, far)[count - 1 :, :], masked[: count - 1, :]], 0)
    right = jnp.concatenate([masked[1:, :], jnp.where(odd, far, near)[:1, :]], 0)
    velocity = jnp.where(live_ref[...] > 0.0, masked + blend * (left + right - 2.0 * masked), 0.0)
    velocity_ref[...] = velocity
    next_ref[...] = latent_ref[...] + -1.0 / STEPS * velocity


def call(kernel, outs, specs, scratch=(), limit=8 << 20):
    return pl.pallas_call(
        kernel,
        out_shape=tuple(jax.ShapeDtypeStruct(shape, dtype) for shape, dtype in outs),
        in_specs=specs,
        out_specs=(VMEM_SPEC,) * len(outs),
        scratch_shapes=list(scratch),
        compiler_params=pltpu.CompilerParams(vmem_limit_bytes=limit),
    )


def exchange(values, axes):
    return lax.all_to_all(values, axes, split_axis=0, concat_axis=0, tiled=True)


def compact_on_device(
    image_states, latent, text_keys, text_values, mod_table, timestep, grid_size, rope_offset,
    w_qkv, q_gain, k_gain, w_out, w_fc1, w_fc2, w_final,
):
    rows = lax.axis_size("row")
    cols = lax.axis_size("col")
    stay = lambda values: pltpu.with_memory_space_constraint(values, pltpu.HBM)
    tile_w, width = image_states.shape
    head = q_gain.shape[0]
    piece = width // 8
    tokens = rows * tile_w
    both = ("col", "row")

    near = [(i, i ^ 1) for i in range(cols)]
    steps = stay(timestep)
    sizes = stay(grid_size.T)
    fc2 = stay(w_fc2)
    sems = lambda count: pltpu.SemaphoreType.DMA((count,))
    steps_space = pltpu.SMEM(timestep.shape, jnp.int32)
    sizes_space = pltpu.SMEM(grid_size.shape[::-1], jnp.int32)
    gain_space = pltpu.VMEM((1, head), f32)
    fc2_part = ((w_fc2.shape[0] // FC_PARTS, width), bf16)

    spread, given, mods, turn, mask = call(
        opening_kernel,
        [
            ((rows, tile_w, width), bf16),
            ((2, text_keys.shape[0], piece), bf16),
            (mod_table.shape, f32),
            ((4, tokens, head), f32),
            ((tokens, tokens), f32),
        ],
        [HBM_SPEC] * 8,
        [sizes_space, sizes_space, gain_space, gain_space, sems(8)],
    )(
        stay(image_states), stay(text_keys), stay(text_values), stay(mod_table), sizes, stay(rope_offset.T),
        stay(q_gain.reshape(1, head)), stay(k_gain.reshape(1, head)),
    )
    other = lax.ppermute(given, "row", [(i, i ^ 1) for i in range(rows)])
    w_x = lax.ppermute(w_out, "col", [(i, i ^ 2) for i in range(cols)])
    w_k = lax.ppermute(w_out, "col", near)
    gathered = exchange(spread, "row")
    half_rows = text_keys.shape[0]
    pieces, fc2_a, text, states, gate = call(
        qkv_kernel,
        [
            ((rows * cols, 4, piece), bf16),
            fc2_part,
            ((2, half_rows, piece), bf16),
            ((tokens, piece), f32),
            ((tokens, piece), f32),
        ],
        [HBM_SPEC] + [VMEM_SPEC] * 3 + [HBM_SPEC] * 3,
        [
            steps_space,
            pltpu.VMEM((tokens, width), f32),
            sems(4),
        ],
    )(
        steps, gathered, mods, lax.ppermute(w_qkv, "col", near), fc2, stay(text_keys), stay(text_values),
    )
    pieces, other, w_k = lax.optimization_barrier((pieces, other, w_k))
    got = exchange(pieces, both).reshape(cols, rows, 4, piece)
    mixed, w_own = call(
        attention_kernel,
        [((rows * cols, 4, piece), bf16), (w_out.shape, bf16)],
        [VMEM_SPEC] * 5 + [HBM_SPEC],
        [pltpu.VMEM((tokens, piece), f32)] * 3 + [sems(1)],
    )(got, text, other, turn, mask, stay(w_out))
    mixed, w_x = lax.optimization_barrier((mixed, w_x))
    w_xk = lax.ppermute(w_x, "col", near)
    all_mixed = exchange(mixed, both)
    (first,) = call(
        out_kernel, [((rows, tokens, piece), bf16)], [VMEM_SPEC] * 7, [pltpu.VMEM((tokens, width), f32)]
    )(all_mixed, states, gate, w_own, w_k, w_x, w_xk)
    all_first = exchange(first, "row")
    terms, first_own, final_here, last, live = call(
        mlp_kernel,
        [
            ((rows, tile_w, width), bf16),
            ((tile_w, width), f32),
            (w_final.shape[::-1], bf16),
            ((2, width), f32),
            (latent.shape, f32),
        ],
        [HBM_SPEC, HBM_SPEC] + [VMEM_SPEC] * 4 + [HBM_SPEC, HBM_SPEC],
        [steps_space, sizes_space, pltpu.VMEM((tokens, width), f32)]
        + [pltpu.VMEM(*fc2_part)] * 2
        + [sems(5)],
        limit=16 << 20,
    )(steps, sizes, all_first, mods, w_fc1, fc2_a, fc2, stay(w_final.T))
    all_terms = exchange(terms, "row")
    (masked,) = call(final_kernel, [(latent.shape, f32)], [VMEM_SPEC] * 5)(all_terms, first_own, last, final_here, live)
    beside = lax.ppermute(masked, "col", near)
    across = lax.ppermute(masked, "col", [(i, i ^ 3) for i in range(cols)])
    return call(blend_kernel, [(latent.shape, f32)] * 2, [VMEM_SPEC] * 5)(masked, live, beside, across, latent)


def solution(mesh):
    placed = (
        P(("row", "col"), None),
        P(("row", "col"), None),
        P("row", "col"),
        P("row", "col"),
        P(),
        P(),
        P(),
        P(),
        P(None, "row"),
        P(),
        P(),
        P("col", "row"),
        P(None, "row"),
        P("row", None),
        P(),
    )
    compact = mesh.shape["row"] == 2 * REQ and mesh.shape["col"] == 4
    return jax.shard_map(
        compact_on_device if compact else on_device,
        mesh=mesh,
        in_specs=placed,
        out_specs=(P(("row", "col"), None), P(("row", "col"), None)),
        check_vma=False,
    )
```

```python
import math

import jax
import jax.numpy as jnp
from jax import lax
from jax.experimental import pallas as pl
from jax.experimental.pallas import tpu as pltpu
from jax.sharding import PartitionSpec as P

REQ = 4
TXT = 256
STEPS = 4


eps_norm = 1e-06
blend = 0.25
mask_floor = -1e30


def with_halo(cells, sides, width):
    for axis, dim in sides:
        count = lax.axis_size(axis)
        ends = count - 1
        head = lax.slice_in_dim(cells, 0, width, axis=dim)
        tail = lax.slice_in_dim(cells, cells.shape[dim] - width, cells.shape[dim], axis=dim)
        cells = jnp.concatenate(
            [
                lax.ppermute(tail, axis, [(i, (i + 1) % count) for i in range(ends)]),
                cells,
                lax.ppermute(head, axis, [((i + 1) % count, i) for i in range(ends)]),
            ],
            axis=dim,
        )
    return cells


def layer_norm(values):
    mean_value = jnp.mean(values, -1, keepdims=True)
    centred = values - mean_value
    return centred * lax.rsqrt(jnp.mean(centred * centred, -1, keepdims=True) + eps_norm)


def modulate(values, shift_vec, scale_vec):
    return (layer_norm(values) * (1.0 + scale_vec) + shift_vec).astype(jnp.bfloat16)


def rope_tables(pos_h, pos_w, head_size):
    time_half = head_size // 16
    axis_dim = (head_size - head_size // 8) // 2
    freq_index = jnp.arange(axis_dim // 2, dtype=jnp.float32)
    frequency = 10000.0 ** (-2.0 * freq_index / axis_dim)
    angles = jnp.concatenate(
        [
            jnp.zeros((pos_h.shape[0], time_half), jnp.float32),
            pos_h[:, None] * frequency[None, :],
            pos_w[:, None] * frequency[None, :],
        ],
        1,
    )
    return (jnp.cos(angles), jnp.sin(angles))


def norm_rope(values, gain_vec, cosine_table, sine_table, head_count, head_size):
    row_total = values.shape[0]
    per_head = values.astype(jnp.float32).reshape(row_total, head_count, head_size)
    per_head = (
        per_head * lax.rsqrt(jnp.mean(per_head * per_head, -1, keepdims=True) + eps_norm) * gain_vec
    )
    paired = per_head.reshape(row_total, head_count, head_size // 2, 2)
    even_part = paired[..., 0]
    odd_part = paired[..., 1]
    cos_wide = cosine_table[:, None, :]
    sin_wide = sine_table[:, None, :]
    turned = jnp.stack(
        [even_part * cos_wide - odd_part * sin_wide, even_part * sin_wide + odd_part * cos_wide], -1
    )
    return turned.reshape(row_total, head_count * head_size).astype(jnp.bfloat16)


def on_device(
    image_states,
    latent,
    text_keys,
    text_values,
    mod_table,
    timestep,
    grid_size,
    rope_offset,
    w_qkv,
    q_gain,
    k_gain,
    w_out,
    w_fc1,
    w_fc2,
    w_final,
):
    col_total = lax.axis_size("col")
    row_pos = lax.axis_index("row")
    col_pos = lax.axis_index("col")
    tile_w = image_states.shape[0]
    width = image_states.shape[1]
    head_size = q_gain.shape[0]
    head_count = width // head_size
    local_heads = head_count // col_total
    request = row_pos % REQ
    grid_row = row_pos // REQ
    grid_col = col_pos * tile_w + jnp.arange(tile_w, dtype=jnp.int32)
    req_slots = jnp.arange(REQ, dtype=jnp.int32)
    req_onehot = req_slots == request
    limits = jnp.sum(jnp.where(req_onehot[:, None], grid_size, 0), 0)
    offsets = jnp.sum(jnp.where(req_onehot[:, None], rope_offset, 0), 0)
    step_now = jnp.sum(jnp.where(req_onehot, timestep, 0))
    token_ok = (grid_row < limits[0]) & (grid_col < limits[1])
    modulation = lax.dynamic_index_in_dim(mod_table, step_now, 0, keepdims=False)
    states = image_states.astype(jnp.float32)
    normed = modulate(states, modulation[0], modulation[1])
    joined_cols = jnp.dot(
        lax.all_gather(normed, "row", axis=0, tiled=True), w_qkv, preferred_element_type=jnp.float32
    ).astype(jnp.bfloat16)
    joined = lax.all_to_all(joined_cols, "row", split_axis=0, concat_axis=1, tiled=True)
    pos_h = jnp.zeros((tile_w,), jnp.float32) + (grid_row + offsets[0]).astype(jnp.float32)
    pos_w = (grid_col + offsets[1]).astype(jnp.float32)
    cosine_table, sine_table = rope_tables(pos_h, pos_w, head_size)
    queries = norm_rope(joined[:, :width], q_gain, cosine_table, sine_table, head_count, head_size)
    image_keys = norm_rope(
        joined[:, width : 2 * width], k_gain, cosine_table, sine_table, head_count, head_size
    )
    q_heads, k_heads, v_heads = (
        lax.all_to_all(queries, "col", split_axis=1, concat_axis=0, tiled=True),
        lax.all_to_all(image_keys, "col", split_axis=1, concat_axis=0, tiled=True),
        lax.all_to_all(joined[:, 2 * width :], "col", split_axis=1, concat_axis=0, tiled=True),
    )
    image_rows = k_heads.shape[0]
    text_rows = text_keys.shape[0]
    shard_rows = image_rows + text_rows
    q_block = q_heads.reshape(image_rows, local_heads, head_size)
    key_rows = jnp.concatenate([k_heads, text_keys], 0)
    value_rows = jnp.concatenate([v_heads, text_values], 0)
    run_max = jnp.full((image_rows, local_heads), mask_floor, jnp.float32)
    key_piece = lax.all_gather(key_rows, "row", axis=0, tiled=True)
    value_piece = lax.all_gather(value_rows, "row", axis=0, tiled=True)
    piece_rows = key_piece.shape[0]
    global_row = jnp.arange(piece_rows, dtype=jnp.int32)
    shard_id = global_row // shard_rows
    within = global_row % shard_rows
    is_image = within < image_rows
    source_col = within // tile_w
    source_cell = within % tile_w
    image_req = shard_id % REQ
    text_req = (shard_id * text_rows + within - image_rows) // TXT
    key_req = jnp.where(is_image, image_req, text_req)
    key_onehot = key_req[:, None] == req_slots[None, :]
    key_height = jnp.sum(jnp.where(key_onehot, grid_size[:, 0][None, :], 0), 1)
    key_width = jnp.sum(jnp.where(key_onehot, grid_size[:, 1][None, :], 0), 1)
    image_ok = (shard_id // REQ < key_height) & (source_col * tile_w + source_cell < key_width)
    key_ok = (key_req == request) & (jnp.logical_not(is_image) | image_ok)
    scores = jnp.einsum(
        "qhd,khd->qhk",
        q_block,
        key_piece.reshape(piece_rows, local_heads, head_size),
        preferred_element_type=jnp.float32,
    ) * head_size ** (-0.5)
    new_max = jnp.maximum(run_max, jnp.max(jnp.where(key_ok, scores, mask_floor), -1))
    weights = jnp.where(key_ok, jnp.exp(scores - new_max[..., None]), 0.0)
    new_sum = jnp.sum(weights, -1)
    new_acc = jnp.einsum(
        "qhk,khd->qhd",
        weights.astype(jnp.bfloat16),
        value_piece.reshape(piece_rows, local_heads, head_size),
        preferred_element_type=jnp.float32,
    )
    mixed = (
        (new_acc / new_sum[..., None])
        .astype(jnp.bfloat16)
        .reshape(image_rows, local_heads * head_size)
    )
    partial_out = jnp.dot(
        mixed, lax.all_gather(w_out, "row", axis=1, tiled=True), preferred_element_type=jnp.float32
    )
    attended = lax.psum_scatter(
        partial_out.astype(jnp.bfloat16), "col", scatter_dimension=0, tiled=True
    ).astype(jnp.float32)
    first_res = (states + modulation[2] * attended).astype(jnp.bfloat16)
    normed_two = modulate(first_res.astype(jnp.float32), modulation[3], modulation[4])
    all_rows = lax.all_gather(normed_two, "row", axis=0, tiled=True)
    hidden = jax.nn.gelu(
        jnp.dot(all_rows, w_fc1, preferred_element_type=jnp.float32), approximate=True
    ).astype(jnp.bfloat16)
    every_term = jnp.dot(hidden, w_fc2, preferred_element_type=jnp.float32)
    every_sum = lax.psum(every_term, "row")
    mlp_out = lax.dynamic_slice_in_dim(every_sum, row_pos * tile_w, tile_w, 0)
    second_res = first_res.astype(jnp.float32) + modulation[5] * mlp_out
    normed_three = modulate(second_res, modulation[6], modulation[7])
    raw_velocity = jnp.dot(normed_three, w_final, preferred_element_type=jnp.float32)
    masked = jnp.where(token_ok[:, None], raw_velocity, 0.0)
    padded = with_halo(masked, (("col", 0),), 1)
    left_side = padded[:-2]
    right_side = padded[2:]
    velocity = jnp.where(
        token_ok[:, None], masked + blend * (left_side + right_side - 2.0 * masked), 0.0
    )
    next_latent = latent + -1.0 / STEPS * velocity
    return (velocity, next_latent)


bf16 = jnp.bfloat16
FC_PARTS = 3
f32 = jnp.float32
VMEM_SPEC = pl.BlockSpec(memory_space=pltpu.VMEM)
HBM_SPEC = pl.BlockSpec(memory_space=pltpu.HBM)


def start_copies(pairs, sems):
    copies = [pltpu.make_async_copy(source, target, sems.at[i]) for i, (source, target) in enumerate(pairs)]
    for copy in copies:
        copy.start()
    return copies


def part_rows(hbm, index):
    size = hbm.shape[0] // FC_PARTS
    return hbm.at[pl.ds(index * size, size), :]


def lane_mean(values):
    return jnp.mean(values, -1, keepdims=True)


def norm_rows(values):
    centred = values - lane_mean(values)
    return centred * lax.rsqrt(lane_mean(centred * centred) + eps_norm)


def per_request(mod_ref, step_ref, slot, rows_each, start, size):
    shape = (REQ * rows_each, size)
    row = lax.broadcasted_iota(jnp.int32, shape, 0) // rows_each
    whole = None
    for q in range(REQ):
        vector = jnp.broadcast_to(mod_ref[step_ref[q], pl.ds(slot, 1), pl.ds(start, size)], shape)
        whole = vector if whole is None else jnp.where(row == q, vector, whole)
    return whole


def qkv_kernel(
    step_hbm, tokens_ref, mod_ref, w_ref, fc2_hbm, text_k_hbm, text_v_hbm, out_ref, fc2_ref, text_ref, states_ref, gate_ref,
    step_ref, order_ref, sems,
):
    row = lax.axis_index("row")
    depth = order_ref.shape[1]
    size = out_ref.shape[2]
    here = pl.ds(pl.multiple_of(lax.rem(row, 2) * size, size), size)
    copies = start_copies(
        [
            (step_hbm, step_ref),
            (text_k_hbm.at[:, here], text_ref.at[0]),
            (text_v_hbm.at[:, here], text_ref.at[1]),
            (part_rows(fc2_hbm, 0), fc2_ref),
        ],
        sems,
    )
    for q in range(REQ):
        for g in range(2):
            order_ref[4 * q + 2 * g : 4 * q + 2 * g + 2, :] = tokens_ref[REQ * g + q].astype(f32)
    out_ref[...] = jnp.zeros_like(out_ref)
    normed = norm_rows(order_ref[...])
    for copy in copies[:1]:
        copy.wait()
    shift = per_request(mod_ref, step_ref, 0, 4, 0, depth)
    scale = per_request(mod_ref, step_ref, 1, 4, 0, depth)
    normed = (normed * (1.0 + scale) + shift).astype(bf16)
    whole = jnp.dot(normed, w_ref[...], preferred_element_type=f32).astype(bf16)
    start = pl.multiple_of(row * size, size)
    states_ref[...] = order_ref[:, pl.ds(start, size)]
    gate_ref[...] = per_request(mod_ref, step_ref, 2, 4, start, size)
    for piece in range(w_ref.shape[1] // size):
        group = lax.rem(row * 3 + piece, 8)
        place = (group // 2) * 8 + lax.rem(group, 2)
        for q in range(REQ):
            out_ref[2 * q + place] = whole[4 * q : 4 * q + 4, piece * size : (piece + 1) * size]
    for copy in copies[1:]:
        copy.wait()


def swap_pairs(values):
    count = values.shape[-1]
    even = lax.rem(lax.broadcasted_iota(jnp.int32, values.shape, 1), 2) == 0
    return jnp.where(even, pltpu.roll(values, count - 1, 1), pltpu.roll(values, 1, 1))


def turn_tables(req, size_ref, offset_ref, q_gain_ref, k_gain_ref, turn_ref, mask_ref):
    _, count, head = turn_ref.shape
    token = lax.broadcasted_iota(jnp.int32, (count, 1), 0)
    pos_h = lax.rem(token, 4) // 2
    pos_w = (token // 4) * 2 + lax.rem(token, 2)
    lane = lax.broadcasted_iota(jnp.int32, (count, head), 1)
    pair = lane // 2
    time_half = head // 16
    axis_dim = (head - head // 8) // 2
    half = axis_dim // 2
    in_h = (pair >= time_half) & (pair < time_half + half)
    index = jnp.where(in_h, pair - time_half, pair - time_half - half).astype(f32)
    frequency = jnp.exp(index * f32(-2.0 * math.log(10000.0) / axis_dim))
    spot = jnp.where(in_h, pos_h + offset_ref[0, req], pos_w + offset_ref[1, req]).astype(f32)
    angle = jnp.where(pair < time_half, 0.0, spot * frequency)
    cosine = jnp.cos(angle)
    sine = jnp.sin(angle)
    sine = jnp.where(lax.rem(lane, 2) == 0, -sine, sine)
    for i, gain_ref in enumerate((q_gain_ref, k_gain_ref)):
        gain = jnp.broadcast_to(gain_ref[...], (count, head))
        turn_ref[2 * i] = gain * cosine
        turn_ref[2 * i + 1] = swap_pairs(gain) * sine
    key = lax.broadcasted_iota(jnp.int32, (count, count), 1)
    live = (lax.rem(key, 4) // 2 < size_ref[0, req]) & ((key // 4) * 2 + lax.rem(key, 2) < size_ref[1, req])
    mask_ref[...] = jnp.where(live, 1.0, 0.0)


def opening_kernel(
    states_hbm, k_hbm, v_hbm, mod_hbm, size_hbm, offset_hbm, q_gain_hbm, k_gain_hbm,
    spread_ref, given_ref, mod_ref, turn_ref, mask_ref, size_ref, offset_ref, q_gain_ref, k_gain_ref, sems,
):
    size = given_ref.shape[2]
    start = (1 - lax.rem(lax.axis_index("row"), 2)) * size
    part = pl.ds(pl.multiple_of(start, size), size)
    states_copy, *text_copies = start_copies(
        [
            (states_hbm, spread_ref.at[0]),
            (k_hbm.at[:, part], given_ref.at[0]),
            (v_hbm.at[:, part], given_ref.at[1]),
            (mod_hbm, mod_ref),
            (size_hbm, size_ref),
            (offset_hbm, offset_ref),
            (q_gain_hbm, q_gain_ref),
            (k_gain_hbm, k_gain_ref),
        ],
        sems,
    )
    states_copy.wait()
    states = spread_ref[0]
    for r in range(1, spread_ref.shape[0]):
        spread_ref[r] = states
    for copy in text_copies:
        copy.wait()
    turn_tables(lax.axis_index("row") // 2, size_ref, offset_ref, q_gain_ref, k_gain_ref, turn_ref, mask_ref)


def attention_kernel(
    rows_ref, text_ref, other_ref, turn_ref, mask_ref, w_hbm, out_ref, w_ref, q_ref, k_ref, v_ref, sems
):
    (w_copy,) = start_copies([(w_hbm, w_ref)], sems)
    group = 2 * lax.axis_index("col") + lax.rem(lax.axis_index("row"), 2)
    count, width = q_ref.shape
    head = turn_ref.shape[2]
    for which, ref in enumerate((q_ref, k_ref, v_ref)):
        source = (8 * which + group) // 3
        for s in range(4):
            ref[4 * s : 4 * s + 4, :] = rows_ref[s, source].astype(f32)

    def turned(values, which):
        values = values * lax.rsqrt(lane_mean(values * values) + eps_norm)
        return (values * turn_ref[2 * which] + swap_pairs(values) * turn_ref[2 * which + 1]).astype(bf16)

    key_ok = mask_ref[...] > 0.0
    contract = (((1,), (1,)), ((), ()))
    scale = head ** (-0.5)
    for h in range(width // head):
        cols = slice(h * head, (h + 1) * head)
        q = turned(q_ref[:, cols], 0)
        k = turned(k_ref[:, cols], 1)
        v = v_ref[:, cols].astype(bf16)
        s_own = lax.dot_general(q, text_ref[0, :, cols], contract, preferred_element_type=f32) * scale
        s_other = lax.dot_general(q, other_ref[0, :, cols], contract, preferred_element_type=f32) * scale
        s_image = lax.dot_general(q, k, contract, preferred_element_type=f32) * scale
        s_image = jnp.where(key_ok, s_image, mask_floor)
        top = jnp.maximum(
            jnp.max(jnp.maximum(s_own, s_other), -1, keepdims=True), jnp.max(s_image, -1, keepdims=True)
        )
        w_own = jnp.exp(s_own - top)
        w_other = jnp.exp(s_other - top)
        w_image = jnp.where(key_ok, jnp.exp(s_image - top), 0.0)
        total = jnp.sum(w_own + w_other, -1, keepdims=True) + jnp.sum(w_image, -1, keepdims=True)
        summed = (
            jnp.dot(w_own.astype(bf16), text_ref[1, :, cols], preferred_element_type=f32)
            + jnp.dot(w_other.astype(bf16), other_ref[1, :, cols], preferred_element_type=f32)
            + jnp.dot(w_image.astype(bf16), v, preferred_element_type=f32)
        )
        mixed = (summed / total).astype(bf16)
        for s in range(4):
            for r in range(8):
                out_ref[8 * s + r, :, cols] = mixed[4 * s : 4 * s + 4, :]
    w_copy.wait()


def out_kernel(mixed_ref, states_ref, gate_ref, w0_ref, w1_ref, w2_ref, w3_ref, out_ref, rows_ref):
    col = lax.axis_index("col")
    depth = w0_ref.shape[0]
    piece = mixed_ref.shape[2]
    for r in range(8):
        for s in range(4):
            at = (2 * s + r % 2) * piece
            rows_ref[4 * (r // 2) : 4 * (r // 2) + 4, at : at + piece] = mixed_ref[8 * s + r].astype(f32)
    attended = 0.0
    for d, w_ref in enumerate((w0_ref, w1_ref, w2_ref, w3_ref)):
        at = pl.multiple_of(jnp.bitwise_xor(col, d) * depth, depth)
        share = rows_ref[:, pl.ds(at, depth)].astype(bf16)
        attended = attended + jnp.dot(share, w_ref[...], preferred_element_type=f32)
    first = (states_ref[...] + gate_ref[...] * attended).astype(bf16)
    for r in range(8):
        out_ref[r] = first


def mlp_kernel(
    step_hbm, size_hbm, first_ref, mod_ref, w1_ref, w2a_ref, w2_hbm, final_hbm, out_ref, own_ref, final_ref, last_ref,
    live_ref, step_ref, size_ref, rows_ref, w2b_ref, w2c_ref, sems,
):
    row = lax.axis_index("row")
    depth = rows_ref.shape[1]
    piece = first_ref.shape[2]
    step_copy, size_copy, *w_copies = start_copies(
        [
            (step_hbm, step_ref),
            (size_hbm, size_ref),
            (part_rows(w2_hbm, 1), w2b_ref),
            (part_rows(w2_hbm, 2), w2c_ref),
            (final_hbm, final_ref),
        ],
        sems,
    )
    for r in range(8):
        rows_ref[:, r * piece : (r + 1) * piece] = first_ref[r].astype(f32)
    normed = norm_rows(rows_ref[...])
    step_copy.wait()
    size_copy.wait()
    shift = per_request(mod_ref, step_ref, 3, 4, 0, depth)
    scale = per_request(mod_ref, step_ref, 4, 4, 0, depth)
    normed = (normed * (1.0 + scale) + shift).astype(bf16)
    own = rows_ref[0:2, :]
    for q in range(REQ):
        for g in range(2):
            own = jnp.where(row == REQ * g + q, rows_ref[4 * q + 2 * g : 4 * q + 2 * g + 2, :], own)
    own_ref[...] = own
    req = lax.rem(row, REQ)
    last_ref[...] = mod_ref[step_ref[req], 6:8, :]
    grid_col = lax.axis_index("col") * live_ref.shape[0] + lax.broadcasted_iota(jnp.int32, live_ref.shape, 0)
    live = (row // REQ < size_ref[0, req]) & (grid_col < size_ref[1, req])
    live_ref[...] = jnp.where(live, 1.0, 0.0)
    hidden = jax.nn.gelu(
        jnp.dot(normed, w1_ref[...], preferred_element_type=f32), approximate=True
    ).astype(bf16)
    size = w2a_ref.shape[0]
    added = 0.0
    for i, w_ref in enumerate((w2a_ref, w2b_ref, w2c_ref)):
        if i > 0:
            w_copies[i - 1].wait()
        added = added + jnp.dot(hidden[:, i * size : (i + 1) * size], w_ref[...], preferred_element_type=f32)
    gate = per_request(mod_ref, step_ref, 5, 4, 0, depth)
    term = (gate * added).astype(out_ref.dtype)
    for q in range(REQ):
        for g in range(2):
            out_ref[REQ * g + q] = term[4 * q + 2 * g : 4 * q + 2 * g + 2, :]
    w_copies[2].wait()


def final_kernel(terms_ref, first_ref, last_ref, w_ref, live_ref, out_ref):
    second = first_ref[...]
    for r in range(8):
        second = second + terms_ref[r].astype(f32)
    normed = (norm_rows(second) * (1.0 + last_ref[1:2, :]) + last_ref[0:1, :]).astype(bf16)
    raw = lax.dot_general(normed, w_ref[...], (((1,), (1,)), ((), ())), preferred_element_type=f32)
    out_ref[...] = jnp.where(live_ref[...] > 0.0, raw, 0.0)


def blend_kernel(masked_ref, live_ref, near_ref, far_ref, latent_ref, velocity_ref, next_ref):
    col = lax.axis_index("col")
    masked = masked_ref[...]
    near = near_ref[...]
    far = jnp.where((col == 1) | (col == 2), far_ref[...], 0.0)
    odd = lax.rem(col, 2) == 1
    count = masked.shape[0]
    left = jnp.concatenate([jnp.where(odd, near, far)[count - 1 :, :], masked[: count - 1, :]], 0)
    right = jnp.concatenate([masked[1:, :], jnp.where(odd, far, near)[:1, :]], 0)
    velocity = jnp.where(live_ref[...] > 0.0, masked + blend * (left + right - 2.0 * masked), 0.0)
    velocity_ref[...] = velocity
    next_ref[...] = latent_ref[...] + -1.0 / STEPS * velocity


def call(kernel, outs, specs, scratch=(), limit=8 << 20):
    return pl.pallas_call(
        kernel,
        out_shape=tuple(jax.ShapeDtypeStruct(shape, dtype) for shape, dtype in outs),
        in_specs=specs,
        out_specs=(VMEM_SPEC,) * len(outs),
        scratch_shapes=list(scratch),
        compiler_params=pltpu.CompilerParams(vmem_limit_bytes=limit),
    )


def exchange(values, axes):
    return lax.all_to_all(values, axes, split_axis=0, concat_axis=0, tiled=True)


def compact_on_device(
    image_states, latent, text_keys, text_values, mod_table, timestep, grid_size, rope_offset,
    w_qkv, q_gain, k_gain, w_out, w_fc1, w_fc2, w_final,
):
    rows = lax.axis_size("row")
    cols = lax.axis_size("col")
    stay = lambda values: pltpu.with_memory_space_constraint(values, pltpu.HBM)
    tile_w, width = image_states.shape
    head = q_gain.shape[0]
    piece = width // 8
    tokens = rows * tile_w
    both = ("col", "row")

    near = [(i, i ^ 1) for i in range(cols)]
    steps = stay(timestep)
    sizes = stay(grid_size.T)
    fc2 = stay(w_fc2)
    sems = lambda count: pltpu.SemaphoreType.DMA((count,))
    steps_space = pltpu.SMEM(timestep.shape, jnp.int32)
    sizes_space = pltpu.SMEM(grid_size.shape[::-1], jnp.int32)
    gain_space = pltpu.VMEM((1, head), f32)
    fc2_part = ((w_fc2.shape[0] // FC_PARTS, width), bf16)

    spread, given, mods, turn, mask = call(
        opening_kernel,
        [
            ((rows, tile_w, width), bf16),
            ((2, text_keys.shape[0], piece), bf16),
            (mod_table.shape, f32),
            ((4, tokens, head), f32),
            ((tokens, tokens), f32),
        ],
        [HBM_SPEC] * 8,
        [sizes_space, sizes_space, gain_space, gain_space, sems(8)],
    )(
        stay(image_states), stay(text_keys), stay(text_values), stay(mod_table), sizes, stay(rope_offset.T),
        stay(q_gain.reshape(1, head)), stay(k_gain.reshape(1, head)),
    )
    other = lax.ppermute(given, "row", [(i, i ^ 1) for i in range(rows)])
    w_x = lax.ppermute(w_out, "col", [(i, i ^ 2) for i in range(cols)])
    w_k = lax.ppermute(w_out, "col", near)
    gathered = exchange(spread, "row")
    half_rows = text_keys.shape[0]
    pieces, fc2_a, text, states, gate = call(
        qkv_kernel,
        [
            ((rows * cols, 4, piece), bf16),
            fc2_part,
            ((2, half_rows, piece), bf16),
            ((tokens, piece), f32),
            ((tokens, piece), f32),
        ],
        [HBM_SPEC] + [VMEM_SPEC] * 3 + [HBM_SPEC] * 3,
        [
            steps_space,
            pltpu.VMEM((tokens, width), f32),
            sems(4),
        ],
    )(
        steps, gathered, mods, lax.ppermute(w_qkv, "col", near), fc2, stay(text_keys), stay(text_values),
    )
    pieces, other, w_k = lax.optimization_barrier((pieces, other, w_k))
    got = exchange(pieces, both).reshape(cols, rows, 4, piece)
    mixed, w_own = call(
        attention_kernel,
        [((rows * cols, 4, piece), bf16), (w_out.shape, bf16)],
        [VMEM_SPEC] * 5 + [HBM_SPEC],
        [pltpu.VMEM((tokens, piece), f32)] * 3 + [sems(1)],
    )(got, text, other, turn, mask, stay(w_out))
    mixed, w_x = lax.optimization_barrier((mixed, w_x))
    w_xk = lax.ppermute(w_x, "col", near)
    all_mixed = exchange(mixed, both)
    (first,) = call(
        out_kernel, [((rows, tokens, piece), bf16)], [VMEM_SPEC] * 7, [pltpu.VMEM((tokens, width), f32)]
    )(all_mixed, states, gate, w_own, w_k, w_x, w_xk)
    all_first = exchange(first, "row")
    terms, first_own, final_here, last, live = call(
        mlp_kernel,
        [
            ((rows, tile_w, width), bf16),
            ((tile_w, width), f32),
            (w_final.shape[::-1], bf16),
            ((2, width), f32),
            (latent.shape, f32),
        ],
        [HBM_SPEC, HBM_SPEC] + [VMEM_SPEC] * 4 + [HBM_SPEC, HBM_SPEC],
        [steps_space, sizes_space, pltpu.VMEM((tokens, width), f32)]
        + [pltpu.VMEM(*fc2_part)] * 2
        + [sems(5)],
        limit=16 << 20,
    )(steps, sizes, all_first, mods, w_fc1, fc2_a, fc2, stay(w_final.T))
    all_terms = exchange(terms, "row")
    (masked,) = call(final_kernel, [(latent.shape, f32)], [VMEM_SPEC] * 5)(all_terms, first_own, last, final_here, live)
    beside = lax.ppermute(masked, "col", near)
    across = lax.ppermute(masked, "col", [(i, i ^ 3) for i in range(cols)])
    return call(blend_kernel, [(latent.shape, f32)] * 2, [VMEM_SPEC] * 5)(masked, live, beside, across, latent)


def solution(mesh):
    placed = (
        P(("row", "col"), None),
        P(("row", "col"), None),
        P("row", "col"),
        P("row", "col"),
        P(),
        P(),
        P(),
        P(),
        P(None, "row"),
        P(),
        P(),
        P("col", "row"),
        P(None, "row"),
        P("row", None),
        P(),
    )
    compact = mesh.shape["row"] == 2 * REQ and mesh.shape["col"] == 4
    return jax.shard_map(
        compact_on_device if compact else on_device,
        mesh=mesh,
        in_specs=placed,
        out_specs=(P(("row", "col"), None), P(("row", "col"), None)),
        check_vma=False,
    )
```

```python
import math

import jax
import jax.numpy as jnp
from jax import lax
from jax.experimental import pallas as pl
from jax.experimental.pallas import tpu as pltpu
from jax.sharding import PartitionSpec as P

REQ = 4
TXT = 256
STEPS = 4


eps_norm = 1e-06
blend = 0.25
mask_floor = -1e30


def with_halo(cells, sides, width):
    for axis, dim in sides:
        count = lax.axis_size(axis)
        ends = count - 1
        head = lax.slice_in_dim(cells, 0, width, axis=dim)
        tail = lax.slice_in_dim(cells, cells.shape[dim] - width, cells.shape[dim], axis=dim)
        cells = jnp.concatenate(
            [
                lax.ppermute(tail, axis, [(i, (i + 1) % count) for i in range(ends)]),
                cells,
                lax.ppermute(head, axis, [((i + 1) % count, i) for i in range(ends)]),
            ],
            axis=dim,
        )
    return cells


def layer_norm(values):
    mean_value = jnp.mean(values, -1, keepdims=True)
    centred = values - mean_value
    return centred * lax.rsqrt(jnp.mean(centred * centred, -1, keepdims=True) + eps_norm)


def modulate(values, shift_vec, scale_vec):
    return (layer_norm(values) * (1.0 + scale_vec) + shift_vec).astype(jnp.bfloat16)


def rope_tables(pos_h, pos_w, head_size):
    time_half = head_size // 16
    axis_dim = (head_size - head_size // 8) // 2
    freq_index = jnp.arange(axis_dim // 2, dtype=jnp.float32)
    frequency = 10000.0 ** (-2.0 * freq_index / axis_dim)
    angles = jnp.concatenate(
        [
            jnp.zeros((pos_h.shape[0], time_half), jnp.float32),
            pos_h[:, None] * frequency[None, :],
            pos_w[:, None] * frequency[None, :],
        ],
        1,
    )
    return (jnp.cos(angles), jnp.sin(angles))


def norm_rope(values, gain_vec, cosine_table, sine_table, head_count, head_size):
    row_total = values.shape[0]
    per_head = values.astype(jnp.float32).reshape(row_total, head_count, head_size)
    per_head = (
        per_head * lax.rsqrt(jnp.mean(per_head * per_head, -1, keepdims=True) + eps_norm) * gain_vec
    )
    paired = per_head.reshape(row_total, head_count, head_size // 2, 2)
    even_part = paired[..., 0]
    odd_part = paired[..., 1]
    cos_wide = cosine_table[:, None, :]
    sin_wide = sine_table[:, None, :]
    turned = jnp.stack(
        [even_part * cos_wide - odd_part * sin_wide, even_part * sin_wide + odd_part * cos_wide], -1
    )
    return turned.reshape(row_total, head_count * head_size).astype(jnp.bfloat16)


def on_device(
    image_states,
    latent,
    text_keys,
    text_values,
    mod_table,
    timestep,
    grid_size,
    rope_offset,
    w_qkv,
    q_gain,
    k_gain,
    w_out,
    w_fc1,
    w_fc2,
    w_final,
):
    col_total = lax.axis_size("col")
    row_pos = lax.axis_index("row")
    col_pos = lax.axis_index("col")
    tile_w = image_states.shape[0]
    width = image_states.shape[1]
    head_size = q_gain.shape[0]
    head_count = width // head_size
    local_heads = head_count // col_total
    request = row_pos % REQ
    grid_row = row_pos // REQ
    grid_col = col_pos * tile_w + jnp.arange(tile_w, dtype=jnp.int32)
    req_slots = jnp.arange(REQ, dtype=jnp.int32)
    req_onehot = req_slots == request
    limits = jnp.sum(jnp.where(req_onehot[:, None], grid_size, 0), 0)
    offsets = jnp.sum(jnp.where(req_onehot[:, None], rope_offset, 0), 0)
    step_now = jnp.sum(jnp.where(req_onehot, timestep, 0))
    token_ok = (grid_row < limits[0]) & (grid_col < limits[1])
    modulation = lax.dynamic_index_in_dim(mod_table, step_now, 0, keepdims=False)
    states = image_states.astype(jnp.float32)
    normed = modulate(states, modulation[0], modulation[1])
    joined_cols = jnp.dot(
        lax.all_gather(normed, "row", axis=0, tiled=True), w_qkv, preferred_element_type=jnp.float32
    ).astype(jnp.bfloat16)
    joined = lax.all_to_all(joined_cols, "row", split_axis=0, concat_axis=1, tiled=True)
    pos_h = jnp.zeros((tile_w,), jnp.float32) + (grid_row + offsets[0]).astype(jnp.float32)
    pos_w = (grid_col + offsets[1]).astype(jnp.float32)
    cosine_table, sine_table = rope_tables(pos_h, pos_w, head_size)
    queries = norm_rope(joined[:, :width], q_gain, cosine_table, sine_table, head_count, head_size)
    image_keys = norm_rope(
        joined[:, width : 2 * width], k_gain, cosine_table, sine_table, head_count, head_size
    )
    q_heads, k_heads, v_heads = (
        lax.all_to_all(queries, "col", split_axis=1, concat_axis=0, tiled=True),
        lax.all_to_all(image_keys, "col", split_axis=1, concat_axis=0, tiled=True),
        lax.all_to_all(joined[:, 2 * width :], "col", split_axis=1, concat_axis=0, tiled=True),
    )
    image_rows = k_heads.shape[0]
    text_rows = text_keys.shape[0]
    shard_rows = image_rows + text_rows
    q_block = q_heads.reshape(image_rows, local_heads, head_size)
    key_rows = jnp.concatenate([k_heads, text_keys], 0)
    value_rows = jnp.concatenate([v_heads, text_values], 0)
    run_max = jnp.full((image_rows, local_heads), mask_floor, jnp.float32)
    key_piece = lax.all_gather(key_rows, "row", axis=0, tiled=True)
    value_piece = lax.all_gather(value_rows, "row", axis=0, tiled=True)
    piece_rows = key_piece.shape[0]
    global_row = jnp.arange(piece_rows, dtype=jnp.int32)
    shard_id = global_row // shard_rows
    within = global_row % shard_rows
    is_image = within < image_rows
    source_col = within // tile_w
    source_cell = within % tile_w
    image_req = shard_id % REQ
    text_req = (shard_id * text_rows + within - image_rows) // TXT
    key_req = jnp.where(is_image, image_req, text_req)
    key_onehot = key_req[:, None] == req_slots[None, :]
    key_height = jnp.sum(jnp.where(key_onehot, grid_size[:, 0][None, :], 0), 1)
    key_width = jnp.sum(jnp.where(key_onehot, grid_size[:, 1][None, :], 0), 1)
    image_ok = (shard_id // REQ < key_height) & (source_col * tile_w + source_cell < key_width)
    key_ok = (key_req == request) & (jnp.logical_not(is_image) | image_ok)
    scores = jnp.einsum(
        "qhd,khd->qhk",
        q_block,
        key_piece.reshape(piece_rows, local_heads, head_size),
        preferred_element_type=jnp.float32,
    ) * head_size ** (-0.5)
    new_max = jnp.maximum(run_max, jnp.max(jnp.where(key_ok, scores, mask_floor), -1))
    weights = jnp.where(key_ok, jnp.exp(scores - new_max[..., None]), 0.0)
    new_sum = jnp.sum(weights, -1)
    new_acc = jnp.einsum(
        "qhk,khd->qhd",
        weights.astype(jnp.bfloat16),
        value_piece.reshape(piece_rows, local_heads, head_size),
        preferred_element_type=jnp.float32,
    )
    mixed = (
        (new_acc / new_sum[..., None])
        .astype(jnp.bfloat16)
        .reshape(image_rows, local_heads * head_size)
    )
    partial_out = jnp.dot(
        mixed, lax.all_gather(w_out, "row", axis=1, tiled=True), preferred_element_type=jnp.float32
    )
    attended = lax.psum_scatter(
        partial_out.astype(jnp.bfloat16), "col", scatter_dimension=0, tiled=True
    ).astype(jnp.float32)
    first_res = (states + modulation[2] * attended).astype(jnp.bfloat16)
    normed_two = modulate(first_res.astype(jnp.float32), modulation[3], modulation[4])
    all_rows = lax.all_gather(normed_two, "row", axis=0, tiled=True)
    hidden = jax.nn.gelu(
        jnp.dot(all_rows, w_fc1, preferred_element_type=jnp.float32), approximate=True
    ).astype(jnp.bfloat16)
    every_term = jnp.dot(hidden, w_fc2, preferred_element_type=jnp.float32)
    every_sum = lax.psum(every_term, "row")
    mlp_out = lax.dynamic_slice_in_dim(every_sum, row_pos * tile_w, tile_w, 0)
    second_res = first_res.astype(jnp.float32) + modulation[5] * mlp_out
    normed_three = modulate(second_res, modulation[6], modulation[7])
    raw_velocity = jnp.dot(normed_three, w_final, preferred_element_type=jnp.float32)
    masked = jnp.where(token_ok[:, None], raw_velocity, 0.0)
    padded = with_halo(masked, (("col", 0),), 1)
    left_side = padded[:-2]
    right_side = padded[2:]
    velocity = jnp.where(
        token_ok[:, None], masked + blend * (left_side + right_side - 2.0 * masked), 0.0
    )
    next_latent = latent + -1.0 / STEPS * velocity
    return (velocity, next_latent)


bf16 = jnp.bfloat16
FC_PARTS = 3
f32 = jnp.float32
VMEM_SPEC = pl.BlockSpec(memory_space=pltpu.VMEM)
HBM_SPEC = pl.BlockSpec(memory_space=pltpu.HBM)


def start_copies(pairs, sems):
    copies = [pltpu.make_async_copy(source, target, sems.at[i]) for i, (source, target) in enumerate(pairs)]
    for copy in copies:
        copy.start()
    return copies


def part_rows(hbm, index):
    size = hbm.shape[0] // FC_PARTS
    return hbm.at[pl.ds(index * size, size), :]


def lane_mean(values):
    return jnp.mean(values, -1, keepdims=True)


def norm_rows(values):
    centred = values - lane_mean(values)
    return centred * lax.rsqrt(lane_mean(centred * centred) + eps_norm)


def per_request(mod_ref, step_ref, slot, rows_each, start, size):
    shape = (REQ * rows_each, size)
    row = lax.broadcasted_iota(jnp.int32, shape, 0) // rows_each
    whole = None
    for q in range(REQ):
        vector = jnp.broadcast_to(mod_ref[step_ref[q], pl.ds(slot, 1), pl.ds(start, size)], shape)
        whole = vector if whole is None else jnp.where(row == q, vector, whole)
    return whole


def qkv_kernel(
    step_hbm, tokens_ref, mod_ref, w_ref, fc2_hbm, text_k_hbm, text_v_hbm, out_ref, fc2_ref, text_ref, states_ref, gate_ref,
    step_ref, order_ref, sems,
):
    row = lax.axis_index("row")
    depth = order_ref.shape[1]
    size = out_ref.shape[2]
    here = pl.ds(pl.multiple_of(lax.rem(row, 2) * size, size), size)
    copies = start_copies(
        [
            (step_hbm, step_ref),
            (text_k_hbm.at[:, here], text_ref.at[0]),
            (text_v_hbm.at[:, here], text_ref.at[1]),
            (part_rows(fc2_hbm, 0), fc2_ref),
        ],
        sems,
    )
    for q in range(REQ):
        for g in range(2):
            order_ref[4 * q + 2 * g : 4 * q + 2 * g + 2, :] = tokens_ref[REQ * g + q].astype(f32)
    out_ref[...] = jnp.zeros_like(out_ref)
    normed = norm_rows(order_ref[...])
    for copy in copies[:1]:
        copy.wait()
    shift = per_request(mod_ref, step_ref, 0, 4, 0, depth)
    scale = per_request(mod_ref, step_ref, 1, 4, 0, depth)
    normed = (normed * (1.0 + scale) + shift).astype(bf16)
    whole = jnp.dot(normed, w_ref[...], preferred_element_type=f32).astype(bf16)
    start = pl.multiple_of(row * size, size)
    states_ref[...] = order_ref[:, pl.ds(start, size)]
    gate_ref[...] = per_request(mod_ref, step_ref, 2, 4, start, size)
    for piece in range(w_ref.shape[1] // size):
        group = lax.rem(row * 3 + piece, 8)
        place = (group // 2) * 8 + lax.rem(group, 2)
        for q in range(REQ):
            out_ref[2 * q + place] = whole[4 * q : 4 * q + 4, piece * size : (piece + 1) * size]
    for copy in copies[1:]:
        copy.wait()


def swap_pairs(values):
    count = values.shape[-1]
    even = lax.rem(lax.broadcasted_iota(jnp.int32, values.shape, 1), 2) == 0
    return jnp.where(even, pltpu.roll(values, count - 1, 1), pltpu.roll(values, 1, 1))


def turn_tables(req, size_ref, offset_ref, q_gain_ref, k_gain_ref, turn_ref, mask_ref):
    _, count, head = turn_ref.shape
    token = lax.broadcasted_iota(jnp.int32, (count, 1), 0)
    pos_h = lax.rem(token, 4) // 2
    pos_w = (token // 4) * 2 + lax.rem(token, 2)
    lane = lax.broadcasted_iota(jnp.int32, (count, head), 1)
    pair = lane // 2
    time_half = head // 16
    axis_dim = (head - head // 8) // 2
    half = axis_dim // 2
    in_h = (pair >= time_half) & (pair < time_half + half)
    index = jnp.where(in_h, pair - time_half, pair - time_half - half).astype(f32)
    frequency = jnp.exp(index * f32(-2.0 * math.log(10000.0) / axis_dim))
    spot = jnp.where(in_h, pos_h + offset_ref[0, req], pos_w + offset_ref[1, req]).astype(f32)
    angle = jnp.where(pair < time_half, 0.0, spot * frequency)
    cosine = jnp.cos(angle)
    sine = jnp.sin(angle)
    sine = jnp.where(lax.rem(lane, 2) == 0, -sine, sine)
    for i, gain_ref in enumerate((q_gain_ref, k_gain_ref)):
        gain = jnp.broadcast_to(gain_ref[...], (count, head))
        turn_ref[2 * i] = gain * cosine
        turn_ref[2 * i + 1] = swap_pairs(gain) * sine
    key = lax.broadcasted_iota(jnp.int32, (count, count), 1)
    live = (lax.rem(key, 4) // 2 < size_ref[0, req]) & ((key // 4) * 2 + lax.rem(key, 2) < size_ref[1, req])
    mask_ref[...] = jnp.where(live, 1.0, 0.0)


def opening_kernel(
    states_hbm, k_hbm, v_hbm, mod_hbm, size_hbm, offset_hbm, q_gain_hbm, k_gain_hbm,
    spread_ref, given_ref, mod_ref, turn_ref, mask_ref, size_ref, offset_ref, q_gain_ref, k_gain_ref, sems,
):
    size = given_ref.shape[2]
    start = (1 - lax.rem(lax.axis_index("row"), 2)) * size
    part = pl.ds(pl.multiple_of(start, size), size)
    states_copy, *text_copies = start_copies(
        [
            (states_hbm, spread_ref.at[0]),
            (k_hbm.at[:, part], given_ref.at[0]),
            (v_hbm.at[:, part], given_ref.at[1]),
            (mod_hbm, mod_ref),
            (size_hbm, size_ref),
            (offset_hbm, offset_ref),
            (q_gain_hbm, q_gain_ref),
            (k_gain_hbm, k_gain_ref),
        ],
        sems,
    )
    states_copy.wait()
    states = spread_ref[0]
    for r in range(1, spread_ref.shape[0]):
        spread_ref[r] = states
    for copy in text_copies[3:]:
        copy.wait()
    turn_tables(lax.axis_index("row") // 2, size_ref, offset_ref, q_gain_ref, k_gain_ref, turn_ref, mask_ref)
    for copy in text_copies[:3]:
        copy.wait()


def attention_kernel(
    rows_ref, text_ref, other_ref, turn_ref, mask_ref, w_hbm, out_ref, w_ref, q_ref, k_ref, v_ref, sems
):
    (w_copy,) = start_copies([(w_hbm, w_ref)], sems)
    group = 2 * lax.axis_index("col") + lax.rem(lax.axis_index("row"), 2)
    count, width = q_ref.shape
    head = turn_ref.shape[2]
    for which, ref in enumerate((q_ref, k_ref, v_ref)):
        source = (8 * which + group) // 3
        for s in range(4):
            ref[4 * s : 4 * s + 4, :] = rows_ref[s, source].astype(f32)

    def turned(values, which):
        values = values * lax.rsqrt(lane_mean(values * values) + eps_norm)
        return (values * turn_ref[2 * which] + swap_pairs(values) * turn_ref[2 * which + 1]).astype(bf16)

    key_ok = mask_ref[...] > 0.0
    contract = (((1,), (1,)), ((), ()))
    scale = head ** (-0.5)
    for h in range(width // head):
        cols = slice(h * head, (h + 1) * head)
        q = turned(q_ref[:, cols], 0)
        k = turned(k_ref[:, cols], 1)
        v = v_ref[:, cols].astype(bf16)
        s_own = lax.dot_general(q, text_ref[0, :, cols], contract, preferred_element_type=f32) * scale
        s_other = lax.dot_general(q, other_ref[0, :, cols], contract, preferred_element_type=f32) * scale
        s_image = lax.dot_general(q, k, contract, preferred_element_type=f32) * scale
        s_image = jnp.where(key_ok, s_image, mask_floor)
        top = jnp.maximum(
            jnp.max(jnp.maximum(s_own, s_other), -1, keepdims=True), jnp.max(s_image, -1, keepdims=True)
        )
        w_own = jnp.exp(s_own - top)
        w_other = jnp.exp(s_other - top)
        w_image = jnp.where(key_ok, jnp.exp(s_image - top), 0.0)
        total = jnp.sum(w_own + w_other, -1, keepdims=True) + jnp.sum(w_image, -1, keepdims=True)
        summed = (
            jnp.dot(w_own.astype(bf16), text_ref[1, :, cols], preferred_element_type=f32)
            + jnp.dot(w_other.astype(bf16), other_ref[1, :, cols], preferred_element_type=f32)
            + jnp.dot(w_image.astype(bf16), v, preferred_element_type=f32)
        )
        mixed = (summed / total).astype(bf16)
        for s in range(4):
            for r in range(8):
                out_ref[8 * s + r, :, cols] = mixed[4 * s : 4 * s + 4, :]
    w_copy.wait()


def out_kernel(mixed_ref, states_ref, gate_ref, w0_ref, w1_ref, w2_ref, w3_ref, out_ref, rows_ref):
    col = lax.axis_index("col")
    depth = w0_ref.shape[0]
    piece = mixed_ref.shape[2]
    for r in range(8):
        for s in range(4):
            at = (2 * s + r % 2) * piece
            rows_ref[4 * (r // 2) : 4 * (r // 2) + 4, at : at + piece] = mixed_ref[8 * s + r].astype(f32)
    attended = 0.0
    for d, w_ref in enumerate((w0_ref, w1_ref, w2_ref, w3_ref)):
        at = pl.multiple_of(jnp.bitwise_xor(col, d) * depth, depth)
        share = rows_ref[:, pl.ds(at, depth)].astype(bf16)
        attended = attended + jnp.dot(share, w_ref[...], preferred_element_type=f32)
    first = (states_ref[...] + gate_ref[...] * attended).astype(bf16)
    for r in range(8):
        out_ref[r] = first


def mlp_kernel(
    step_hbm, size_hbm, first_ref, mod_ref, w1_ref, w2a_ref, w2_hbm, final_hbm, out_ref, own_ref, final_ref, last_ref,
    live_ref, step_ref, size_ref, rows_ref, w2b_ref, w2c_ref, sems,
):
    row = lax.axis_index("row")
    depth = rows_ref.shape[1]
    piece = first_ref.shape[2]
    step_copy, size_copy, *w_copies = start_copies(
        [
            (step_hbm, step_ref),
            (size_hbm, size_ref),
            (part_rows(w2_hbm, 1), w2b_ref),
            (part_rows(w2_hbm, 2), w2c_ref),
            (final_hbm, final_ref),
        ],
        sems,
    )
    for r in range(8):
        rows_ref[:, r * piece : (r + 1) * piece] = first_ref[r].astype(f32)
    normed = norm_rows(rows_ref[...])
    step_copy.wait()
    size_copy.wait()
    shift = per_request(mod_ref, step_ref, 3, 4, 0, depth)
    scale = per_request(mod_ref, step_ref, 4, 4, 0, depth)
    normed = (normed * (1.0 + scale) + shift).astype(bf16)
    own = rows_ref[0:2, :]
    for q in range(REQ):
        for g in range(2):
            own = jnp.where(row == REQ * g + q, rows_ref[4 * q + 2 * g : 4 * q + 2 * g + 2, :], own)
    own_ref[...] = own
    req = lax.rem(row, REQ)
    last_ref[...] = mod_ref[step_ref[req], 6:8, :]
    grid_col = lax.axis_index("col") * live_ref.shape[0] + lax.broadcasted_iota(jnp.int32, live_ref.shape, 0)
    live = (row // REQ < size_ref[0, req]) & (grid_col < size_ref[1, req])
    live_ref[...] = jnp.where(live, 1.0, 0.0)
    hidden = jax.nn.gelu(
        jnp.dot(normed, w1_ref[...], preferred_element_type=f32), approximate=True
    ).astype(bf16)
    size = w2a_ref.shape[0]
    added = 0.0
    for i, w_ref in enumerate((w2a_ref, w2b_ref, w2c_ref)):
        if i > 0:
            w_copies[i - 1].wait()
        added = added + jnp.dot(hidden[:, i * size : (i + 1) * size], w_ref[...], preferred_element_type=f32)
    gate = per_request(mod_ref, step_ref, 5, 4, 0, depth)
    term = (gate * added).astype(out_ref.dtype)
    for q in range(REQ):
        for g in range(2):
            out_ref[REQ * g + q] = term[4 * q + 2 * g : 4 * q + 2 * g + 2, :]
    w_copies[2].wait()


def final_kernel(terms_ref, first_ref, last_ref, w_ref, live_ref, out_ref):
    second = first_ref[...]
    for r in range(8):
        second = second + terms_ref[r].astype(f32)
    normed = (norm_rows(second) * (1.0 + last_ref[1:2, :]) + last_ref[0:1, :]).astype(bf16)
    raw = lax.dot_general(normed, w_ref[...], (((1,), (1,)), ((), ())), preferred_element_type=f32)
    out_ref[...] = jnp.where(live_ref[...] > 0.0, raw, 0.0)


def blend_kernel(masked_ref, live_ref, near_ref, far_ref, latent_ref, velocity_ref, next_ref):
    col = lax.axis_index("col")
    masked = masked_ref[...]
    near = near_ref[...]
    far = jnp.where((col == 1) | (col == 2), far_ref[...], 0.0)
    odd = lax.rem(col, 2) == 1
    count = masked.shape[0]
    left = jnp.concatenate([jnp.where(odd, near, far)[count - 1 :, :], masked[: count - 1, :]], 0)
    right = jnp.concatenate([masked[1:, :], jnp.where(odd, far, near)[:1, :]], 0)
    velocity = jnp.where(live_ref[...] > 0.0, masked + blend * (left + right - 2.0 * masked), 0.0)
    velocity_ref[...] = velocity
    next_ref[...] = latent_ref[...] + -1.0 / STEPS * velocity


def call(kernel, outs, specs, scratch=(), limit=8 << 20):
    return pl.pallas_call(
        kernel,
        out_shape=tuple(jax.ShapeDtypeStruct(shape, dtype) for shape, dtype in outs),
        in_specs=specs,
        out_specs=(VMEM_SPEC,) * len(outs),
        scratch_shapes=list(scratch),
        compiler_params=pltpu.CompilerParams(vmem_limit_bytes=limit),
    )


def exchange(values, axes):
    return lax.all_to_all(values, axes, split_axis=0, concat_axis=0, tiled=True)


def compact_on_device(
    image_states, latent, text_keys, text_values, mod_table, timestep, grid_size, rope_offset,
    w_qkv, q_gain, k_gain, w_out, w_fc1, w_fc2, w_final,
):
    rows = lax.axis_size("row")
    cols = lax.axis_size("col")
    stay = lambda values: pltpu.with_memory_space_constraint(values, pltpu.HBM)
    tile_w, width = image_states.shape
    head = q_gain.shape[0]
    piece = width // 8
    tokens = rows * tile_w
    both = ("col", "row")

    near = [(i, i ^ 1) for i in range(cols)]
    steps = stay(timestep)
    sizes = stay(grid_size.T)
    fc2 = stay(w_fc2)
    sems = lambda count: pltpu.SemaphoreType.DMA((count,))
    steps_space = pltpu.SMEM(timestep.shape, jnp.int32)
    sizes_space = pltpu.SMEM(grid_size.shape[::-1], jnp.int32)
    gain_space = pltpu.VMEM((1, head), f32)
    fc2_part = ((w_fc2.shape[0] // FC_PARTS, width), bf16)

    spread, given, mods, turn, mask = call(
        opening_kernel,
        [
            ((rows, tile_w, width), bf16),
            ((2, text_keys.shape[0], piece), bf16),
            (mod_table.shape, f32),
            ((4, tokens, head), f32),
            ((tokens, tokens), f32),
        ],
        [HBM_SPEC] * 8,
        [sizes_space, sizes_space, gain_space, gain_space, sems(8)],
    )(
        stay(image_states), stay(text_keys), stay(text_values), stay(mod_table), sizes, stay(rope_offset.T),
        stay(q_gain.reshape(1, head)), stay(k_gain.reshape(1, head)),
    )
    other = lax.ppermute(given, "row", [(i, i ^ 1) for i in range(rows)])
    w_x = lax.ppermute(w_out, "col", [(i, i ^ 2) for i in range(cols)])
    w_k = lax.ppermute(w_out, "col", near)
    gathered = exchange(spread, "row")
    half_rows = text_keys.shape[0]
    pieces, fc2_a, text, states, gate = call(
        qkv_kernel,
        [
            ((rows * cols, 4, piece), bf16),
            fc2_part,
            ((2, half_rows, piece), bf16),
            ((tokens, piece), f32),
            ((tokens, piece), f32),
        ],
        [HBM_SPEC] + [VMEM_SPEC] * 3 + [HBM_SPEC] * 3,
        [
            steps_space,
            pltpu.VMEM((tokens, width), f32),
            sems(4),
        ],
    )(
        steps, gathered, mods, lax.ppermute(w_qkv, "col", near), fc2, stay(text_keys), stay(text_values),
    )
    pieces, other, w_k = lax.optimization_barrier((pieces, other, w_k))
    got = exchange(pieces, both).reshape(cols, rows, 4, piece)
    mixed, w_own = call(
        attention_kernel,
        [((rows * cols, 4, piece), bf16), (w_out.shape, bf16)],
        [VMEM_SPEC] * 5 + [HBM_SPEC],
        [pltpu.VMEM((tokens, piece), f32)] * 3 + [sems(1)],
    )(got, text, other, turn, mask, stay(w_out))
    mixed, w_x = lax.optimization_barrier((mixed, w_x))
    w_xk = lax.ppermute(w_x, "col", near)
    all_mixed = exchange(mixed, both)
    (first,) = call(
        out_kernel, [((rows, tokens, piece), bf16)], [VMEM_SPEC] * 7, [pltpu.VMEM((tokens, width), f32)]
    )(all_mixed, states, gate, w_own, w_k, w_x, w_xk)
    all_first = exchange(first, "row")
    terms, first_own, final_here, last, live = call(
        mlp_kernel,
        [
            ((rows, tile_w, width), bf16),
            ((tile_w, width), f32),
            (w_final.shape[::-1], bf16),
            ((2, width), f32),
            (latent.shape, f32),
        ],
        [HBM_SPEC, HBM_SPEC] + [VMEM_SPEC] * 4 + [HBM_SPEC, HBM_SPEC],
        [steps_space, sizes_space, pltpu.VMEM((tokens, width), f32)]
        + [pltpu.VMEM(*fc2_part)] * 2
        + [sems(5)],
        limit=16 << 20,
    )(steps, sizes, all_first, mods, w_fc1, fc2_a, fc2, stay(w_final.T))
    all_terms = exchange(terms, "row")
    (masked,) = call(final_kernel, [(latent.shape, f32)], [VMEM_SPEC] * 5)(all_terms, first_own, last, final_here, live)
    beside = lax.ppermute(masked, "col", near)
    across = lax.ppermute(masked, "col", [(i, i ^ 3) for i in range(cols)])
    return call(blend_kernel, [(latent.shape, f32)] * 2, [VMEM_SPEC] * 5)(masked, live, beside, across, latent)


def solution(mesh):
    placed = (
        P(("row", "col"), None),
        P(("row", "col"), None),
        P("row", "col"),
        P("row", "col"),
        P(),
        P(),
        P(),
        P(),
        P(None, "row"),
        P(),
        P(),
        P("col", "row"),
        P(None, "row"),
        P("row", None),
        P(),
    )
    compact = mesh.shape["row"] == 2 * REQ and mesh.shape["col"] == 4
    return jax.shard_map(
        compact_on_device if compact else on_device,
        mesh=mesh,
        in_specs=placed,
        out_specs=(P(("row", "col"), None), P(("row", "col"), None)),
        check_vma=False,
    )
```

```python
import math

import jax
import jax.numpy as jnp
from jax import lax
from jax.experimental import pallas as pl
from jax.experimental.pallas import tpu as pltpu
from jax.sharding import PartitionSpec as P

REQ = 4
TXT = 256
STEPS = 4


eps_norm = 1e-06
blend = 0.25
mask_floor = -1e30


def with_halo(cells, sides, width):
    for axis, dim in sides:
        count = lax.axis_size(axis)
        ends = count - 1
        head = lax.slice_in_dim(cells, 0, width, axis=dim)
        tail = lax.slice_in_dim(cells, cells.shape[dim] - width, cells.shape[dim], axis=dim)
        cells = jnp.concatenate(
            [
                lax.ppermute(tail, axis, [(i, (i + 1) % count) for i in range(ends)]),
                cells,
                lax.ppermute(head, axis, [((i + 1) % count, i) for i in range(ends)]),
            ],
            axis=dim,
        )
    return cells


def layer_norm(values):
    mean_value = jnp.mean(values, -1, keepdims=True)
    centred = values - mean_value
    return centred * lax.rsqrt(jnp.mean(centred * centred, -1, keepdims=True) + eps_norm)


def modulate(values, shift_vec, scale_vec):
    return (layer_norm(values) * (1.0 + scale_vec) + shift_vec).astype(jnp.bfloat16)


def rope_tables(pos_h, pos_w, head_size):
    time_half = head_size // 16
    axis_dim = (head_size - head_size // 8) // 2
    freq_index = jnp.arange(axis_dim // 2, dtype=jnp.float32)
    frequency = 10000.0 ** (-2.0 * freq_index / axis_dim)
    angles = jnp.concatenate(
        [
            jnp.zeros((pos_h.shape[0], time_half), jnp.float32),
            pos_h[:, None] * frequency[None, :],
            pos_w[:, None] * frequency[None, :],
        ],
        1,
    )
    return (jnp.cos(angles), jnp.sin(angles))


def norm_rope(values, gain_vec, cosine_table, sine_table, head_count, head_size):
    row_total = values.shape[0]
    per_head = values.astype(jnp.float32).reshape(row_total, head_count, head_size)
    per_head = (
        per_head * lax.rsqrt(jnp.mean(per_head * per_head, -1, keepdims=True) + eps_norm) * gain_vec
    )
    paired = per_head.reshape(row_total, head_count, head_size // 2, 2)
    even_part = paired[..., 0]
    odd_part = paired[..., 1]
    cos_wide = cosine_table[:, None, :]
    sin_wide = sine_table[:, None, :]
    turned = jnp.stack(
        [even_part * cos_wide - odd_part * sin_wide, even_part * sin_wide + odd_part * cos_wide], -1
    )
    return turned.reshape(row_total, head_count * head_size).astype(jnp.bfloat16)


def on_device(
    image_states,
    latent,
    text_keys,
    text_values,
    mod_table,
    timestep,
    grid_size,
    rope_offset,
    w_qkv,
    q_gain,
    k_gain,
    w_out,
    w_fc1,
    w_fc2,
    w_final,
):
    col_total = lax.axis_size("col")
    row_pos = lax.axis_index("row")
    col_pos = lax.axis_index("col")
    tile_w = image_states.shape[0]
    width = image_states.shape[1]
    head_size = q_gain.shape[0]
    head_count = width // head_size
    local_heads = head_count // col_total
    request = row_pos % REQ
    grid_row = row_pos // REQ
    grid_col = col_pos * tile_w + jnp.arange(tile_w, dtype=jnp.int32)
    req_slots = jnp.arange(REQ, dtype=jnp.int32)
    req_onehot = req_slots == request
    limits = jnp.sum(jnp.where(req_onehot[:, None], grid_size, 0), 0)
    offsets = jnp.sum(jnp.where(req_onehot[:, None], rope_offset, 0), 0)
    step_now = jnp.sum(jnp.where(req_onehot, timestep, 0))
    token_ok = (grid_row < limits[0]) & (grid_col < limits[1])
    modulation = lax.dynamic_index_in_dim(mod_table, step_now, 0, keepdims=False)
    states = image_states.astype(jnp.float32)
    normed = modulate(states, modulation[0], modulation[1])
    joined_cols = jnp.dot(
        lax.all_gather(normed, "row", axis=0, tiled=True), w_qkv, preferred_element_type=jnp.float32
    ).astype(jnp.bfloat16)
    joined = lax.all_to_all(joined_cols, "row", split_axis=0, concat_axis=1, tiled=True)
    pos_h = jnp.zeros((tile_w,), jnp.float32) + (grid_row + offsets[0]).astype(jnp.float32)
    pos_w = (grid_col + offsets[1]).astype(jnp.float32)
    cosine_table, sine_table = rope_tables(pos_h, pos_w, head_size)
    queries = norm_rope(joined[:, :width], q_gain, cosine_table, sine_table, head_count, head_size)
    image_keys = norm_rope(
        joined[:, width : 2 * width], k_gain, cosine_table, sine_table, head_count, head_size
    )
    q_heads, k_heads, v_heads = (
        lax.all_to_all(queries, "col", split_axis=1, concat_axis=0, tiled=True),
        lax.all_to_all(image_keys, "col", split_axis=1, concat_axis=0, tiled=True),
        lax.all_to_all(joined[:, 2 * width :], "col", split_axis=1, concat_axis=0, tiled=True),
    )
    image_rows = k_heads.shape[0]
    text_rows = text_keys.shape[0]
    shard_rows = image_rows + text_rows
    q_block = q_heads.reshape(image_rows, local_heads, head_size)
    key_rows = jnp.concatenate([k_heads, text_keys], 0)
    value_rows = jnp.concatenate([v_heads, text_values], 0)
    run_max = jnp.full((image_rows, local_heads), mask_floor, jnp.float32)
    key_piece = lax.all_gather(key_rows, "row", axis=0, tiled=True)
    value_piece = lax.all_gather(value_rows, "row", axis=0, tiled=True)
    piece_rows = key_piece.shape[0]
    global_row = jnp.arange(piece_rows, dtype=jnp.int32)
    shard_id = global_row // shard_rows
    within = global_row % shard_rows
    is_image = within < image_rows
    source_col = within // tile_w
    source_cell = within % tile_w
    image_req = shard_id % REQ
    text_req = (shard_id * text_rows + within - image_rows) // TXT
    key_req = jnp.where(is_image, image_req, text_req)
    key_onehot = key_req[:, None] == req_slots[None, :]
    key_height = jnp.sum(jnp.where(key_onehot, grid_size[:, 0][None, :], 0), 1)
    key_width = jnp.sum(jnp.where(key_onehot, grid_size[:, 1][None, :], 0), 1)
    image_ok = (shard_id // REQ < key_height) & (source_col * tile_w + source_cell < key_width)
    key_ok = (key_req == request) & (jnp.logical_not(is_image) | image_ok)
    scores = jnp.einsum(
        "qhd,khd->qhk",
        q_block,
        key_piece.reshape(piece_rows, local_heads, head_size),
        preferred_element_type=jnp.float32,
    ) * head_size ** (-0.5)
    new_max = jnp.maximum(run_max, jnp.max(jnp.where(key_ok, scores, mask_floor), -1))
    weights = jnp.where(key_ok, jnp.exp(scores - new_max[..., None]), 0.0)
    new_sum = jnp.sum(weights, -1)
    new_acc = jnp.einsum(
        "qhk,khd->qhd",
        weights.astype(jnp.bfloat16),
        value_piece.reshape(piece_rows, local_heads, head_size),
        preferred_element_type=jnp.float32,
    )
    mixed = (
        (new_acc / new_sum[..., None])
        .astype(jnp.bfloat16)
        .reshape(image_rows, local_heads * head_size)
    )
    partial_out = jnp.dot(
        mixed, lax.all_gather(w_out, "row", axis=1, tiled=True), preferred_element_type=jnp.float32
    )
    attended = lax.psum_scatter(
        partial_out.astype(jnp.bfloat16), "col", scatter_dimension=0, tiled=True
    ).astype(jnp.float32)
    first_res = (states + modulation[2] * attended).astype(jnp.bfloat16)
    normed_two = modulate(first_res.astype(jnp.float32), modulation[3], modulation[4])
    all_rows = lax.all_gather(normed_two, "row", axis=0, tiled=True)
    hidden = jax.nn.gelu(
        jnp.dot(all_rows, w_fc1, preferred_element_type=jnp.float32), approximate=True
    ).astype(jnp.bfloat16)
    every_term = jnp.dot(hidden, w_fc2, preferred_element_type=jnp.float32)
    every_sum = lax.psum(every_term, "row")
    mlp_out = lax.dynamic_slice_in_dim(every_sum, row_pos * tile_w, tile_w, 0)
    second_res = first_res.astype(jnp.float32) + modulation[5] * mlp_out
    normed_three = modulate(second_res, modulation[6], modulation[7])
    raw_velocity = jnp.dot(normed_three, w_final, preferred_element_type=jnp.float32)
    masked = jnp.where(token_ok[:, None], raw_velocity, 0.0)
    padded = with_halo(masked, (("col", 0),), 1)
    left_side = padded[:-2]
    right_side = padded[2:]
    velocity = jnp.where(
        token_ok[:, None], masked + blend * (left_side + right_side - 2.0 * masked), 0.0
    )
    next_latent = latent + -1.0 / STEPS * velocity
    return (velocity, next_latent)


bf16 = jnp.bfloat16
FC_PARTS = 3
f32 = jnp.float32
VMEM_SPEC = pl.BlockSpec(memory_space=pltpu.VMEM)
HBM_SPEC = pl.BlockSpec(memory_space=pltpu.HBM)


def start_copies(pairs, sems):
    copies = [pltpu.make_async_copy(source, target, sems.at[i]) for i, (source, target) in enumerate(pairs)]
    for copy in copies:
        copy.start()
    return copies


def part_rows(hbm, index):
    size = hbm.shape[0] // FC_PARTS
    return hbm.at[pl.ds(index * size, size), :]


def lane_mean(values):
    return jnp.mean(values, -1, keepdims=True)


def norm_rows(values):
    centred = values - lane_mean(values)
    return centred * lax.rsqrt(lane_mean(centred * centred) + eps_norm)


def per_request(mod_ref, step_ref, slot, rows_each, start, size):
    shape = (REQ * rows_each, size)
    row = lax.broadcasted_iota(jnp.int32, shape, 0) // rows_each
    whole = None
    for q in range(REQ):
        vector = jnp.broadcast_to(mod_ref[step_ref[q], pl.ds(slot, 1), pl.ds(start, size)], shape)
        whole = vector if whole is None else jnp.where(row == q, vector, whole)
    return whole


def qkv_kernel(
    step_hbm, tokens_ref, mod_ref, w_ref, fc2_hbm, text_k_hbm, text_v_hbm, out_ref, fc2_ref, text_ref, states_ref, gate_ref,
    step_ref, order_ref, sems,
):
    row = lax.axis_index("row")
    depth = order_ref.shape[1]
    size = out_ref.shape[2]
    here = pl.ds(pl.multiple_of(lax.rem(row, 2) * size, size), size)
    copies = start_copies(
        [
            (step_hbm, step_ref),
            (text_k_hbm.at[:, here], text_ref.at[0]),
            (text_v_hbm.at[:, here], text_ref.at[1]),
            (part_rows(fc2_hbm, 0), fc2_ref),
        ],
        sems,
    )
    for q in range(REQ):
        for g in range(2):
            order_ref[4 * q + 2 * g : 4 * q + 2 * g + 2, :] = tokens_ref[REQ * g + q].astype(f32)
    out_ref[...] = jnp.zeros_like(out_ref)
    normed = norm_rows(order_ref[...])
    for copy in copies[:1]:
        copy.wait()
    shift = per_request(mod_ref, step_ref, 0, 4, 0, depth)
    scale = per_request(mod_ref, step_ref, 1, 4, 0, depth)
    normed = (normed * (1.0 + scale) + shift).astype(bf16)
    whole = jnp.dot(normed, w_ref[...], preferred_element_type=f32).astype(bf16)
    start = pl.multiple_of(row * size, size)
    states_ref[...] = order_ref[:, pl.ds(start, size)]
    gate_ref[...] = per_request(mod_ref, step_ref, 2, 4, start, size)
    for piece in range(w_ref.shape[1] // size):
        group = lax.rem(row * 3 + piece, 8)
        place = (group // 2) * 8 + lax.rem(group, 2)
        for q in range(REQ):
            out_ref[2 * q + place] = whole[4 * q : 4 * q + 4, piece * size : (piece + 1) * size]
    for copy in copies[1:]:
        copy.wait()


def swap_pairs(values):
    count = values.shape[-1]
    even = lax.rem(lax.broadcasted_iota(jnp.int32, values.shape, 1), 2) == 0
    return jnp.where(even, pltpu.roll(values, count - 1, 1), pltpu.roll(values, 1, 1))


def turn_tables(req, size_ref, offset_ref, q_gain_ref, k_gain_ref, turn_ref, mask_ref):
    _, count, head = turn_ref.shape
    token = lax.broadcasted_iota(jnp.int32, (count, 1), 0)
    pos_h = lax.rem(token, 4) // 2
    pos_w = (token // 4) * 2 + lax.rem(token, 2)
    lane = lax.broadcasted_iota(jnp.int32, (count, head), 1)
    pair = lane // 2
    time_half = head // 16
    axis_dim = (head - head // 8) // 2
    half = axis_dim // 2
    in_h = (pair >= time_half) & (pair < time_half + half)
    index = jnp.where(in_h, pair - time_half, pair - time_half - half).astype(f32)
    frequency = jnp.exp(index * f32(-2.0 * math.log(10000.0) / axis_dim))
    spot = jnp.where(in_h, pos_h + offset_ref[0, req], pos_w + offset_ref[1, req]).astype(f32)
    angle = jnp.where(pair < time_half, 0.0, spot * frequency)
    cosine = jnp.cos(angle)
    sine = jnp.sin(angle)
    sine = jnp.where(lax.rem(lane, 2) == 0, -sine, sine)
    for i, gain_ref in enumerate((q_gain_ref, k_gain_ref)):
        gain = jnp.broadcast_to(gain_ref[...], (count, head))
        turn_ref[2 * i] = gain * cosine
        turn_ref[2 * i + 1] = swap_pairs(gain) * sine
    key = lax.broadcasted_iota(jnp.int32, (count, count), 1)
    live = (lax.rem(key, 4) // 2 < size_ref[0, req]) & ((key // 4) * 2 + lax.rem(key, 2) < size_ref[1, req])
    mask_ref[...] = jnp.where(live, 1.0, 0.0)


def opening_kernel(
    states_hbm, k_hbm, v_hbm, mod_hbm, size_hbm, offset_hbm, q_gain_hbm, k_gain_hbm,
    spread_ref, given_ref, mod_ref, turn_ref, mask_ref, size_ref, offset_ref, q_gain_ref, k_gain_ref, sems,
):
    size = given_ref.shape[2]
    start = (1 - lax.rem(lax.axis_index("row"), 2)) * size
    part = pl.ds(pl.multiple_of(start, size), size)
    states_copy, *text_copies = start_copies(
        [
            (states_hbm, spread_ref.at[0]),
            (size_hbm, size_ref),
            (offset_hbm, offset_ref),
            (q_gain_hbm, q_gain_ref),
            (k_gain_hbm, k_gain_ref),
            (k_hbm.at[:, part], given_ref.at[0]),
            (v_hbm.at[:, part], given_ref.at[1]),
            (mod_hbm, mod_ref),
        ],
        sems,
    )
    states_copy.wait()
    states = spread_ref[0]
    for r in range(1, spread_ref.shape[0]):
        spread_ref[r] = states
    for copy in text_copies[:4]:
        copy.wait()
    turn_tables(lax.axis_index("row") // 2, size_ref, offset_ref, q_gain_ref, k_gain_ref, turn_ref, mask_ref)
    for copy in text_copies[4:]:
        copy.wait()


def attention_kernel(
    rows_ref, text_ref, other_ref, turn_ref, mask_ref, w_hbm, out_ref, w_ref, q_ref, k_ref, v_ref, sems
):
    (w_copy,) = start_copies([(w_hbm, w_ref)], sems)
    group = 2 * lax.axis_index("col") + lax.rem(lax.axis_index("row"), 2)
    count, width = q_ref.shape
    head = turn_ref.shape[2]
    for which, ref in enumerate((q_ref, k_ref, v_ref)):
        source = (8 * which + group) // 3
        for s in range(4):
            ref[4 * s : 4 * s + 4, :] = rows_ref[s, source].astype(f32)

    def turned(values, which):
        values = values * lax.rsqrt(lane_mean(values * values) + eps_norm)
        return (values * turn_ref[2 * which] + swap_pairs(values) * turn_ref[2 * which + 1]).astype(bf16)

    key_ok = mask_ref[...] > 0.0
    contract = (((1,), (1,)), ((), ()))
    scale = head ** (-0.5)
    for h in range(width // head):
        cols = slice(h * head, (h + 1) * head)
        q = turned(q_ref[:, cols], 0)
        k = turned(k_ref[:, cols], 1)
        v = v_ref[:, cols].astype(bf16)
        s_own = lax.dot_general(q, text_ref[0, :, cols], contract, preferred_element_type=f32) * scale
        s_other = lax.dot_general(q, other_ref[0, :, cols], contract, preferred_element_type=f32) * scale
        s_image = lax.dot_general(q, k, contract, preferred_element_type=f32) * scale
        s_image = jnp.where(key_ok, s_image, mask_floor)
        top = jnp.maximum(
            jnp.max(jnp.maximum(s_own, s_other), -1, keepdims=True), jnp.max(s_image, -1, keepdims=True)
        )
        w_own = jnp.exp(s_own - top)
        w_other = jnp.exp(s_other - top)
        w_image = jnp.where(key_ok, jnp.exp(s_image - top), 0.0)
        total = jnp.sum(w_own + w_other, -1, keepdims=True) + jnp.sum(w_image, -1, keepdims=True)
        summed = (
            jnp.dot(w_own.astype(bf16), text_ref[1, :, cols], preferred_element_type=f32)
            + jnp.dot(w_other.astype(bf16), other_ref[1, :, cols], preferred_element_type=f32)
            + jnp.dot(w_image.astype(bf16), v, preferred_element_type=f32)
        )
        mixed = (summed / total).astype(bf16)
        for s in range(4):
            for r in range(8):
                out_ref[8 * s + r, :, cols] = mixed[4 * s : 4 * s + 4, :]
    w_copy.wait()


def out_kernel(mixed_ref, states_ref, gate_ref, w0_ref, w1_ref, w2_ref, w3_ref, out_ref, rows_ref):
    col = lax.axis_index("col")
    depth = w0_ref.shape[0]
    piece = mixed_ref.shape[2]
    for r in range(8):
        for s in range(4):
            at = (2 * s + r % 2) * piece
            rows_ref[4 * (r // 2) : 4 * (r // 2) + 4, at : at + piece] = mixed_ref[8 * s + r].astype(f32)
    attended = 0.0
    for d, w_ref in enumerate((w0_ref, w1_ref, w2_ref, w3_ref)):
        at = pl.multiple_of(jnp.bitwise_xor(col, d) * depth, depth)
        share = rows_ref[:, pl.ds(at, depth)].astype(bf16)
        attended = attended + jnp.dot(share, w_ref[...], preferred_element_type=f32)
    first = (states_ref[...] + gate_ref[...] * attended).astype(bf16)
    for r in range(8):
        out_ref[r] = first


def mlp_kernel(
    step_hbm, size_hbm, first_ref, mod_ref, w1_ref, w2a_ref, w2_hbm, final_hbm, out_ref, own_ref, final_ref, last_ref,
    live_ref, step_ref, size_ref, rows_ref, w2b_ref, w2c_ref, sems,
):
    row = lax.axis_index("row")
    depth = rows_ref.shape[1]
    piece = first_ref.shape[2]
    step_copy, size_copy, *w_copies = start_copies(
        [
            (step_hbm, step_ref),
            (size_hbm, size_ref),
            (part_rows(w2_hbm, 1), w2b_ref),
            (part_rows(w2_hbm, 2), w2c_ref),
            (final_hbm, final_ref),
        ],
        sems,
    )
    for r in range(8):
        rows_ref[:, r * piece : (r + 1) * piece] = first_ref[r].astype(f32)
    normed = norm_rows(rows_ref[...])
    step_copy.wait()
    size_copy.wait()
    shift = per_request(mod_ref, step_ref, 3, 4, 0, depth)
    scale = per_request(mod_ref, step_ref, 4, 4, 0, depth)
    normed = (normed * (1.0 + scale) + shift).astype(bf16)
    own = rows_ref[0:2, :]
    for q in range(REQ):
        for g in range(2):
            own = jnp.where(row == REQ * g + q, rows_ref[4 * q + 2 * g : 4 * q + 2 * g + 2, :], own)
    own_ref[...] = own
    req = lax.rem(row, REQ)
    last_ref[...] = mod_ref[step_ref[req], 6:8, :]
    grid_col = lax.axis_index("col") * live_ref.shape[0] + lax.broadcasted_iota(jnp.int32, live_ref.shape, 0)
    live = (row // REQ < size_ref[0, req]) & (grid_col < size_ref[1, req])
    live_ref[...] = jnp.where(live, 1.0, 0.0)
    hidden = jax.nn.gelu(
        jnp.dot(normed, w1_ref[...], preferred_element_type=f32), approximate=True
    ).astype(bf16)
    size = w2a_ref.shape[0]
    added = 0.0
    for i, w_ref in enumerate((w2a_ref, w2b_ref, w2c_ref)):
        if i > 0:
            w_copies[i - 1].wait()
        added = added + jnp.dot(hidden[:, i * size : (i + 1) * size], w_ref[...], preferred_element_type=f32)
    gate = per_request(mod_ref, step_ref, 5, 4, 0, depth)
    term = (gate * added).astype(out_ref.dtype)
    for q in range(REQ):
        for g in range(2):
            out_ref[REQ * g + q] = term[4 * q + 2 * g : 4 * q + 2 * g + 2, :]
    w_copies[2].wait()


def final_kernel(terms_ref, first_ref, last_ref, w_ref, live_ref, out_ref):
    second = first_ref[...]
    for r in range(8):
        second = second + terms_ref[r].astype(f32)
    normed = (norm_rows(second) * (1.0 + last_ref[1:2, :]) + last_ref[0:1, :]).astype(bf16)
    raw = lax.dot_general(normed, w_ref[...], (((1,), (1,)), ((), ())), preferred_element_type=f32)
    out_ref[...] = jnp.where(live_ref[...] > 0.0, raw, 0.0)


def blend_kernel(masked_ref, live_ref, near_ref, far_ref, latent_ref, velocity_ref, next_ref):
    col = lax.axis_index("col")
    masked = masked_ref[...]
    near = near_ref[...]
    far = jnp.where((col == 1) | (col == 2), far_ref[...], 0.0)
    odd = lax.rem(col, 2) == 1
    count = masked.shape[0]
    left = jnp.concatenate([jnp.where(odd, near, far)[count - 1 :, :], masked[: count - 1, :]], 0)
    right = jnp.concatenate([masked[1:, :], jnp.where(odd, far, near)[:1, :]], 0)
    velocity = jnp.where(live_ref[...] > 0.0, masked + blend * (left + right - 2.0 * masked), 0.0)
    velocity_ref[...] = velocity
    next_ref[...] = latent_ref[...] + -1.0 / STEPS * velocity


def call(kernel, outs, specs, scratch=(), limit=8 << 20):
    return pl.pallas_call(
        kernel,
        out_shape=tuple(jax.ShapeDtypeStruct(shape, dtype) for shape, dtype in outs),
        in_specs=specs,
        out_specs=(VMEM_SPEC,) * len(outs),
        scratch_shapes=list(scratch),
        compiler_params=pltpu.CompilerParams(vmem_limit_bytes=limit),
    )


def exchange(values, axes):
    return lax.all_to_all(values, axes, split_axis=0, concat_axis=0, tiled=True)


def compact_on_device(
    image_states, latent, text_keys, text_values, mod_table, timestep, grid_size, rope_offset,
    w_qkv, q_gain, k_gain, w_out, w_fc1, w_fc2, w_final,
):
    rows = lax.axis_size("row")
    cols = lax.axis_size("col")
    stay = lambda values: pltpu.with_memory_space_constraint(values, pltpu.HBM)
    tile_w, width = image_states.shape
    head = q_gain.shape[0]
    piece = width // 8
    tokens = rows * tile_w
    both = ("col", "row")

    near = [(i, i ^ 1) for i in range(cols)]
    steps = stay(timestep)
    sizes = stay(grid_size.T)
    fc2 = stay(w_fc2)
    sems = lambda count: pltpu.SemaphoreType.DMA((count,))
    steps_space = pltpu.SMEM(timestep.shape, jnp.int32)
    sizes_space = pltpu.SMEM(grid_size.shape[::-1], jnp.int32)
    gain_space = pltpu.VMEM((1, head), f32)
    fc2_part = ((w_fc2.shape[0] // FC_PARTS, width), bf16)

    spread, given, mods, turn, mask = call(
        opening_kernel,
        [
            ((rows, tile_w, width), bf16),
            ((2, text_keys.shape[0], piece), bf16),
            (mod_table.shape, f32),
            ((4, tokens, head), f32),
            ((tokens, tokens), f32),
        ],
        [HBM_SPEC] * 8,
        [sizes_space, sizes_space, gain_space, gain_space, sems(8)],
    )(
        stay(image_states), stay(text_keys), stay(text_values), stay(mod_table), sizes, stay(rope_offset.T),
        stay(q_gain.reshape(1, head)), stay(k_gain.reshape(1, head)),
    )
    other = lax.ppermute(given, "row", [(i, i ^ 1) for i in range(rows)])
    w_x = lax.ppermute(w_out, "col", [(i, i ^ 2) for i in range(cols)])
    w_k = lax.ppermute(w_out, "col", near)
    gathered = exchange(spread, "row")
    half_rows = text_keys.shape[0]
    pieces, fc2_a, text, states, gate = call(
        qkv_kernel,
        [
            ((rows * cols, 4, piece), bf16),
            fc2_part,
            ((2, half_rows, piece), bf16),
            ((tokens, piece), f32),
            ((tokens, piece), f32),
        ],
        [HBM_SPEC] + [VMEM_SPEC] * 3 + [HBM_SPEC] * 3,
        [
            steps_space,
            pltpu.VMEM((tokens, width), f32),
            sems(4),
        ],
    )(
        steps, gathered, mods, lax.ppermute(w_qkv, "col", near), fc2, stay(text_keys), stay(text_values),
    )
    pieces, other, w_k = lax.optimization_barrier((pieces, other, w_k))
    got = exchange(pieces, both).reshape(cols, rows, 4, piece)
    mixed, w_own = call(
        attention_kernel,
        [((rows * cols, 4, piece), bf16), (w_out.shape, bf16)],
        [VMEM_SPEC] * 5 + [HBM_SPEC],
        [pltpu.VMEM((tokens, piece), f32)] * 3 + [sems(1)],
    )(got, text, other, turn, mask, stay(w_out))
    mixed, w_x = lax.optimization_barrier((mixed, w_x))
    w_xk = lax.ppermute(w_x, "col", near)
    all_mixed = exchange(mixed, both)
    (first,) = call(
        out_kernel, [((rows, tokens, piece), bf16)], [VMEM_SPEC] * 7, [pltpu.VMEM((tokens, width), f32)]
    )(all_mixed, states, gate, w_own, w_k, w_x, w_xk)
    all_first = exchange(first, "row")
    terms, first_own, final_here, last, live = call(
        mlp_kernel,
        [
            ((rows, tile_w, width), bf16),
            ((tile_w, width), f32),
            (w_final.shape[::-1], bf16),
            ((2, width), f32),
            (latent.shape, f32),
        ],
        [HBM_SPEC, HBM_SPEC] + [VMEM_SPEC] * 4 + [HBM_SPEC, HBM_SPEC],
        [steps_space, sizes_space, pltpu.VMEM((tokens, width), f32)]
        + [pltpu.VMEM(*fc2_part)] * 2
        + [sems(5)],
        limit=16 << 20,
    )(steps, sizes, all_first, mods, w_fc1, fc2_a, fc2, stay(w_final.T))
    all_terms = exchange(terms, "row")
    (masked,) = call(final_kernel, [(latent.shape, f32)], [VMEM_SPEC] * 5)(all_terms, first_own, last, final_here, live)
    beside = lax.ppermute(masked, "col", near)
    across = lax.ppermute(masked, "col", [(i, i ^ 3) for i in range(cols)])
    return call(blend_kernel, [(latent.shape, f32)] * 2, [VMEM_SPEC] * 5)(masked, live, beside, across, latent)


def solution(mesh):
    placed = (
        P(("row", "col"), None),
        P(("row", "col"), None),
        P("row", "col"),
        P("row", "col"),
        P(),
        P(),
        P(),
        P(),
        P(None, "row"),
        P(),
        P(),
        P("col", "row"),
        P(None, "row"),
        P("row", None),
        P(),
    )
    compact = mesh.shape["row"] == 2 * REQ and mesh.shape["col"] == 4
    return jax.shard_map(
        compact_on_device if compact else on_device,
        mesh=mesh,
        in_specs=placed,
        out_specs=(P(("row", "col"), None), P(("row", "col"), None)),
        check_vma=False,
    )
```
